32 devices in a mesh: gx: 8 (over z, core), gy: 4 (over y, x).
Axes of the slice: x: 2, y: 2, z: 4, core: 2. Of those that a mesh axis runs over, the one named last changes fastest.
Arguments:
- tracers: bfloat16 [8, 64, 32, 256], P(None, 'gx', 'gy'), may hold values from -6 to 6
- velocity: float32 [2, 64, 32], P(None, 'gx', 'gy'), may hold values from -0.04 to 0.04
- inflow: int32 [4, 64, 32], P(None, 'gx', 'gy'), may hold values from 0 to 1, as said below
- leaf_solve: float32 [256, 256], replicated, may hold values from -0.375 to 0.375
- leaf_skeleton: float32 [256, 64], replicated, may hold values from -0.375 to 0.375
- leaf_lift: float32 [64, 256], replicated, may hold values from -0.75 to 0.75
- merge_first: float32 [128, 64], replicated, may hold values from -0.5 to 0.5
- merge_second: float32 [128, 128], replicated, may hold values from -0.5 to 0.5
- merge_rest: float32 [9, 256, 128], replicated, may hold values from -0.375 to 0.375
- parent_first: float32 [64, 128], replicated, may hold values from -0.75 to 0.75
- parent_second: float32 [128, 128], replicated, may hold values from -0.5 to 0.5
- parent_rest: float32 [9, 128, 256], replicated, may hold values from -0.5 to 0.5
- sibling_first: float32 [128, 128], replicated, may hold values from -0.125 to 0.125
- sibling_second: float32 [128, 128], replicated, may hold values from -0.125 to 0.125
- sibling_rest: float32 [9, 256, 256], replicated, may hold values from -0.09375 to 0.09375
- root_map: float32 [128, 128], replicated, may hold values from -0.5 to 0.5
Outputs:
- updated: bfloat16 [8, 64, 32, 256], P(None, 'gx', 'gy')
The draws below stay inside these ranges and needn't reach their ends.
Inputs may be any that keep to these rules, and one draw needn't show every extreme that they name: inflow[0] of leaf (i, j) equals 1 minus inflow[1] of leaf (i - 1, j), and inflow[2] of leaf (i, j) equals 1 minus inflow[3] of leaf (i, j - 1); inflow[1] is 0 on the last leaves along the first dimension and inflow[3] on the last leaves along the second.
All inputs are finite; a program needn't handle non-finite values.
Results may differ from the reference program's by a relative error of at most 0.001.
Values may be sent and summed in bfloat16 or wider, within the bound.
A program may use at most 64 MiB of HBM per device.

```python
import jax
import jax.numpy as jnp
from jax import lax

TRACERS = 8
NODE = 16
NODES = 256
LEAF_SKEL = 64
RANK = 128
LEAF_SIDE = 8
LEAVES_X = 64
LEAVES_Y = 32
LEVELS = 11
N_GX = 8
N_GY = 4


def draw_inflow(key, part):
    key_first, key_second = jax.random.split(jax.random.fold_in(key, 11))
    low_first = jax.random.randint(key_first, (LEAVES_X, LEAVES_Y), 0, 2, dtype=jnp.int32)
    low_second = jax.random.randint(key_second, (LEAVES_X, LEAVES_Y), 0, 2, dtype=jnp.int32)
    high_first = jnp.concatenate([1 - low_first[1:], jnp.zeros((1, LEAVES_Y), jnp.int32)], axis=0)
    high_second = jnp.concatenate([1 - low_second[:, 1:], jnp.zeros((LEAVES_X, 1), jnp.int32)], axis=1)
    return jnp.stack([low_first, high_first, low_second, high_second]).astype(jnp.int32)


def shard_levels(key, extent, shards, least, top_value):
    level = 1.0
    for dim, blocks in shards:
        heights = jax.random.uniform(jax.random.fold_in(jax.random.fold_in(key, 6), dim), (blocks,), jnp.float32, least / len(shards), top_value / len(shards))
        level = level * jnp.repeat(jnp.exp(heights), extent[dim] // blocks).reshape((-1,) + (1,) * (len(extent) - 1 - dim))
    return level


def normal_values(stream_key, dims, deviation, most, cuts=(), held_as=jnp.bfloat16):
    result = jax.random.normal(stream_key, dims, jnp.float32) * deviation
    if len(cuts) > 0:
        result = shard_levels(stream_key, dims, cuts, -0.22, 0.18) * result
    return jnp.clip(result, min=-most, max=most).astype(held_as)


def setup_inputs(seed: int = 0) -> dict:
    seeds = jax.random.split(jax.random.key(seed), 17)
    return {
        "tracers": normal_values(seeds[0], (TRACERS, LEAVES_X, LEAVES_Y, NODES), 1.0, 6.0, ((1, 8), (2, 4))),
        "velocity": jnp.clip(jax.random.uniform(seeds[1], (2, LEAVES_X, LEAVES_Y), jnp.float32, -0.04, 0.04) * shard_levels(seeds[1], (2, LEAVES_X, LEAVES_Y), ((1, 8), (2, 4)), -0.4, 0.0), -0.04, 0.04),
        "inflow": draw_inflow(jax.random.fold_in(seeds[16], 71), 0),
        "leaf_solve": normal_values(seeds[3], (NODES, NODES), NODES ** -0.5, 0.375, (), jnp.float32),
        "leaf_skeleton": normal_values(seeds[4], (NODES, LEAF_SKEL), NODES ** -0.5, 0.375, (), jnp.float32),
        "leaf_lift": normal_values(seeds[5], (LEAF_SKEL, NODES), LEAF_SKEL ** -0.5, 0.75, (), jnp.float32),
        "merge_first": normal_values(seeds[6], (2 * LEAF_SKEL, LEAF_SKEL), (2 * LEAF_SKEL) ** -0.5, 0.5, (), jnp.float32),
        "merge_second": normal_values(seeds[7], (2 * LEAF_SKEL, RANK), (2 * LEAF_SKEL) ** -0.5, 0.5, (), jnp.float32),
        "merge_rest": normal_values(seeds[8], (LEVELS - 2, 2 * RANK, RANK), (2 * RANK) ** -0.5, 0.375, (), jnp.float32),
        "parent_first": normal_values(seeds[9], (LEAF_SKEL, 2 * LEAF_SKEL), LEAF_SKEL ** -0.5, 0.75, (), jnp.float32),
        "parent_second": normal_values(seeds[10], (RANK, 2 * LEAF_SKEL), RANK ** -0.5, 0.5, (), jnp.float32),
        "parent_rest": normal_values(seeds[11], (LEVELS - 2, RANK, 2 * RANK), RANK ** -0.5, 0.5, (), jnp.float32),
        "sibling_first": normal_values(seeds[12], (2 * LEAF_SKEL, 2 * LEAF_SKEL), (32 * LEAF_SKEL) ** -0.5, 0.125, (), jnp.float32),
        "sibling_second": normal_values(seeds[13], (2 * LEAF_SKEL, 2 * LEAF_SKEL), (32 * LEAF_SKEL) ** -0.5, 0.125, (), jnp.float32),
        "sibling_rest": normal_values(seeds[14], (LEVELS - 2, 2 * RANK, 2 * RANK), (32 * RANK) ** -0.5, 0.09375, (), jnp.float32),
        "root_map": normal_values(seeds[15], (RANK, RANK), RANK ** -0.5, 0.5, (), jnp.float32),
    }


highest = lax.Precision.HIGHEST


def product(left, right):
    return jnp.dot(left, right, precision=highest, preferred_element_type=jnp.float32)


def spectral_matrix(node_count):
    node_index = jnp.arange(node_count)
    points = -jnp.cos(jnp.pi * node_index.astype(jnp.float32) / (node_count - 1))
    end_weights = jnp.where((node_index == 0) | (node_index == node_count - 1), 2.0, 1.0)
    parity = jnp.where(node_index % 2 == 0, 1.0, -1.0)
    weights = (end_weights * parity).astype(jnp.float32)
    identity = jnp.eye(node_count, dtype=jnp.float32)
    offsets = points[:, None] - points[None, :] + identity
    matrix = (weights[:, None] / weights[None, :]) / offsets * (1.0 - identity)
    return matrix - jnp.diag(jnp.sum(matrix, axis=1))


def derivative_tables(node_count):
    spectral = spectral_matrix(node_count)
    identity = jnp.eye(node_count, dtype=jnp.float32)
    return jnp.concatenate([jnp.kron(spectral, identity).T, jnp.kron(identity, spectral).T], axis=1)


def side_table(node_count):
    node_index = jnp.arange(node_count * node_count)
    along_first = node_index // node_count
    along_second = node_index % node_count
    position = jnp.arange(node_count)[:, None]
    table_rows = [(along_first[None, :] == 0) & (along_second[None, :] == position),
                  (along_first[None, :] == node_count - 1) & (along_second[None, :] == position),
                  (along_second[None, :] == 0) & (along_first[None, :] == position),
                  (along_second[None, :] == node_count - 1) & (along_first[None, :] == position)]
    return jnp.concatenate(table_rows, axis=0).astype(jnp.float32)


def edge_values(tracer_field, node_count):
    node_grid = tracer_field.reshape(tracer_field.shape[:-1] + (node_count, node_count))
    return (node_grid[..., 0, :], node_grid[..., node_count - 1, :],
            node_grid[..., :, 0], node_grid[..., :, node_count - 1])


def forcing_term(tracer_field, own_edges, neighbours, velocity, inflow):
    node_count = own_edges[0].shape[-1]
    square = node_count * node_count
    gradients = product(tracer_field, derivative_tables(node_count))
    advective = velocity[0][None, :, :, None] * gradients[..., :square] + velocity[1][None, :, :, None] * gradients[..., square:]
    penalty_terms = []
    for side_index in range(4):
        strength = inflow[side_index].astype(jnp.float32) * (node_count * jnp.abs(velocity[side_index // 2]))
        penalty_terms.append(strength[None, :, :, None] * (neighbours[side_index] - own_edges[side_index]))
    penalty = product(jnp.concatenate(penalty_terms, axis=-1), side_table(node_count))
    return tracer_field - advective + penalty


def level_operators(level, tables):
    if level == 0:
        return tables[0]
    if level == 1:
        return tables[1]
    return tuple(stacked[level - 2] for stacked in tables[2])


def split_pairs(current, merge_axis):
    new_shape = current.shape[:merge_axis] + (current.shape[merge_axis] // 2, 2) + current.shape[merge_axis + 1:]
    paired = current.reshape(new_shape)
    return lax.index_in_dim(paired, 0, merge_axis + 1, False), lax.index_in_dim(paired, 1, merge_axis + 1, False)


def join_pairs(former, latter, merge_axis):
    joined = jnp.stack([former, latter], axis=merge_axis + 1)
    new_shape = list(former.shape)
    new_shape[merge_axis] = new_shape[merge_axis] * 2
    return joined.reshape(tuple(new_shape))


def ascend(current, merge_plan, start_level, tables):
    levels = []
    for offset, merge_axis in enumerate(merge_plan):
        level = start_level + offset
        former, latter = split_pairs(current, merge_axis)
        levels.append((former, latter, merge_axis, level))
        current = product(jnp.concatenate([former, latter], axis=-1), level_operators(level, tables)[0])
    return current, levels


def descend(boundary, levels, tables):
    for former, latter, merge_axis, level in reversed(levels):
        operators = level_operators(level, tables)
        joined_pair = product(boundary, operators[1]) + product(
            jnp.concatenate([former, latter], axis=-1), operators[2])
        half_width = joined_pair.shape[-1] // 2
        boundary = join_pairs(joined_pair[..., :half_width], joined_pair[..., half_width:], merge_axis)
    return boundary


def local_plan(leaf_side):
    merge_plan = []
    block_span = leaf_side
    while block_span > 1:
        merge_plan = merge_plan + [1, 2]
        block_span = block_span // 2
    return merge_plan


def cross_plan(count_first, count_second):
    merge_plan = []
    while count_first * count_second > 1:
        if count_first >= count_second:
            merge_plan.append(1)
            count_first = count_first // 2
        else:
            merge_plan.append(2)
            count_second = count_second // 2
    return merge_plan


def reference(tracers, velocity, inflow, leaf_solve, leaf_skeleton, leaf_lift, merge_first, merge_second, merge_rest,
              parent_first, parent_second, parent_rest, sibling_first, sibling_second, sibling_rest, root_map):
    merge_plan = local_plan(LEAF_SIDE) + cross_plan(N_GX, N_GY)
    tables = ((merge_first, parent_first, sibling_first), (merge_second, parent_second, sibling_second),
              (merge_rest, parent_rest, sibling_rest))

    def one_tracer(tracer_slice):
        tracer_field = tracer_slice.astype(jnp.float32)[None]
        own_edges = edge_values(tracer_field, NODE)
        zeros_first = jnp.zeros_like(own_edges[0][:, :1])
        zeros_second = jnp.zeros_like(own_edges[2][:, :, :1])
        neighbours = (jnp.concatenate([zeros_first, own_edges[1][:, :-1]], axis=1),
                      jnp.concatenate([own_edges[0][:, 1:], zeros_first], axis=1),
                      jnp.concatenate([zeros_second, own_edges[3][:, :, :-1]], axis=2),
                      jnp.concatenate([own_edges[2][:, :, 1:], zeros_second], axis=2))
        forcing = forcing_term(tracer_field, own_edges, neighbours, velocity, inflow)
        skeleton = product(forcing, leaf_skeleton)
        tree_root, levels = ascend(skeleton, merge_plan, 0, tables)
        leaf_boundary = descend(product(tree_root, root_map), levels, tables)
        updated = product(forcing, leaf_solve) + product(leaf_boundary, leaf_lift)
        return updated.astype(jnp.bfloat16)[0]

    return lax.map(one_tracer, tracers)
```

```python
import functools

import jax
import jax.numpy as jnp
import numpy as np
from jax import lax
from jax.experimental import pallas as pl
from jax.experimental.pallas import tpu as pltpu
from jax.sharding import PartitionSpec as P

NODE = 16
SQUARE = NODE * NODE
F32 = jnp.float32
BF16 = jnp.bfloat16
VMEM_LIMIT = 32 * 1024 * 1024
MESH = pl.DeviceIdType.MESH
LAST_STAGE = 5
FOLDED = 3


def local_plan(leaf_side):
    merge_plan = []
    block_span = leaf_side
    while block_span > 1:
        merge_plan = merge_plan + [1, 2]
        block_span = block_span // 2
    return merge_plan


def cross_plan(count_first, count_second):
    merge_plan = []
    bits = {"gx": 0, "gy": 0}
    while count_first * count_second > 1:
        if count_first >= count_second:
            axis, count_first = "gx", count_first // 2
        else:
            axis, count_second = "gy", count_second // 2
        merge_plan.append((axis, bits[axis]))
        bits[axis] += 1
    return merge_plan


def staged(plan):
    stages, rest = [], list(plan)
    while len(rest) > LAST_STAGE:
        size = min(3, len(rest) - LAST_STAGE)
        stages.append(rest[:size])
        rest = rest[size:]
    return stages + [rest]


def point_tables():
    index = np.arange(NODE)
    points = -np.cos(np.pi * index / (NODE - 1))
    weights = np.where(index % 2 == 0, 1.0, -1.0)
    weights[[0, NODE - 1]] *= 2.0
    eye = np.eye(NODE)
    matrix = weights[:, None] / weights[None, :] / (points[:, None] - points[None, :] + eye)
    matrix = matrix * (1.0 - eye)
    matrix = matrix - np.diag(matrix.sum(axis=1))
    both = np.concatenate([np.kron(matrix, eye).T, np.kron(eye, matrix).T], axis=1)
    both = both.astype(np.float32)
    high = both.astype(jnp.bfloat16)
    low = (both - high.astype(np.float32)).astype(jnp.bfloat16)
    facing = np.zeros((SQUARE, 2 * SQUARE), np.float32)
    last = NODE - 1
    for k in range(NODE):
        facing[last * NODE + k, k] = 1.0
        facing[k, last * NODE + k] = 1.0
        facing[k * NODE + last, SQUARE + k * NODE] = 1.0
        facing[k * NODE, SQUARE + k * NODE + last] = 1.0
    return np.concatenate([high, low, facing.astype(jnp.bfloat16)], axis=1)


def split(x):
    high = x.astype(BF16)
    return high, (x - high.astype(F32)).astype(BF16)


def dot(left, right):
    return jnp.dot(left, right, preferred_element_type=F32)


def dot_across(left, right):
    return lax.dot_general(left, right, (((1,), (1,)), ((), ())), preferred_element_type=F32)


def product(x, weight, dot=dot):
    high, low = weight
    rows = x.shape[0]
    if rows >= 64:
        x_high, x_low = split(x)
        return dot(x_high, high) + dot(x_low, high) + dot(x_high, low)
    rest = x - x.astype(BF16).astype(F32)
    both = jnp.concatenate([x, rest], axis=0).astype(BF16)
    out = dot(both, high) + dot(both, low)
    return out[:rows] + out[rows:]


def lanes(shape):
    return lax.broadcasted_iota(jnp.int32, shape, len(shape) - 1)


def left_half(shape):
    return lanes(shape) < shape[-1] // 2


def narrow(x, table):
    rows = x.shape[0]
    rest = x - x.astype(BF16).astype(F32)
    out = dot(jnp.concatenate([x, rest], axis=0).astype(BF16), table)
    out = out[:rows] + out[rows:]
    return out[:, :128] + out[:, 128:]


def broad(x, table):
    rows = x.shape[0]
    rest = x - x.astype(BF16).astype(F32)
    both = jnp.concatenate([x, rest], axis=0).astype(BF16)
    out = dot(jnp.concatenate([both, both], axis=1), table)
    return out[:rows] + out[rows:]


def rows_to_lanes(x, count):
    size = x.shape[0] // count
    return jnp.concatenate([x[k * size : (k + 1) * size] for k in range(count)], axis=1)


def lanes_to_rows(x):
    return jnp.concatenate([x[:, k : k + 128] for k in range(0, x.shape[1], 128)], axis=0)


def quarters(x):
    return [x[:128, :128], x[:128, 128:], x[128:, :128], x[128:, 128:]]


def merge_pair(former, latter):
    wide = product(former, split(rows_to_lanes(latter, 2)))
    return jnp.concatenate(quarters(wide), axis=0)


def parent_pair(upper, lower):
    a, b, c, d = quarters(product(lanes_to_rows(upper), split(lower)))
    return jnp.concatenate([a, c, b, d], axis=1)


def wide_split(x):
    return jnp.concatenate(split(x), axis=1)


def tall_split(x):
    return jnp.concatenate(split(x), axis=0)


def kernel(stages, leaf_side, tracer_count, *refs):
    names = ["u", "velocity", "inflow", "tables", "leaf_solve", "leaf_skeleton", "leaf_lift"]
    names += [a + "_" + b for a in ("merge", "parent", "sibling") for b in ("first", "second", "rest")]
    names += ["root_map"]
    hbm = dict(zip(names, refs[: len(names)]))
    out_ref = refs[len(names)]
    rest = refs[len(names) + 1 :]
    v = dict(zip(names, rest[: len(names)]))
    (
        load_sem, field, near, coef, force, solved,
        up_leaf, up_low, up_high, up_cross, fold, down_high, down_low, down_leaf,
        send_x, send_y, halo_x, halo_y, halo_send, halo_recv, chain,
    ) = rest[len(names) : len(names) + 21]
    stage_refs = rest[len(names) + 21 :]
    T, L = tracer_count, leaf_side
    leaves = L * L
    rows = T * leaves
    half = SQUARE // 2

    loads = {}
    for k, name in enumerate(names):
        loads[name] = pltpu.make_async_copy(hbm[name], v[name], load_sem.at[k])
    order = ["u", "tables", "velocity", "inflow", "leaf_skeleton", "merge_first", "merge_second"]
    order += ["merge_rest", "parent_rest", "sibling_rest", "root_map", "parent_second", "parent_first"]
    order += ["leaf_lift", "leaf_solve", "sibling_first", "sibling_second"]
    for name in order:
        loads[name].start()

    place = {"gx": lax.axis_index("gx"), "gy": lax.axis_index("gy")}
    count = {"gx": lax.axis_size("gx"), "gy": lax.axis_size("gy")}
    bit_of = lambda axis, bit: lax.rem(place[axis] // (1 << bit), 2)

    def partner(stage, mask):
        target = dict(place)
        for k, (axis, bit) in enumerate(stage):
            if mask >> (len(stage) - 1 - k) & 1:
                target[axis] = target[axis] + (1 - 2 * bit_of(axis, bit)) * (1 << bit)
        return (target["gx"], target["gy"])

    barrier = pltpu.get_barrier_semaphore()
    expected = jnp.int32(0)
    has, beside = {}, {}
    for axis in ("gx", "gy"):
        for way in (-1, 1):
            spot = dict(place)
            spot[axis] = spot[axis] + way
            beside[axis, way] = (spot["gx"], spot["gy"])
            has[axis, way] = place[axis] > 0 if way < 0 else place[axis] < count[axis] - 1

            @pl.when(has[axis, way])
            def _(axis=axis, way=way):
                pl.semaphore_signal(barrier, inc=1, device_id=beside[axis, way], device_id_type=MESH)

            expected = expected + jnp.where(has[axis, way], 1, 0)
    for stage in stages:
        for mask in reversed(range(1, 1 << len(stage))):
            pl.semaphore_signal(barrier, inc=1, device_id=partner(stage, mask), device_id_type=MESH)
            expected = expected + 1

    def spot_of(i, j):
        return sum(
            ((i >> b & 1) << (5 - 2 * b)) + ((j >> b & 1) << (4 - 2 * b)) for b in range(3)
        )

    grid = sorted((spot_of(i, j), i, j) for i in range(L) for j in range(L))
    block = lambda i, j: slice(spot_of(i, j) * T, spot_of(i, j) * T + T)
    by_tracer = lambda i, j, h: pl.ds(h * rows + i * L + j, T, stride=leaves)

    loads["u"].wait()
    plain = v["u"][...].astype(F32).reshape(rows, SQUARE)
    for h in range(2):
        field[h * rows : (h + 1) * rows, :] = plain[:, h * half : (h + 1) * half]
    u = jnp.concatenate(
        [
            jnp.concatenate([field[by_tracer(i, j, h), :] for _, i, j in grid], axis=0)
            for h in range(2)
        ],
        axis=1,
    )
    ub = u.astype(BF16)
    loads["tables"].wait()
    near[...] = dot(ub, v["tables"][:, 4 * SQUARE :])
    line = lambda spots, c: jnp.concatenate(
        [near[block(i, j), c * half : (c + 1) * half] for i, j in spots], axis=0
    )
    side = lambda axis, k: [(k, m) if axis == "gx" else (m, k) for m in range(L)]
    send_x[1] = line(side("gx", L - 1), 0).astype(BF16)
    send_x[0] = line(side("gx", 0), 1).astype(BF16)
    for k in range(2):
        spots = side("gy", k * (L - 1))
        send_y[k] = (line(spots, 2) + pltpu.roll(line(spots, 3), 2, 1)).astype(BF16)
    pl.semaphore_wait(barrier, expected)

    def halo_copy(axis, way):
        k = 0 if way < 0 else 1
        source, target = (send_x, halo_x) if axis == "gx" else (send_y, halo_y)
        slot = k + (0 if axis == "gx" else 2)
        return pltpu.make_async_remote_copy(
            src_ref=source.at[k],
            dst_ref=target.at[k],
            send_sem=halo_send.at[slot],
            recv_sem=halo_recv.at[slot],
            device_id=beside[axis, way],
            device_id_type=MESH,
        )

    sides = [("gy", -1), ("gy", 1), ("gx", -1), ("gx", 1)]
    for axis, way in sides:

        @pl.when(has[axis, way])
        def _(axis=axis, way=way):
            halo_copy(axis, way).start()

    plan = [entry for stage in stages for entry in stage]
    bits = [bit_of(axis, bit) for axis, bit in plan]
    own_half = lambda k, w: jnp.where(bits[k] == 1, w[:, 128:], w[:, :128])
    twice = lambda w, axis: jnp.concatenate([w, w], axis=axis)
    merge = lambda k: v["merge_rest"][k]
    parent = lambda k: v["parent_rest"][k]

    def folded(levels, top, siblings):
        weights = top
        for k in reversed(levels):
            groups = 1 << (levels[-1] - k)
            if weights is not None:
                weights = product(merge(4 + k), split(weights))
            elif siblings:
                weights = jnp.zeros((256, 128), F32)
            else:
                weights = merge(4 + k)
            blocks = [weights[:, g * 128 : (g + 1) * 128] for g in range(groups)]
            if siblings:
                sibling = own_half(k, v["sibling_rest"][4 + k])
                if k > 0:
                    sibling = product(sibling, split(chain[k - 1]))
                mine = jnp.int32(0)
                for later in levels:
                    if later > k:
                        mine = mine + bits[later] * (1 << (levels[-1] - later))
                blocks = [x + jnp.where(mine == g, sibling, 0.0) for g, x in enumerate(blocks)]
            weights = jnp.concatenate([x[:128] for x in blocks] + [x[128:] for x in blocks], axis=1)
        return lanes_to_rows(weights)

    first = len(plan) - len(stages[-1])
    last_levels = list(range(first, len(plan)))
    direct, folds = last_levels[: -FOLDED], last_levels[-FOLDED:]
    assert len(direct) == 2
    slots, groups = 1 << len(last_levels), 1 << len(folds)

    for name in ("leaf_skeleton", "merge_first", "merge_second", "merge_rest"):
        loads[name].wait()
    two = [
        product(v["merge_first"][...].T, split(v["merge_second"][d * 64 : (d + 1) * 64, :]))
        for d in range(2)
    ]
    four = jnp.concatenate([two[d][c * 64 : (c + 1) * 64] for c in range(2) for d in range(2)], axis=1)
    up_leaf[...] = wide_split(lanes_to_rows(product(v["leaf_skeleton"][...].T, split(four))))
    up_low[...] = wide_split(merge_pair(merge(0), merge(1)))
    up_high[...] = wide_split(merge_pair(merge(2), merge(3)))
    up_cross[...] = wide_split(folded(direct, None, False))

    for name in ("parent_rest", "sibling_rest", "root_map"):
        loads[name].wait()
    previous = None
    for k in range(len(plan)):
        own = own_half(k, parent(4 + k))
        previous = own if k == 0 else product(own, split(previous))
        chain[k] = previous
    previous = product(v["root_map"][...], split(previous))
    fold[: groups * 128, :] = wide_split(folded(folds, previous, True))
    fold[groups * 128 :, :] = wide_split(folded(direct, None, True))
    down_high[...] = tall_split(parent_pair(parent(3), parent(2)))
    down_low[...] = tall_split(parent_pair(parent(1), parent(0)))
    for name in ("parent_second", "parent_first", "leaf_lift"):
        loads[name].wait()
    halves = lambda x: jnp.concatenate([x, pltpu.roll(x, 64, 1)], axis=0)[:, :64]
    lifts = product(halves(v["parent_first"][...]), split(v["leaf_lift"][...]))
    lifts = jnp.concatenate([lifts[:64], lifts[64:]], axis=1)
    lifts = product(halves(v["parent_second"][...]), split(lifts))
    down_leaf[...] = tall_split(
        jnp.concatenate(
            [
                lifts[d * 128 : (d + 1) * 128, c * SQUARE : (c + 1) * SQUARE]
                for c in range(2)
                for d in range(2)
            ],
            axis=1,
        )
    )

    loads["velocity"].wait()
    loads["inflow"].wait()
    own = lax.broadcasted_iota(jnp.int32, (leaves, L), 0) % L == lanes((leaves, L))

    def column(values):
        wide = jnp.concatenate(
            [jnp.broadcast_to(values[i : i + 1, :], (L, L)) for i in range(L)], axis=0
        )
        return jnp.sum(jnp.where(own, wide, 0.0), axis=1, keepdims=True)

    speed = [v["velocity"][k] for k in range(2)]
    columns = [column(x) for x in speed]
    columns += [
        column(v["inflow"][s].astype(F32) * (NODE * jnp.abs(speed[s // 2]))) for s in range(4)
    ]
    for k, x in enumerate(columns):
        coef[k] = jnp.broadcast_to(x, (leaves, half))
    tile = (T, half)
    on_0, on_1 = lanes(tile) < NODE, lanes(tile) >= half - NODE
    on_2, on_3 = lanes(tile) % NODE == 0, lanes(tile) % NODE == NODE - 1
    at_leaf = lambda k, i, j: jnp.broadcast_to(coef[k, i * L + j : i * L + j + 1, :], tile)
    keep_if = lambda mask, x: jnp.where(mask, x, 0.0)
    strength = lambda s, i, j: at_leaf(2 + s, i, j)

    for q in range(4):
        low, top = q * rows // 4, (q + 1) * rows // 4
        part = ub[low:top]
        grads = dot(part, v["tables"][:, : 2 * SQUARE])
        grads = grads + dot(part, v["tables"][:, 2 * SQUARE : 4 * SQUARE])
        for spot, i, j in grid[q * leaves // 4 : (q + 1) * leaves // 4]:
            at = slice(spot * T, spot * T + T)
            inside = slice(spot * T - low, spot * T + T - low)
            speeds = [at_leaf(k, i, j) for k in range(2)]
            w = [strength(s, i, j) for s in range(4)]
            w_2, w_3 = keep_if(on_2, w[2]), keep_if(on_3, w[3])
            for c in range(2):
                cut = slice(c * half, (c + 1) * half)
                far = slice((2 + c) * half, (3 + c) * half)
                total = u[at, cut] * (1.0 - (keep_if((on_0, on_1)[c], w[c]) + w_2 + w_3))
                total = total - speeds[0] * grads[inside, cut] - speeds[1] * grads[inside, far]
                ahead = i - 1 if c == 0 else i + 1
                if 0 <= ahead < L:
                    total = total + w[c] * near[block(ahead, j), cut]
                if j > 0:
                    total = total + w_2 * near[block(i, j - 1), far]
                if j < L - 1:
                    total = total + w_3 * near[block(i, j + 1), far]
                force[at, cut] = total

    for axis, way in sides:
        slot = 1 if way < 0 else 0

        @pl.when(has[axis, way])
        def _(axis=axis, way=way):
            halo_copy(axis, -way).wait_recv()

        @pl.when(jnp.logical_not(has[axis, way]))
        def _(axis=axis, slot=slot):
            target = halo_x if axis == "gx" else halo_y
            target[slot] = jnp.zeros_like(target[slot])

    for axis, way in sides:
        slot = 1 if way < 0 else 0
        arrived = (halo_x if axis == "gx" else halo_y)[slot].astype(F32)
        shifted = pltpu.roll(arrived, 126, 1) if axis == "gy" else None
        for m, (i, j) in enumerate(side(axis, 0 if way < 0 else L - 1)):
            inside = slice(m * T, m * T + T)
            if axis == "gx":
                c = 0 if way < 0 else 1
                cut = slice(c * half, (c + 1) * half)
                force[block(i, j), cut] = force[block(i, j), cut] + strength(c, i, j) * arrived[inside]
            else:
                w = keep_if(on_2, strength(2, i, j)) if way < 0 else keep_if(on_3, strength(3, i, j))
                for c, x in enumerate((arrived, shifted)):
                    cut = slice(c * half, (c + 1) * half)
                    force[block(i, j), cut] = force[block(i, j), cut] + w * x[inside]

    high, low = split(rows_to_lanes(force[...], 4))
    wide = dot(high, up_leaf[...])
    current_16 = wide[:, :128] + wide[:, 128:] + dot(low, up_leaf[:, :128])
    current_4 = narrow(rows_to_lanes(current_16, 4), up_low[...])
    current = narrow(rows_to_lanes(current_4, 4), up_high[...])

    joined = lambda x: rows_to_lanes(x, 2)
    level = 4
    path = []
    for number, stage in enumerate(stages):
        pool, stage_send, stage_recv = stage_refs[3 * number : 3 * number + 3]
        own_slot = jnp.int32(0)
        for axis, bit in stage:
            own_slot = own_slot * 2 + bit_of(axis, bit)
        pool[own_slot] = current
        copies = [
            pltpu.make_async_remote_copy(
                src_ref=pool.at[own_slot],
                dst_ref=pool.at[own_slot],
                send_sem=stage_send.at[mask],
                recv_sem=stage_recv.at[mask],
                device_id=partner(stage, mask),
                device_id_type=MESH,
            )
            for mask in range(1, 1 << len(stage))
        ]
        for copy in reversed(copies):
            copy.start()
        if number == 0:
            for name in ("leaf_solve", "sibling_first", "sibling_second"):
                loads[name].wait()
            forcing = force[...]
            sibling = lambda k: split(v["sibling_rest"][k])
            is_left = lambda x: left_half(x.shape)
            spread = lambda x: jnp.concatenate(
                [jnp.where(is_left(x), x, 0.0), jnp.where(is_left(x), 0.0, x)], axis=0
            )

            def gathered(x):
                middle = x.shape[0] // 2
                return jnp.where(is_left(x[:middle]), x[:middle], x[middle:])

            cat_0 = gathered(product(forcing, split(twice(v["leaf_skeleton"][...], 0)), dot_across))
            cat_1 = gathered(product(cat_0, split(twice(v["merge_first"][...], 0)), dot_across))
            cats = [joined(current_16)]
            cats.append(joined(product(cats[0], split(merge(0)))))
            cats.append(joined(current_4))
            cats.append(joined(product(cats[2], split(merge(2)))))
            own_part = product(cats[3], sibling(3))
            for k in (2, 1, 0):
                own_part = product(lanes_to_rows(own_part), split(parent(k)))
                own_part = own_part + product(cats[k], sibling(k))
            own_part = product(lanes_to_rows(own_part), split(v["parent_second"][...]))
            own_part = own_part + product(cat_1, split(v["sibling_second"][...]))
            own_part = product(spread(own_part), split(twice(v["parent_first"][...], 0)))
            own_part = own_part + product(cat_0, split(v["sibling_first"][...]))
            own_part = product(spread(own_part), split(twice(v["leaf_lift"][...], 0)))
            solved[...] = own_part + product(forcing, split(v["leaf_solve"][...]))
        if number == len(stages) - 1:
            known = jnp.zeros((T, 128), F32)
            for k, term in enumerate(path):
                term = own_half(k, term)
                known = known + (product(term, split(chain[k - 1])) if k > 0 else term)
        for copy in copies:
            copy.wait()
        if number == len(stages) - 1:
            break
        current = pool[...].reshape(T << len(stage), 128)
        for k, (axis, bit) in enumerate(stage):
            cat = joined(current)
            mine = cat
            for later_axis, later_bit in stage[k + 1 :]:
                middle = mine.shape[0] // 2
                mine = jnp.where(bit_of(later_axis, later_bit) == 1, mine[middle:], mine[:middle])
            path.append(product(mine, split(v["sibling_rest"][level])))
            current = product(cat, split(merge(level)))
            level += 1

    everyone = pool[...].reshape(slots * T, 128)
    merged = narrow(rows_to_lanes(everyone, slots // groups), up_cross[...])
    mine = jnp.int32(0)
    for k in folds:
        mine = mine * 2 + bits[k]
    slabs = [rows_to_lanes(merged, groups)]
    slabs += [pool[k * groups + mine] for k in range(slots // groups)]
    boundary = narrow(jnp.concatenate(slabs, axis=1), fold[...]) + known
    boundary = lanes_to_rows(broad(boundary, down_high[...]))
    boundary = lanes_to_rows(broad(boundary, down_low[...]))
    high, low = split(boundary)
    lifted = dot(twice(high, 1), down_leaf[...]) + dot(low, down_leaf[:128, :])
    for spot, i, j in grid:
        q, inside = divmod(spot, leaves // 4)
        for h in range(2):
            at = q * SQUARE + h * half
            one = lifted[inside * T : (inside + 1) * T, at : at + half]
            one = one + solved[spot * T : spot * T + T, h * half : (h + 1) * half]
            field[by_tracer(i, j, h), :] = one
    updated = jnp.concatenate([field[:rows, :], field[rows:, :]], axis=1)
    out_ref[...] = updated.reshape(out_ref.shape).astype(out_ref.dtype)
    for axis, way in sides:

        @pl.when(has[axis, way])
        def _(axis=axis, way=way):
            halo_copy(axis, way).wait_send()


def local(tables, count_first, count_second, tracers, *operands):
    T, L = tracers.shape[0], tracers.shape[1]
    assert L == 8 and local_plan(L) == [1, 2] * 3
    stages = staged(cross_plan(count_first, count_second))
    rows = T * L * L
    args = [tracers, operands[0], operands[1], tables] + list(operands[2:])
    args[5], args[7] = args[5].T, args[7].T
    depth = operands[7].shape[0]
    vmem, dma = pltpu.VMEM, pltpu.SemaphoreType.DMA
    scratch = [vmem(a.shape, a.dtype) for a in args]
    slots = 1 << len(stages[-1])
    groups = 1 << FOLDED
    scratch += [
        dma((len(args),)),
        vmem((2 * rows, 128), F32),
        vmem((rows, 2 * SQUARE), F32),
        vmem((6, L * L, 128), F32),
        vmem((rows, SQUARE), F32),
        vmem((rows, SQUARE), F32),
        vmem((4 * SQUARE, 256), BF16),
        vmem((512, 256), BF16),
        vmem((512, 256), BF16),
        vmem((slots // groups * 128, 256), BF16),
        vmem(((groups + slots // groups) * 128, 256), BF16),
        vmem((256, 512), BF16),
        vmem((256, 512), BF16),
        vmem((256, 4 * SQUARE), BF16),
        vmem((2, T * L, 128), BF16),
        vmem((2, T * L, 128), BF16),
        vmem((2, T * L, 128), BF16),
        vmem((2, T * L, 128), BF16),
        dma((4,)),
        dma((4,)),
        vmem((depth, 128, 128), F32),
    ]
    for stage in stages:
        slots = 1 << len(stage)
        scratch += [vmem((slots, T, 128), F32), dma((slots,)), dma((slots,))]
    return pl.pallas_call(
        functools.partial(kernel, stages, L, T),
        out_shape=jax.ShapeDtypeStruct(tracers.shape, tracers.dtype),
        in_specs=[pl.BlockSpec(memory_space=pl.ANY)] * len(args),
        out_specs=pl.BlockSpec(memory_space=pltpu.VMEM),
        scratch_shapes=scratch,
        compiler_params=pltpu.CompilerParams(
            collective_id=0, has_side_effects=True, vmem_limit_bytes=VMEM_LIMIT
        ),
    )(*[pltpu.with_memory_space_constraint(a, pltpu.HBM) for a in args])


def solution(mesh):
    tables = point_tables()
    split_both = P(None, "gx", "gy")
    in_specs = (P(None, "gx", "gy", None), split_both, split_both) + (P(),) * 13

    def body(*args):
        return local(
            jnp.asarray(tables), mesh.shape["gx"], mesh.shape["gy"], *args
        )

    return jax.shard_map(
        body,
        mesh=mesh,
        in_specs=in_specs,
        out_specs=P(None, "gx", "gy", None),
        check_vma=False,
    )
```

```python
import functools

import jax
import jax.numpy as jnp
import numpy as np
from jax import lax
from jax.experimental import pallas as pl
from jax.experimental.pallas import tpu as pltpu
from jax.sharding import PartitionSpec as P

NODE = 16
SQUARE = NODE * NODE
F32 = jnp.float32
BF16 = jnp.bfloat16
VMEM_LIMIT = 32 * 1024 * 1024
MESH = pl.DeviceIdType.MESH
LAST_STAGE = 5
FOLDED = 3


def local_plan(leaf_side):
    merge_plan = []
    block_span = leaf_side
    while block_span > 1:
        merge_plan = merge_plan + [1, 2]
        block_span = block_span // 2
    return merge_plan


def cross_plan(count_first, count_second):
    merge_plan = []
    bits = {"gx": 0, "gy": 0}
    while count_first * count_second > 1:
        if count_first >= count_second:
            axis, count_first = "gx", count_first // 2
        else:
            axis, count_second = "gy", count_second // 2
        merge_plan.append((axis, bits[axis]))
        bits[axis] += 1
    return merge_plan


def staged(plan):
    stages, rest = [], list(plan)
    while len(rest) > LAST_STAGE:
        size = min(3, len(rest) - LAST_STAGE)
        stages.append(rest[:size])
        rest = rest[size:]
    return stages + [rest]


def point_tables():
    index = np.arange(NODE)
    points = -np.cos(np.pi * index / (NODE - 1))
    weights = np.where(index % 2 == 0, 1.0, -1.0)
    weights[[0, NODE - 1]] *= 2.0
    eye = np.eye(NODE)
    matrix = weights[:, None] / weights[None, :] / (points[:, None] - points[None, :] + eye)
    matrix = matrix * (1.0 - eye)
    matrix = matrix - np.diag(matrix.sum(axis=1))
    both = np.concatenate([np.kron(matrix, eye).T, np.kron(eye, matrix).T], axis=1)
    both = both.astype(np.float32)
    high = both.astype(jnp.bfloat16)
    low = (both - high.astype(np.float32)).astype(jnp.bfloat16)
    facing = np.zeros((SQUARE, 2 * SQUARE), np.float32)
    last = NODE - 1
    for k in range(NODE):
        facing[last * NODE + k, k] = 1.0
        facing[k, last * NODE + k] = 1.0
        facing[k * NODE + last, SQUARE + k * NODE] = 1.0
        facing[k * NODE, SQUARE + k * NODE + last] = 1.0
    return np.concatenate([high, low, facing.astype(jnp.bfloat16)], axis=1)


def split(x):
    high = x.astype(BF16)
    return high, (x - high.astype(F32)).astype(BF16)


def dot(left, right):
    return jnp.dot(left, right, preferred_element_type=F32)


def product(x, weight):
    high, low = weight
    rows, depth = x.shape
    wide = high.shape[1]
    if rows < 64:
        rest = x - x.astype(BF16).astype(F32)
        both = jnp.concatenate([x, rest], axis=0).astype(BF16)
        if depth == 128:
            both = jnp.concatenate([both, both], axis=1)
            out = dot(both, jnp.concatenate([high, low], axis=0))
        else:
            out = dot(both, high) + dot(both, low)
        return out[:rows] + out[rows:]
    x_high, x_low = split(x)
    if wide == 128:
        weights = jnp.concatenate([high, low], axis=1)
        if depth == 128:
            weights = jnp.concatenate([weights, weights], axis=0)
            out = dot(jnp.concatenate([x_high, x_low], axis=1), weights)
            return out[:, :128] + out[:, 128:]
        out = dot(x_high, weights)
        return out[:, :128] + dot(x_low, high) + out[:, 128:]
    if depth == 128:
        out = dot(jnp.concatenate([x_high, x_high], axis=1), jnp.concatenate([high, low], axis=0))
        return out + dot(x_low, high)
    return dot(x_high, high) + dot(x_low, high) + dot(x_high, low)


def spread_product(x, weight):
    high, low = split(x)
    moved = pltpu.roll(x - high.astype(F32), 64, 1).astype(BF16)
    is_left = left_half(x.shape)
    zero = jnp.zeros_like(high)
    first = [jnp.where(is_left, high, moved), jnp.where(is_left, high, zero)]
    second = [jnp.where(is_left, moved, high), jnp.where(is_left, zero, high)]
    both = jnp.concatenate([jnp.concatenate(k, axis=1) for k in (first, second)], axis=0)
    return dot(both, jnp.concatenate([weight[0]] * 2 + [weight[1]] * 2, axis=0))


def lanes(shape):
    return lax.broadcasted_iota(jnp.int32, shape, len(shape) - 1)


def left_half(shape):
    return lanes(shape) < shape[-1] // 2


def narrow(x, table):
    rows = x.shape[0]
    rest = x - x.astype(BF16).astype(F32)
    out = dot(jnp.concatenate([x, rest], axis=0).astype(BF16), table)
    out = out[:rows] + out[rows:]
    return out[:, :128] + out[:, 128:]


def broad(x, table):
    rows = x.shape[0]
    rest = x - x.astype(BF16).astype(F32)
    both = jnp.concatenate([x, rest], axis=0).astype(BF16)
    out = dot(jnp.concatenate([both, both], axis=1), table)
    return out[:rows] + out[rows:]


def rows_to_lanes(x, count):
    size = x.shape[0] // count
    return jnp.concatenate([x[k * size : (k + 1) * size] for k in range(count)], axis=1)


def lanes_to_rows(x):
    return jnp.concatenate([x[:, k : k + 128] for k in range(0, x.shape[1], 128)], axis=0)


def quarters(x):
    return [x[:128, :128], x[:128, 128:], x[128:, :128], x[128:, 128:]]


def merge_pair(former, latter):
    wide = product(former, split(rows_to_lanes(latter, 2)))
    return jnp.concatenate(quarters(wide), axis=0)


def parent_pair(upper, lower):
    a, b, c, d = quarters(product(lanes_to_rows(upper), split(lower)))
    return jnp.concatenate([a, c, b, d], axis=1)


def wide_split(x):
    return jnp.concatenate(split(x), axis=1)


def tall_split(x):
    return jnp.concatenate(split(x), axis=0)


def kernel(stages, leaf_side, tracer_count, *refs):
    names = ["u", "velocity", "inflow", "tables", "leaf_solve", "leaf_skeleton", "leaf_lift"]
    names += [a + "_" + b for a in ("merge", "parent", "sibling") for b in ("first", "second", "rest")]
    names += ["root_map"]
    hbm = dict(zip(names, refs[: len(names)]))
    out_ref = refs[len(names)]
    rest = refs[len(names) + 1 :]
    v = dict(zip(names, rest[: len(names)]))
    (
        load_sem, field, near, coef, force, solved,
        up_leaf, up_low, up_high, up_cross, fold, down_high, down_low, down_leaf,
        send_x, send_y, halo_x, halo_y, halo_send, halo_recv,
    ) = rest[len(names) : len(names) + 20]
    stage_refs = rest[len(names) + 20 :]
    T, L = tracer_count, leaf_side
    leaves = L * L
    rows = T * leaves
    half = SQUARE // 2

    loads = {}
    for k, name in enumerate(names):
        loads[name] = pltpu.make_async_copy(hbm[name], v[name], load_sem.at[k])
    order = ["u", "tables", "velocity", "inflow", "leaf_skeleton", "merge_first", "merge_second"]
    order += ["merge_rest", "parent_rest", "sibling_rest", "root_map", "parent_second", "parent_first"]
    order += ["leaf_lift", "leaf_solve", "sibling_first", "sibling_second"]
    for name in order:
        loads[name].start()

    place = {"gx": lax.axis_index("gx"), "gy": lax.axis_index("gy")}
    count = {"gx": lax.axis_size("gx"), "gy": lax.axis_size("gy")}
    bit_of = lambda axis, bit: lax.rem(place[axis] // (1 << bit), 2)

    def partner(stage, mask):
        target = dict(place)
        for k, (axis, bit) in enumerate(stage):
            if mask >> (len(stage) - 1 - k) & 1:
                target[axis] = target[axis] + (1 - 2 * bit_of(axis, bit)) * (1 << bit)
        return (target["gx"], target["gy"])

    barrier = pltpu.get_barrier_semaphore()
    expected = jnp.int32(0)
    has, beside = {}, {}
    for axis in ("gx", "gy"):
        for way in (-1, 1):
            spot = dict(place)
            spot[axis] = spot[axis] + way
            beside[axis, way] = (spot["gx"], spot["gy"])
            has[axis, way] = place[axis] > 0 if way < 0 else place[axis] < count[axis] - 1

            @pl.when(has[axis, way])
            def _(axis=axis, way=way):
                pl.semaphore_signal(barrier, inc=1, device_id=beside[axis, way], device_id_type=MESH)

            expected = expected + jnp.where(has[axis, way], 1, 0)
    for stage in stages:
        for mask in reversed(range(1, 1 << len(stage))):
            pl.semaphore_signal(barrier, inc=1, device_id=partner(stage, mask), device_id_type=MESH)
            expected = expected + 1

    def spot_of(i, j):
        return sum(
            ((i >> b & 1) << (5 - 2 * b)) + ((j >> b & 1) << (4 - 2 * b)) for b in range(3)
        )

    grid = sorted((spot_of(i, j), i, j) for i in range(L) for j in range(L))
    block = lambda i, j: slice(spot_of(i, j) * T, spot_of(i, j) * T + T)
    by_tracer = lambda i, j, h: pl.ds(h * rows + i * L + j, T, stride=leaves)

    loads["u"].wait()
    plain = v["u"][...].astype(F32).reshape(rows, SQUARE)
    for h in range(2):
        field[h * rows : (h + 1) * rows, :] = plain[:, h * half : (h + 1) * half]
    u = jnp.concatenate(
        [
            jnp.concatenate([field[by_tracer(i, j, h), :] for _, i, j in grid], axis=0)
            for h in range(2)
        ],
        axis=1,
    )
    force[...] = u
    loads["tables"].wait()
    near[...] = dot(u.astype(BF16), v["tables"][:, 4 * SQUARE :])
    line = lambda spots, c: jnp.concatenate(
        [near[block(i, j), c * half : (c + 1) * half] for i, j in spots], axis=0
    )
    side = lambda axis, k: [(k, m) if axis == "gx" else (m, k) for m in range(L)]
    send_x[1] = line(side("gx", L - 1), 0).astype(BF16)
    send_x[0] = line(side("gx", 0), 1).astype(BF16)
    for k in range(2):
        spots = side("gy", k * (L - 1))
        send_y[k] = (line(spots, 2) + pltpu.roll(line(spots, 3), 2, 1)).astype(BF16)
    def halo_copy(axis, way):
        k = 0 if way < 0 else 1
        source, target = (send_x, halo_x) if axis == "gx" else (send_y, halo_y)
        slot = k + (0 if axis == "gx" else 2)
        return pltpu.make_async_remote_copy(
            src_ref=source.at[k],
            dst_ref=target.at[k],
            send_sem=halo_send.at[slot],
            recv_sem=halo_recv.at[slot],
            device_id=beside[axis, way],
            device_id_type=MESH,
        )

    sides = [("gy", -1), ("gy", 1), ("gx", -1), ("gx", 1)]
    plan = [entry for stage in stages for entry in stage]
    bits = [bit_of(axis, bit) for axis, bit in plan]
    own_half = lambda k, w: jnp.where(bits[k] == 1, w[:, 128:], w[:, :128])
    twice = lambda w, axis: jnp.concatenate([w, w], axis=axis)
    merge = lambda k: v["merge_rest"][k]
    parent = lambda k: v["parent_rest"][k]

    own_parent = lambda k: own_half(k, parent(4 + k))

    def chained():
        chain = [own_parent(0)]
        for k in range(1, len(plan)):
            step = own_parent(k)
            if k > 1:
                step = product(step, split(own_parent(k - 1)))
            chain.append(product(step, split(chain[max(k - 2, 0)])))
        return chain

    def folded(levels, top, siblings, chain=()):
        weights = top
        for k in reversed(levels):
            groups = 1 << (levels[-1] - k)
            if weights is not None:
                weights = product(merge(4 + k), split(weights))
            elif siblings:
                weights = jnp.zeros((256, 128), F32)
            else:
                weights = merge(4 + k)
            blocks = [weights[:, g * 128 : (g + 1) * 128] for g in range(groups)]
            if siblings:
                sibling = own_half(k, v["sibling_rest"][4 + k])
                if k > 0:
                    sibling = product(sibling, split(chain[k - 1]))
                mine = jnp.int32(0)
                for later in levels:
                    if later > k:
                        mine = mine + bits[later] * (1 << (levels[-1] - later))
                blocks = [x + jnp.where(mine == g, sibling, 0.0) for g, x in enumerate(blocks)]
            weights = jnp.concatenate([x[:128] for x in blocks] + [x[128:] for x in blocks], axis=1)
        return lanes_to_rows(weights)

    first = len(plan) - len(stages[-1])
    last_levels = list(range(first, len(plan)))
    direct, folds = last_levels[: -FOLDED], last_levels[-FOLDED:]
    assert len(direct) == 2
    slots, groups = 1 << len(last_levels), 1 << len(folds)

    def prepare_up():
        for name in ("leaf_skeleton", "merge_first", "merge_second", "merge_rest"):
            loads[name].wait()
        two = [
            product(v["merge_first"][...].T, split(v["merge_second"][d * 64 : (d + 1) * 64, :]))
            for d in range(2)
        ]
        four = jnp.concatenate([two[d][c * 64 : (c + 1) * 64] for c in range(2) for d in range(2)], axis=1)
        up_leaf[...] = wide_split(lanes_to_rows(product(v["leaf_skeleton"][...].T, split(four))))
        up_low[...] = wide_split(merge_pair(merge(0), merge(1)))
        up_high[...] = wide_split(merge_pair(merge(2), merge(3)))
        up_cross[...] = wide_split(folded(direct, None, False))


    def prepare_down():
        for name in ("parent_rest", "sibling_rest", "root_map"):
            loads[name].wait()
        chain = chained()
        top = product(product(v["root_map"][...], split(own_parent(len(plan) - 1))), split(chain[-2]))
        fold[: groups * 128, :] = wide_split(folded(folds, top, True, chain))
        fold[groups * 128 :, :] = wide_split(folded(direct, None, True, chain))
        down_high[...] = tall_split(parent_pair(parent(3), parent(2)))
        down_low[...] = tall_split(parent_pair(parent(1), parent(0)))
        for name in ("parent_second", "parent_first", "leaf_lift"):
            loads[name].wait()
        halves = lambda x: jnp.concatenate([x, pltpu.roll(x, 64, 1)], axis=0)[:, :64]
        lifts = product(halves(v["parent_first"][...]), split(v["leaf_lift"][...]))
        lifts = jnp.concatenate([lifts[:64], lifts[64:]], axis=1)
        lifts = product(halves(v["parent_second"][...]), split(lifts))
        down_leaf[...] = tall_split(
            jnp.concatenate(
                [
                    lifts[d * 128 : (d + 1) * 128, c * SQUARE : (c + 1) * SQUARE]
                    for c in range(2)
                    for d in range(2)
                ],
                axis=1,
            )
        )

    own = lax.broadcasted_iota(jnp.int32, (leaves, L), 0) % L == lanes((leaves, L))

    def column(values):
        wide = jnp.concatenate(
            [jnp.broadcast_to(values[i : i + 1, :], (L, L)) for i in range(L)], axis=0
        )
        return jnp.sum(jnp.where(own, wide, 0.0), axis=1, keepdims=True)

    tile = (T, half)
    on_0, on_1 = lanes(tile) < NODE, lanes(tile) >= half - NODE
    on_2, on_3 = lanes(tile) % NODE == 0, lanes(tile) % NODE == NODE - 1
    at_leaf = lambda k, i, j: jnp.broadcast_to(coef[k, i * L + j : i * L + j + 1, :], tile)
    keep_if = lambda mask, x: jnp.where(mask, x, 0.0)
    strength = lambda s, i, j: at_leaf(2 + s, i, j)


    def interior():
        loads["velocity"].wait()
        loads["inflow"].wait()
        speed = [v["velocity"][k] for k in range(2)]
        columns = [column(x) for x in speed]
        columns += [
            column(v["inflow"][s].astype(F32) * (NODE * jnp.abs(speed[s // 2]))) for s in range(4)
        ]
        for k, x in enumerate(columns):
            coef[k] = jnp.broadcast_to(x, (leaves, half))

        for q in range(4):
            low, top = q * rows // 4, (q + 1) * rows // 4
            u = force[low:top, :]
            part = u.astype(BF16)
            grads = dot(part, v["tables"][:, : 2 * SQUARE])
            grads = grads + dot(part, v["tables"][:, 2 * SQUARE : 4 * SQUARE])
            for spot, i, j in grid[q * leaves // 4 : (q + 1) * leaves // 4]:
                at = slice(spot * T, spot * T + T)
                inside = slice(spot * T - low, spot * T + T - low)
                speeds = [at_leaf(k, i, j) for k in range(2)]
                w = [strength(s, i, j) for s in range(4)]
                w_2, w_3 = keep_if(on_2, w[2]), keep_if(on_3, w[3])
                for c in range(2):
                    cut = slice(c * half, (c + 1) * half)
                    far = slice((2 + c) * half, (3 + c) * half)
                    total = u[inside, cut] * (1.0 - (keep_if((on_0, on_1)[c], w[c]) + w_2 + w_3))
                    total = total - speeds[0] * grads[inside, cut] - speeds[1] * grads[inside, far]
                    ahead = i - 1 if c == 0 else i + 1
                    if 0 <= ahead < L:
                        total = total + w[c] * near[block(ahead, j), cut]
                    if j > 0:
                        total = total + w_2 * near[block(i, j - 1), far]
                    if j < L - 1:
                        total = total + w_3 * near[block(i, j + 1), far]
                    force[at, cut] = total


    def announce():
        pl.semaphore_wait(barrier, expected)
        for axis, way in sides:

            @pl.when(has[axis, way])
            def _(axis=axis, way=way):
                halo_copy(axis, way).start()


    announce()
    prepare_up()
    interior()

    for axis, way in sides:
        slot = 1 if way < 0 else 0

        @pl.when(has[axis, way])
        def _(axis=axis, way=way):
            halo_copy(axis, -way).wait_recv()

        @pl.when(jnp.logical_not(has[axis, way]))
        def _(axis=axis, slot=slot):
            target = halo_x if axis == "gx" else halo_y
            target[slot] = jnp.zeros_like(target[slot])

    for axis, way in sides:
        slot = 1 if way < 0 else 0
        arrived = (halo_x if axis == "gx" else halo_y)[slot].astype(F32)
        shifted = pltpu.roll(arrived, 126, 1) if axis == "gy" else None
        for m, (i, j) in enumerate(side(axis, 0 if way < 0 else L - 1)):
            inside = slice(m * T, m * T + T)
            if axis == "gx":
                c = 0 if way < 0 else 1
                cut = slice(c * half, (c + 1) * half)
                force[block(i, j), cut] = force[block(i, j), cut] + strength(c, i, j) * arrived[inside]
            else:
                w = keep_if(on_2, strength(2, i, j)) if way < 0 else keep_if(on_3, strength(3, i, j))
                for c, x in enumerate((arrived, shifted)):
                    cut = slice(c * half, (c + 1) * half)
                    force[block(i, j), cut] = force[block(i, j), cut] + w * x[inside]

    high, low = split(rows_to_lanes(force[...], 4))
    wide = dot(high, up_leaf[...])
    current_16 = wide[:, :128] + wide[:, 128:] + dot(low, up_leaf[:, :128])
    current_4 = narrow(rows_to_lanes(current_16, 4), up_low[...])
    current = narrow(rows_to_lanes(current_4, 4), up_high[...])

    joined = lambda x: rows_to_lanes(x, 2)
    level = 4
    path = []
    for number, stage in enumerate(stages):
        pool, stage_send, stage_recv = stage_refs[3 * number : 3 * number + 3]
        own_slot = jnp.int32(0)
        for axis, bit in stage:
            own_slot = own_slot * 2 + bit_of(axis, bit)
        pool[own_slot] = current
        copies = [
            pltpu.make_async_remote_copy(
                src_ref=pool.at[own_slot],
                dst_ref=pool.at[own_slot],
                send_sem=stage_send.at[mask],
                recv_sem=stage_recv.at[mask],
                device_id=partner(stage, mask),
                device_id_type=MESH,
            )
            for mask in range(1, 1 << len(stage))
        ]
        for copy in reversed(copies):
            copy.start()
        if number == 0:
            prepare_down()
            for name in ("leaf_solve", "sibling_first", "sibling_second"):
                loads[name].wait()
            forcing = force[...]
            sibling = lambda k: split(v["sibling_rest"][k])
            is_left = lambda x: left_half(x.shape)

            def gathered(x):
                middle = x.shape[0] // 2
                return jnp.where(is_left(x[:middle]), x[:middle], x[middle:])

            cat_0 = gathered(product(forcing, split(twice(v["leaf_skeleton"][...], 0).T)))
            cat_1 = gathered(product(cat_0, split(twice(v["merge_first"][...], 0).T)))
            cats = [joined(current_16)]
            cats.append(joined(product(cats[0], split(merge(0)))))
            cats.append(joined(current_4))
            cats.append(joined(product(cats[2], split(merge(2)))))
            own_part = product(cats[3], sibling(3))
            for k in (2, 1, 0):
                own_part = product(lanes_to_rows(own_part), split(parent(k)))
                own_part = own_part + product(cats[k], sibling(k))
            own_part = product(lanes_to_rows(own_part), split(v["parent_second"][...]))
            own_part = own_part + product(cat_1, split(v["sibling_second"][...]))
            own_part = spread_product(own_part, split(v["parent_first"][...]))
            own_part = own_part + product(cat_0, split(v["sibling_first"][...]))
            own_part = spread_product(own_part, split(v["leaf_lift"][...]))
            solved[...] = own_part + product(forcing, split(v["leaf_solve"][...]))
        if number == len(stages) - 1:
            known = jnp.zeros((T, 128), F32)
            chain = chained() if path else ()
            for k, term in enumerate(path):
                term = own_half(k, term)
                known = known + (product(term, split(chain[k - 1])) if k > 0 else term)
        for copy in copies:
            copy.wait()
        if number == len(stages) - 1:
            break
        current = pool[...].reshape(T << len(stage), 128)
        for k, (axis, bit) in enumerate(stage):
            cat = joined(current)
            mine = cat
            for later_axis, later_bit in stage[k + 1 :]:
                middle = mine.shape[0] // 2
                mine = jnp.where(bit_of(later_axis, later_bit) == 1, mine[middle:], mine[:middle])
            path.append(product(mine, split(v["sibling_rest"][level])))
            current = product(cat, split(merge(level)))
            level += 1

    everyone = pool[...].reshape(slots * T, 128)
    merged = narrow(rows_to_lanes(everyone, slots // groups), up_cross[...])
    mine = jnp.int32(0)
    for k in folds:
        mine = mine * 2 + bits[k]
    slabs = [rows_to_lanes(merged, groups)]
    slabs += [pool[k * groups + mine] for k in range(slots // groups)]
    boundary = narrow(jnp.concatenate(slabs, axis=1), fold[...]) + known
    boundary = lanes_to_rows(broad(boundary, down_high[...]))
    boundary = lanes_to_rows(broad(boundary, down_low[...]))
    high, low = split(boundary)
    lifted = dot(twice(high, 1), down_leaf[...]) + dot(low, down_leaf[:128, :])
    for spot, i, j in grid:
        q, inside = divmod(spot, leaves // 4)
        for h in range(2):
            at = q * SQUARE + h * half
            one = lifted[inside * T : (inside + 1) * T, at : at + half]
            one = one + solved[spot * T : spot * T + T, h * half : (h + 1) * half]
            field[by_tracer(i, j, h), :] = one
    updated = jnp.concatenate([field[:rows, :], field[rows:, :]], axis=1)
    out_ref[...] = updated.reshape(out_ref.shape).astype(out_ref.dtype)
    for axis, way in sides:

        @pl.when(has[axis, way])
        def _(axis=axis, way=way):
            halo_copy(axis, way).wait_send()


def local(tables, count_first, count_second, tracers, *operands):
    T, L = tracers.shape[0], tracers.shape[1]
    assert L == 8 and local_plan(L) == [1, 2] * 3
    stages = staged(cross_plan(count_first, count_second))
    rows = T * L * L
    args = [tracers, operands[0], operands[1], tables] + list(operands[2:])
    args[5], args[7] = args[5].T, args[7].T
    vmem, dma = pltpu.VMEM, pltpu.SemaphoreType.DMA
    scratch = [vmem(a.shape, a.dtype) for a in args]
    slots = 1 << len(stages[-1])
    groups = 1 << FOLDED
    scratch += [
        dma((len(args),)),
        vmem((2 * rows, 128), F32),
        vmem((rows, 2 * SQUARE), F32),
        vmem((6, L * L, 128), F32),
        vmem((rows, SQUARE), F32),
        vmem((rows, SQUARE), F32),
        vmem((4 * SQUARE, 256), BF16),
        vmem((512, 256), BF16),
        vmem((512, 256), BF16),
        vmem((slots // groups * 128, 256), BF16),
        vmem(((groups + slots // groups) * 128, 256), BF16),
        vmem((256, 512), BF16),
        vmem((256, 512), BF16),
        vmem((256, 4 * SQUARE), BF16),
        vmem((2, T * L, 128), BF16),
        vmem((2, T * L, 128), BF16),
        vmem((2, T * L, 128), BF16),
        vmem((2, T * L, 128), BF16),
        dma((4,)),
        dma((4,)),
    ]
    for stage in stages:
        slots = 1 << len(stage)
        scratch += [vmem((slots, T, 128), F32), dma((slots,)), dma((slots,))]
    return pl.pallas_call(
        functools.partial(kernel, stages, L, T),
        out_shape=jax.ShapeDtypeStruct(tracers.shape, tracers.dtype),
        in_specs=[pl.BlockSpec(memory_space=pl.ANY)] * len(args),
        out_specs=pl.BlockSpec(memory_space=pltpu.VMEM),
        scratch_shapes=scratch,
        compiler_params=pltpu.CompilerParams(
            collective_id=0, has_side_effects=True, vmem_limit_bytes=VMEM_LIMIT
        ),
    )(*[pltpu.with_memory_space_constraint(a, pltpu.HBM) for a in args])


def solution(mesh):
    tables = point_tables()
    split_both = P(None, "gx", "gy")
    in_specs = (P(None, "gx", "gy", None), split_both, split_both) + (P(),) * 13

    def body(*args):
        return local(
            jnp.asarray(tables), mesh.shape["gx"], mesh.shape["gy"], *args
        )

    return jax.shard_map(
        body,
        mesh=mesh,
        in_specs=in_specs,
        out_specs=P(None, "gx", "gy", None),
        check_vma=False,
    )
```

```python
import functools

import jax
import jax.numpy as jnp
import numpy as np
from jax import lax
from jax.experimental import pallas as pl
from jax.experimental.pallas import tpu as pltpu
from jax.sharding import PartitionSpec as P

NODE = 16
SQUARE = NODE * NODE
F32 = jnp.float32
BF16 = jnp.bfloat16
VMEM_LIMIT = 32 * 1024 * 1024
MESH = pl.DeviceIdType.MESH
LAST_STAGE = 5
FOLDED = 3


def local_plan(leaf_side):
    merge_plan = []
    block_span = leaf_side
    while block_span > 1:
        merge_plan = merge_plan + [1, 2]
        block_span = block_span // 2
    return merge_plan


def cross_plan(count_first, count_second):
    merge_plan = []
    bits = {"gx": 0, "gy": 0}
    while count_first * count_second > 1:
        if count_first >= count_second:
            axis, count_first = "gx", count_first // 2
        else:
            axis, count_second = "gy", count_second // 2
        merge_plan.append((axis, bits[axis]))
        bits[axis] += 1
    return merge_plan


def staged(plan):
    stages, rest = [], list(plan)
    while len(rest) > LAST_STAGE:
        size = min(3, len(rest) - LAST_STAGE)
        stages.append(rest[:size])
        rest = rest[size:]
    return stages + [rest]


def point_tables():
    index = np.arange(NODE)
    points = -np.cos(np.pi * index / (NODE - 1))
    weights = np.where(index % 2 == 0, 1.0, -1.0)
    weights[[0, NODE - 1]] *= 2.0
    eye = np.eye(NODE)
    matrix = weights[:, None] / weights[None, :] / (points[:, None] - points[None, :] + eye)
    matrix = matrix * (1.0 - eye)
    matrix = matrix - np.diag(matrix.sum(axis=1))
    both = np.concatenate([np.kron(matrix, eye).T, np.kron(eye, matrix).T], axis=1)
    both = both.astype(np.float32)
    high = both.astype(jnp.bfloat16)
    low = (both - high.astype(np.float32)).astype(jnp.bfloat16)
    facing = np.zeros((SQUARE, 2 * SQUARE), np.float32)
    last = NODE - 1
    for k in range(NODE):
        facing[last * NODE + k, k] = 1.0
        facing[k, last * NODE + k] = 1.0
        facing[k * NODE + last, SQUARE + k * NODE] = 1.0
        facing[k * NODE, SQUARE + k * NODE + last] = 1.0
    return np.concatenate([high, low, facing.astype(jnp.bfloat16)], axis=1)


def split(x):
    high = x.astype(BF16)
    return high, (x - high.astype(F32)).astype(BF16)


def dot(left, right):
    return jnp.dot(left, right, preferred_element_type=F32)


def product(x, weight):
    high, low = weight
    rows, depth = x.shape
    wide = high.shape[1]
    if rows < 64:
        rest = x - x.astype(BF16).astype(F32)
        both = jnp.concatenate([x, rest], axis=0).astype(BF16)
        if depth == 128:
            both = jnp.concatenate([both, both], axis=1)
            out = dot(both, jnp.concatenate([high, low], axis=0))
        else:
            out = dot(both, high) + dot(both, low)
        return out[:rows] + out[rows:]
    x_high, x_low = split(x)
    if wide == 128:
        weights = jnp.concatenate([high, low], axis=1)
        if depth == 128:
            weights = jnp.concatenate([weights, weights], axis=0)
            out = dot(jnp.concatenate([x_high, x_low], axis=1), weights)
            return out[:, :128] + out[:, 128:]
        out = dot(x_high, weights)
        return out[:, :128] + dot(x_low, high) + out[:, 128:]
    if depth == 128:
        out = dot(jnp.concatenate([x_high, x_high], axis=1), jnp.concatenate([high, low], axis=0))
        return out + dot(x_low, high)
    return dot(x_high, high) + dot(x_low, high) + dot(x_high, low)


def spread_product(x, weight):
    high, low = split(x)
    moved = pltpu.roll(x - high.astype(F32), 64, 1).astype(BF16)
    is_left = left_half(x.shape)
    zero = jnp.zeros_like(high)
    first = [jnp.where(is_left, high, moved), jnp.where(is_left, high, zero)]
    second = [jnp.where(is_left, moved, high), jnp.where(is_left, zero, high)]
    both = jnp.concatenate([jnp.concatenate(k, axis=1) for k in (first, second)], axis=0)
    return dot(both, jnp.concatenate([weight[0]] * 2 + [weight[1]] * 2, axis=0))


def lanes(shape):
    return lax.broadcasted_iota(jnp.int32, shape, len(shape) - 1)


def left_half(shape):
    return lanes(shape) < shape[-1] // 2


def narrow(x, table):
    rows = x.shape[0]
    rest = x - x.astype(BF16).astype(F32)
    out = dot(jnp.concatenate([x, rest], axis=0).astype(BF16), table)
    out = out[:rows] + out[rows:]
    return out[:, :128] + out[:, 128:]


def broad(x, table):
    rows = x.shape[0]
    rest = x - x.astype(BF16).astype(F32)
    both = jnp.concatenate([x, rest], axis=0).astype(BF16)
    out = dot(jnp.concatenate([both, both], axis=1), table)
    return out[:rows] + out[rows:]


def rows_to_lanes(x, count):
    size = x.shape[0] // count
    return jnp.concatenate([x[k * size : (k + 1) * size] for k in range(count)], axis=1)


def lanes_to_rows(x):
    return jnp.concatenate([x[:, k : k + 128] for k in range(0, x.shape[1], 128)], axis=0)


def quarters(x):
    return [x[:128, :128], x[:128, 128:], x[128:, :128], x[128:, 128:]]


def merge_pair(former, latter):
    wide = product(former, split(rows_to_lanes(latter, 2)))
    return jnp.concatenate(quarters(wide), axis=0)


def parent_pair(upper, lower):
    a, b, c, d = quarters(product(lanes_to_rows(upper), split(lower)))
    return jnp.concatenate([a, c, b, d], axis=1)


def wide_split(x):
    return jnp.concatenate(split(x), axis=1)


def tall_split(x):
    return jnp.concatenate(split(x), axis=0)


def kernel(stages, leaf_side, tracer_count, *refs):
    names = ["u", "velocity", "inflow", "tables", "leaf_solve", "leaf_skeleton", "leaf_lift"]
    names += [a + "_" + b for a in ("merge", "parent", "sibling") for b in ("first", "second", "rest")]
    names += ["root_map"]
    hbm = dict(zip(names, refs[: len(names)]))
    out_ref = refs[len(names)]
    rest = refs[len(names) + 1 :]
    v = dict(zip(names, rest[: len(names)]))
    (
        load_sem, field, near, coef, force, solved,
        up_leaf, up_low, up_high, up_cross, fold, down_high, down_low, down_leaf,
        send_x, send_y, halo_x, halo_y, halo_send, halo_recv, here,
    ) = rest[len(names) : len(names) + 21]
    stage_refs = rest[len(names) + 21 :]
    T, L = tracer_count, leaf_side
    leaves = L * L
    rows = T * leaves
    half = SQUARE // 2

    loads = {}
    for k, name in enumerate(names):
        loads[name] = pltpu.make_async_copy(hbm[name], v[name], load_sem.at[k])
    order = ["u", "tables", "velocity", "inflow", "leaf_skeleton", "merge_first", "merge_second"]
    order += ["merge_rest", "parent_rest", "sibling_rest", "root_map", "parent_second", "parent_first"]
    order += ["leaf_lift", "leaf_solve", "sibling_first", "sibling_second"]
    for name in order:
        loads[name].start()

    place = {"gx": lax.axis_index("gx"), "gy": lax.axis_index("gy")}
    count = {"gx": lax.axis_size("gx"), "gy": lax.axis_size("gy")}
    bit_of = lambda axis, bit: lax.rem(place[axis] // (1 << bit), 2)

    def partner(stage, mask):
        target = dict(place)
        for k, (axis, bit) in enumerate(stage):
            if mask >> (len(stage) - 1 - k) & 1:
                target[axis] = target[axis] + (1 - 2 * bit_of(axis, bit)) * (1 << bit)
        return (target["gx"], target["gy"])

    barrier = pltpu.get_barrier_semaphore()
    expected = jnp.int32(0)
    has, beside = {}, {}
    for axis in ("gx", "gy"):
        for way in (-1, 1):
            spot = dict(place)
            spot[axis] = spot[axis] + way
            beside[axis, way] = (spot["gx"], spot["gy"])
            has[axis, way] = place[axis] > 0 if way < 0 else place[axis] < count[axis] - 1

            @pl.when(has[axis, way])
            def _(axis=axis, way=way):
                pl.semaphore_signal(barrier, inc=1, device_id=beside[axis, way], device_id_type=MESH)

            expected = expected + jnp.where(has[axis, way], 1, 0)
    for stage in stages[:-1]:
        for mask in range(1, 1 << len(stage)):
            pl.semaphore_signal(barrier, inc=1, device_id=partner(stage, mask), device_id_type=MESH)
            expected = expected + 1

    by_rank = sorted(stages[-1], key=lambda e: (e == ("gx", 0), e[0] == "gy", -e[1]))
    slots = 1 << len(by_rank)
    rank = jnp.int32(0)
    for axis, bit in by_rank:
        rank = rank * 2 + bit_of(axis, bit)

    def ranked(number):
        target = dict(place)
        for k, (axis, bit) in enumerate(reversed(by_rank)):
            wanted = lax.rem(number // (1 << k), 2)
            target[axis] = target[axis] + (wanted - bit_of(axis, bit)) * (1 << bit)
        return (target["gx"], target["gy"])

    def greet(number, carry):
        pl.semaphore_signal(barrier, inc=1, device_id=ranked(number), device_id_type=MESH)
        return carry

    def answer(number, carry):
        pl.semaphore_signal(here, inc=1, device_id=ranked(number), device_id_type=MESH)
        return carry

    lax.fori_loop(rank + 1, slots, greet, 0)
    expected = expected + rank

    def spot_of(i, j):
        return sum(
            ((i >> b & 1) << (5 - 2 * b)) + ((j >> b & 1) << (4 - 2 * b)) for b in range(3)
        )

    grid = sorted((spot_of(i, j), i, j) for i in range(L) for j in range(L))
    block = lambda i, j: slice(spot_of(i, j) * T, spot_of(i, j) * T + T)
    by_tracer = lambda i, j, h: pl.ds(h * rows + i * L + j, T, stride=leaves)

    loads["u"].wait()
    plain = v["u"][...].astype(F32).reshape(rows, SQUARE)
    for h in range(2):
        field[h * rows : (h + 1) * rows, :] = plain[:, h * half : (h + 1) * half]
    u = jnp.concatenate(
        [
            jnp.concatenate([field[by_tracer(i, j, h), :] for _, i, j in grid], axis=0)
            for h in range(2)
        ],
        axis=1,
    )
    force[...] = u
    loads["tables"].wait()
    near[...] = dot(u.astype(BF16), v["tables"][:, 4 * SQUARE :])
    line = lambda spots, c: jnp.concatenate(
        [near[block(i, j), c * half : (c + 1) * half] for i, j in spots], axis=0
    )
    side = lambda axis, k: [(k, m) if axis == "gx" else (m, k) for m in range(L)]
    send_x[1] = line(side("gx", L - 1), 0).astype(BF16)
    send_x[0] = line(side("gx", 0), 1).astype(BF16)
    for k in range(2):
        spots = side("gy", k * (L - 1))
        send_y[k] = (line(spots, 2) + pltpu.roll(line(spots, 3), 2, 1)).astype(BF16)
    def halo_copy(axis, way):
        k = 0 if way < 0 else 1
        source, target = (send_x, halo_x) if axis == "gx" else (send_y, halo_y)
        slot = k + (0 if axis == "gx" else 2)
        return pltpu.make_async_remote_copy(
            src_ref=source.at[k],
            dst_ref=target.at[k],
            send_sem=halo_send.at[slot],
            recv_sem=halo_recv.at[slot],
            device_id=beside[axis, way],
            device_id_type=MESH,
        )

    sides = [("gy", -1), ("gy", 1), ("gx", -1), ("gx", 1)]
    plan = [entry for stage in stages for entry in stage]
    bits = [bit_of(axis, bit) for axis, bit in plan]
    own_half = lambda k, w: jnp.where(bits[k] == 1, w[:, 128:], w[:, :128])
    twice = lambda w, axis: jnp.concatenate([w, w], axis=axis)
    merge = lambda k: v["merge_rest"][k]
    parent = lambda k: v["parent_rest"][k]

    own_parent = lambda k: own_half(k, parent(4 + k))

    def chained():
        chain = [own_parent(0)]
        for k in range(1, len(plan)):
            step = own_parent(k)
            if k > 1:
                step = product(step, split(own_parent(k - 1)))
            chain.append(product(step, split(chain[max(k - 2, 0)])))
        return chain

    def folded(levels, top, siblings, chain=()):
        weights = top
        for k in reversed(levels):
            groups = 1 << (levels[-1] - k)
            if weights is not None:
                weights = product(merge(4 + k), split(weights))
            elif siblings:
                weights = jnp.zeros((256, 128), F32)
            else:
                weights = merge(4 + k)
            blocks = [weights[:, g * 128 : (g + 1) * 128] for g in range(groups)]
            if siblings:
                sibling = own_half(k, v["sibling_rest"][4 + k])
                if k > 0:
                    sibling = product(sibling, split(chain[k - 1]))
                mine = jnp.int32(0)
                for later in levels:
                    if later > k:
                        mine = mine + bits[later] * (1 << (levels[-1] - later))
                blocks = [x + jnp.where(mine == g, sibling, 0.0) for g, x in enumerate(blocks)]
            weights = jnp.concatenate([x[:128] for x in blocks] + [x[128:] for x in blocks], axis=1)
        return lanes_to_rows(weights)

    first = len(plan) - len(stages[-1])
    last_levels = list(range(first, len(plan)))
    direct, folds = last_levels[: -FOLDED], last_levels[-FOLDED:]
    assert len(direct) == 2
    groups = 1 << len(folds)

    def prepare_up():
        for name in ("leaf_skeleton", "merge_first", "merge_second", "merge_rest"):
            loads[name].wait()
        two = [
            product(v["merge_first"][...].T, split(v["merge_second"][d * 64 : (d + 1) * 64, :]))
            for d in range(2)
        ]
        four = jnp.concatenate([two[d][c * 64 : (c + 1) * 64] for c in range(2) for d in range(2)], axis=1)
        up_leaf[...] = wide_split(lanes_to_rows(product(v["leaf_skeleton"][...].T, split(four))))
        up_low[...] = wide_split(merge_pair(merge(0), merge(1)))
        up_high[...] = wide_split(merge_pair(merge(2), merge(3)))
        up_cross[...] = wide_split(folded(direct, None, False))


    def prepare_down():
        for name in ("parent_rest", "sibling_rest", "root_map"):
            loads[name].wait()
        chain = chained()
        top = product(product(v["root_map"][...], split(own_parent(len(plan) - 1))), split(chain[-2]))
        fold[: groups * 128, :] = wide_split(folded(folds, top, True, chain))
        fold[groups * 128 :, :] = wide_split(folded(direct, None, True, chain))
        down_high[...] = tall_split(parent_pair(parent(3), parent(2)))
        down_low[...] = tall_split(parent_pair(parent(1), parent(0)))
        for name in ("parent_second", "parent_first", "leaf_lift"):
            loads[name].wait()
        halves = lambda x: jnp.concatenate([x, pltpu.roll(x, 64, 1)], axis=0)[:, :64]
        lifts = product(halves(v["parent_first"][...]), split(v["leaf_lift"][...]))
        lifts = jnp.concatenate([lifts[:64], lifts[64:]], axis=1)
        lifts = product(halves(v["parent_second"][...]), split(lifts))
        down_leaf[...] = tall_split(
            jnp.concatenate(
                [
                    lifts[d * 128 : (d + 1) * 128, c * SQUARE : (c + 1) * SQUARE]
                    for c in range(2)
                    for d in range(2)
                ],
                axis=1,
            )
        )

    own = lax.broadcasted_iota(jnp.int32, (leaves, L), 0) % L == lanes((leaves, L))

    def column(values):
        wide = jnp.concatenate(
            [jnp.broadcast_to(values[i : i + 1, :], (L, L)) for i in range(L)], axis=0
        )
        return jnp.sum(jnp.where(own, wide, 0.0), axis=1, keepdims=True)

    tile = (T, half)
    on_0, on_1 = lanes(tile) < NODE, lanes(tile) >= half - NODE
    on_2, on_3 = lanes(tile) % NODE == 0, lanes(tile) % NODE == NODE - 1
    at_leaf = lambda k, i, j: jnp.broadcast_to(coef[k, i * L + j : i * L + j + 1, :], tile)
    keep_if = lambda mask, x: jnp.where(mask, x, 0.0)
    strength = lambda s, i, j: at_leaf(2 + s, i, j)


    def interior():
        loads["velocity"].wait()
        loads["inflow"].wait()
        speed = [v["velocity"][k] for k in range(2)]
        columns = [column(x) for x in speed]
        columns += [
            column(v["inflow"][s].astype(F32) * (NODE * jnp.abs(speed[s // 2]))) for s in range(4)
        ]
        for k, x in enumerate(columns):
            coef[k] = jnp.broadcast_to(x, (leaves, half))

        for q in range(4):
            low, top = q * rows // 4, (q + 1) * rows // 4
            u = force[low:top, :]
            part = u.astype(BF16)
            grads = dot(part, v["tables"][:, : 2 * SQUARE])
            grads = grads + dot(part, v["tables"][:, 2 * SQUARE : 4 * SQUARE])
            for spot, i, j in grid[q * leaves // 4 : (q + 1) * leaves // 4]:
                at = slice(spot * T, spot * T + T)
                inside = slice(spot * T - low, spot * T + T - low)
                speeds = [at_leaf(k, i, j) for k in range(2)]
                w = [strength(s, i, j) for s in range(4)]
                w_2, w_3 = keep_if(on_2, w[2]), keep_if(on_3, w[3])
                for c in range(2):
                    cut = slice(c * half, (c + 1) * half)
                    far = slice((2 + c) * half, (3 + c) * half)
                    total = u[inside, cut] * (1.0 - (keep_if((on_0, on_1)[c], w[c]) + w_2 + w_3))
                    total = total - speeds[0] * grads[inside, cut] - speeds[1] * grads[inside, far]
                    ahead = i - 1 if c == 0 else i + 1
                    if 0 <= ahead < L:
                        total = total + w[c] * near[block(ahead, j), cut]
                    if j > 0:
                        total = total + w_2 * near[block(i, j - 1), far]
                    if j < L - 1:
                        total = total + w_3 * near[block(i, j + 1), far]
                    force[at, cut] = total


    def announce():
        pl.semaphore_wait(barrier, expected)
        for axis, way in sides:

            @pl.when(has[axis, way])
            def _(axis=axis, way=way):
                halo_copy(axis, way).start()

        lax.fori_loop(0, rank, answer, 0)

    announce()
    prepare_up()
    interior()

    for axis, way in sides:
        slot = 1 if way < 0 else 0

        @pl.when(has[axis, way])
        def _(axis=axis, way=way):
            halo_copy(axis, -way).wait_recv()

        @pl.when(jnp.logical_not(has[axis, way]))
        def _(axis=axis, slot=slot):
            target = halo_x if axis == "gx" else halo_y
            target[slot] = jnp.zeros_like(target[slot])

    for axis, way in sides:
        slot = 1 if way < 0 else 0
        arrived = (halo_x if axis == "gx" else halo_y)[slot].astype(F32)
        shifted = pltpu.roll(arrived, 126, 1) if axis == "gy" else None
        for m, (i, j) in enumerate(side(axis, 0 if way < 0 else L - 1)):
            inside = slice(m * T, m * T + T)
            if axis == "gx":
                c = 0 if way < 0 else 1
                cut = slice(c * half, (c + 1) * half)
                force[block(i, j), cut] = force[block(i, j), cut] + strength(c, i, j) * arrived[inside]
            else:
                w = keep_if(on_2, strength(2, i, j)) if way < 0 else keep_if(on_3, strength(3, i, j))
                for c, x in enumerate((arrived, shifted)):
                    cut = slice(c * half, (c + 1) * half)
                    force[block(i, j), cut] = force[block(i, j), cut] + w * x[inside]

    high, low = split(rows_to_lanes(force[...], 4))
    wide = dot(high, up_leaf[...])
    current_16 = wide[:, :128] + wide[:, 128:] + dot(low, up_leaf[:, :128])
    current_4 = narrow(rows_to_lanes(current_16, 4), up_low[...])
    current = narrow(rows_to_lanes(current_4, 4), up_high[...])

    joined = lambda x: rows_to_lanes(x, 2)
    level = 4
    path = []
    for number, stage in enumerate(stages):
        pool, stage_send, stage_recv = stage_refs[3 * number : 3 * number + 3]
        own_slot = jnp.int32(0)
        for axis, bit in stage:
            own_slot = own_slot * 2 + bit_of(axis, bit)
        pool[own_slot] = current
        final = number == len(stages) - 1
        copies = [] if final else [
            pltpu.make_async_remote_copy(
                src_ref=pool.at[own_slot],
                dst_ref=pool.at[own_slot],
                send_sem=stage_send.at[mask],
                recv_sem=stage_recv.at[mask],
                device_id=partner(stage, mask),
                device_id_type=MESH,
            )
            for mask in range(1, 1 << len(stage))
        ]
        for copy in reversed(copies):
            copy.start()
        if final:

            @pl.when(rank < slots - 1)
            def _():
                pl.semaphore_wait(here, slots - 1 - rank)

            others = lambda n, own: n + jnp.where(n >= own, 1, 0)
            for n in range(slots - 1):
                other = others(n, own_slot)
                sent = pltpu.make_async_remote_copy(
                    src_ref=pool.at[own_slot],
                    dst_ref=pool.at[own_slot],
                    send_sem=stage_send.at[n],
                    recv_sem=stage_recv.at[own_slot],
                    device_id=ranked(others(n, rank)),
                    device_id_type=MESH,
                )
                sent.start()
                copies.append((sent, other))
        if number == 0:
            prepare_down()
            for name in ("leaf_solve", "sibling_first", "sibling_second"):
                loads[name].wait()
            forcing = force[...]
            sibling = lambda k: split(v["sibling_rest"][k])
            is_left = lambda x: left_half(x.shape)

            def gathered(x):
                middle = x.shape[0] // 2
                return jnp.where(is_left(x[:middle]), x[:middle], x[middle:])

            cat_0 = gathered(product(forcing, split(twice(v["leaf_skeleton"][...], 0).T)))
            cat_1 = gathered(product(cat_0, split(twice(v["merge_first"][...], 0).T)))
            cats = [joined(current_16)]
            cats.append(joined(product(cats[0], split(merge(0)))))
            cats.append(joined(current_4))
            cats.append(joined(product(cats[2], split(merge(2)))))
            own_part = product(cats[3], sibling(3))
            for k in (2, 1, 0):
                own_part = product(lanes_to_rows(own_part), split(parent(k)))
                own_part = own_part + product(cats[k], sibling(k))
            own_part = product(lanes_to_rows(own_part), split(v["parent_second"][...]))
            own_part = own_part + product(cat_1, split(v["sibling_second"][...]))
            own_part = spread_product(own_part, split(v["parent_first"][...]))
            own_part = own_part + product(cat_0, split(v["sibling_first"][...]))
            own_part = spread_product(own_part, split(v["leaf_lift"][...]))
            solved[...] = own_part + product(forcing, split(v["leaf_solve"][...]))
        if final:
            known = jnp.zeros((T, 128), F32)
            chain = chained() if path else ()
            for k, term in enumerate(path):
                term = own_half(k, term)
                known = known + (product(term, split(chain[k - 1])) if k > 0 else term)
        if final:
            for n, (sent, other) in enumerate(copies):
                pltpu.make_async_remote_copy(
                    src_ref=pool.at[own_slot],
                    dst_ref=pool.at[other],
                    send_sem=stage_send.at[0],
                    recv_sem=stage_recv.at[other],
                    device_id=ranked(others(n, rank)),
                    device_id_type=MESH,
                ).wait_recv()
            break
        for copy in copies:
            copy.wait()
        current = pool[...].reshape(T << len(stage), 128)
        for k, (axis, bit) in enumerate(stage):
            cat = joined(current)
            mine = cat
            for later_axis, later_bit in stage[k + 1 :]:
                middle = mine.shape[0] // 2
                mine = jnp.where(bit_of(later_axis, later_bit) == 1, mine[middle:], mine[:middle])
            path.append(product(mine, split(v["sibling_rest"][level])))
            current = product(cat, split(merge(level)))
            level += 1

    everyone = pool[...].reshape(slots * T, 128)
    merged = narrow(rows_to_lanes(everyone, slots // groups), up_cross[...])
    mine = jnp.int32(0)
    for k in folds:
        mine = mine * 2 + bits[k]
    slabs = [rows_to_lanes(merged, groups)]
    slabs += [pool[k * groups + mine] for k in range(slots // groups)]
    boundary = narrow(jnp.concatenate(slabs, axis=1), fold[...]) + known
    boundary = lanes_to_rows(broad(boundary, down_high[...]))
    boundary = lanes_to_rows(broad(boundary, down_low[...]))
    high, low = split(boundary)
    lifted = dot(twice(high, 1), down_leaf[...]) + dot(low, down_leaf[:128, :])
    for spot, i, j in grid:
        q, inside = divmod(spot, leaves // 4)
        for h in range(2):
            at = q * SQUARE + h * half
            one = lifted[inside * T : (inside + 1) * T, at : at + half]
            one = one + solved[spot * T : spot * T + T, h * half : (h + 1) * half]
            field[by_tracer(i, j, h), :] = one
    updated = jnp.concatenate([field[:rows, :], field[rows:, :]], axis=1)
    out_ref[...] = updated.reshape(out_ref.shape).astype(out_ref.dtype)
    for sent, _ in copies:
        sent.wait_send()
    for axis, way in sides:

        @pl.when(has[axis, way])
        def _(axis=axis, way=way):
            halo_copy(axis, way).wait_send()


def local(tables, count_first, count_second, tracers, *operands):
    T, L = tracers.shape[0], tracers.shape[1]
    assert L == 8 and local_plan(L) == [1, 2] * 3
    stages = staged(cross_plan(count_first, count_second))
    rows = T * L * L
    args = [tracers, operands[0], operands[1], tables] + list(operands[2:])
    args[5], args[7] = args[5].T, args[7].T
    vmem, dma = pltpu.VMEM, pltpu.SemaphoreType.DMA
    scratch = [vmem(a.shape, a.dtype) for a in args]
    slots = 1 << len(stages[-1])
    groups = 1 << FOLDED
    scratch += [
        dma((len(args),)),
        vmem((2 * rows, 128), F32),
        vmem((rows, 2 * SQUARE), F32),
        vmem((6, L * L, 128), F32),
        vmem((rows, SQUARE), F32),
        vmem((rows, SQUARE), F32),
        vmem((4 * SQUARE, 256), BF16),
        vmem((512, 256), BF16),
        vmem((512, 256), BF16),
        vmem((slots // groups * 128, 256), BF16),
        vmem(((groups + slots // groups) * 128, 256), BF16),
        vmem((256, 512), BF16),
        vmem((256, 512), BF16),
        vmem((256, 4 * SQUARE), BF16),
        vmem((2, T * L, 128), BF16),
        vmem((2, T * L, 128), BF16),
        vmem((2, T * L, 128), BF16),
        vmem((2, T * L, 128), BF16),
        dma((4,)),
        dma((4,)),
        pltpu.SemaphoreType.REGULAR,
    ]
    for stage in stages:
        slots = 1 << len(stage)
        scratch += [vmem((slots, T, 128), F32), dma((slots,)), dma((slots,))]
    return pl.pallas_call(
        functools.partial(kernel, stages, L, T),
        out_shape=jax.ShapeDtypeStruct(tracers.shape, tracers.dtype),
        in_specs=[pl.BlockSpec(memory_space=pl.ANY)] * len(args),
        out_specs=pl.BlockSpec(memory_space=pltpu.VMEM),
        scratch_shapes=scratch,
        compiler_params=pltpu.CompilerParams(
            collective_id=0, has_side_effects=True, vmem_limit_bytes=VMEM_LIMIT
        ),
    )(*[pltpu.with_memory_space_constraint(a, pltpu.HBM) for a in args])


def solution(mesh):
    tables = point_tables()
    split_both = P(None, "gx", "gy")
    in_specs = (P(None, "gx", "gy", None), split_both, split_both) + (P(),) * 13

    def body(*args):
        return local(
            jnp.asarray(tables), mesh.shape["gx"], mesh.shape["gy"], *args
        )

    return jax.shard_map(
        body,
        mesh=mesh,
        in_specs=in_specs,
        out_specs=P(None, "gx", "gy", None),
        check_vma=False,
    )
```

```python
import functools

import jax
import jax.numpy as jnp
import numpy as np
from jax import lax
from jax.experimental import pallas as pl
from jax.experimental.pallas import tpu as pltpu
from jax.sharding import PartitionSpec as P

NODE = 16
SQUARE = NODE * NODE
F32 = jnp.float32
BF16 = jnp.bfloat16
VMEM_LIMIT = 32 * 1024 * 1024
MESH = pl.DeviceIdType.MESH
LAST_STAGE = 5
FOLDED = 3


def local_plan(leaf_side):
    merge_plan = []
    block_span = leaf_side
    while block_span > 1:
        merge_plan = merge_plan + [1, 2]
        block_span = block_span // 2
    return merge_plan


def cross_plan(count_first, count_second):
    merge_plan = []
    bits = {"gx": 0, "gy": 0}
    while count_first * count_second > 1:
        if count_first >= count_second:
            axis, count_first = "gx", count_first // 2
        else:
            axis, count_second = "gy", count_second // 2
        merge_plan.append((axis, bits[axis]))
        bits[axis] += 1
    return merge_plan


def staged(plan):
    stages, rest = [], list(plan)
    while len(rest) > LAST_STAGE:
        size = min(3, len(rest) - LAST_STAGE)
        stages.append(rest[:size])
        rest = rest[size:]
    return stages + [rest]


def point_tables():
    index = np.arange(NODE)
    points = -np.cos(np.pi * index / (NODE - 1))
    weights = np.where(index % 2 == 0, 1.0, -1.0)
    weights[[0, NODE - 1]] *= 2.0
    eye = np.eye(NODE)
    matrix = weights[:, None] / weights[None, :] / (points[:, None] - points[None, :] + eye)
    matrix = matrix * (1.0 - eye)
    matrix = matrix - np.diag(matrix.sum(axis=1))
    both = np.concatenate([np.kron(matrix, eye).T, np.kron(eye, matrix).T], axis=1)
    both = both.astype(np.float32)
    high = both.astype(jnp.bfloat16)
    low = (both - high.astype(np.float32)).astype(jnp.bfloat16)
    facing = np.zeros((SQUARE, 2 * SQUARE), np.float32)
    last = NODE - 1
    for k in range(NODE):
        facing[last * NODE + k, k] = 1.0
        facing[k, last * NODE + k] = 1.0
        facing[k * NODE + last, SQUARE + k * NODE] = 1.0
        facing[k * NODE, SQUARE + k * NODE + last] = 1.0
    return np.concatenate([high, low, facing.astype(jnp.bfloat16)], axis=1)


def split(x):
    high = x.astype(BF16)
    return high, (x - high.astype(F32)).astype(BF16)


def dot(left, right):
    return jnp.dot(left, right, preferred_element_type=F32)


def product(x, weight):
    high, low = weight
    rows, depth = x.shape
    wide = high.shape[1]
    if rows < 64:
        rest = x - x.astype(BF16).astype(F32)
        both = jnp.concatenate([x, rest], axis=0).astype(BF16)
        if depth == 128:
            both = jnp.concatenate([both, both], axis=1)
            out = dot(both, jnp.concatenate([high, low], axis=0))
        else:
            out = dot(both, high) + dot(both, low)
        return out[:rows] + out[rows:]
    x_high, x_low = split(x)
    if wide == 128:
        weights = jnp.concatenate([high, low], axis=1)
        if depth == 128:
            weights = jnp.concatenate([weights, weights], axis=0)
            out = dot(jnp.concatenate([x_high, x_low], axis=1), weights)
            return out[:, :128] + out[:, 128:]
        out = dot(x_high, weights)
        return out[:, :128] + dot(x_low, high) + out[:, 128:]
    if depth == 128:
        out = dot(jnp.concatenate([x_high, x_high], axis=1), jnp.concatenate([high, low], axis=0))
        return out + dot(x_low, high)
    return dot(x_high, high) + dot(x_low, high) + dot(x_high, low)


def spread_product(x, weight):
    high, low = split(x)
    moved = pltpu.roll(x - high.astype(F32), 64, 1).astype(BF16)
    is_left = left_half(x.shape)
    zero = jnp.zeros_like(high)
    first = [jnp.where(is_left, high, moved), jnp.where(is_left, high, zero)]
    second = [jnp.where(is_left, moved, high), jnp.where(is_left, zero, high)]
    both = jnp.concatenate([jnp.concatenate(k, axis=1) for k in (first, second)], axis=0)
    return dot(both, jnp.concatenate([weight[0]] * 2 + [weight[1]] * 2, axis=0))


def lanes(shape):
    return lax.broadcasted_iota(jnp.int32, shape, len(shape) - 1)


def left_half(shape):
    return lanes(shape) < shape[-1] // 2


def narrow(x, table):
    rows = x.shape[0]
    rest = x - x.astype(BF16).astype(F32)
    out = dot(jnp.concatenate([x, rest], axis=0).astype(BF16), table)
    out = out[:rows] + out[rows:]
    return out[:, :128] + out[:, 128:]


def broad(x, table):
    rows = x.shape[0]
    rest = x - x.astype(BF16).astype(F32)
    both = jnp.concatenate([x, rest], axis=0).astype(BF16)
    out = dot(jnp.concatenate([both, both], axis=1), table)
    return out[:rows] + out[rows:]


def rows_to_lanes(x, count):
    size = x.shape[0] // count
    return jnp.concatenate([x[k * size : (k + 1) * size] for k in range(count)], axis=1)


def lanes_to_rows(x):
    return jnp.concatenate([x[:, k : k + 128] for k in range(0, x.shape[1], 128)], axis=0)


def quarters(x):
    return [x[:128, :128], x[:128, 128:], x[128:, :128], x[128:, 128:]]


def merge_pair(former, latter):
    wide = product(former, split(rows_to_lanes(latter, 2)))
    return jnp.concatenate(quarters(wide), axis=0)


def parent_pair(upper, lower):
    a, b, c, d = quarters(product(lanes_to_rows(upper), split(lower)))
    return jnp.concatenate([a, c, b, d], axis=1)


def wide_split(x):
    return jnp.concatenate(split(x), axis=1)


def tall_split(x):
    return jnp.concatenate(split(x), axis=0)


def kernel(stages, leaf_side, tracer_count, *refs):
    names = ["u", "velocity", "inflow", "tables", "leaf_solve", "leaf_skeleton", "leaf_lift"]
    names += [a + "_" + b for a in ("merge", "parent", "sibling") for b in ("first", "second", "rest")]
    names += ["root_map"]
    hbm = dict(zip(names, refs[: len(names)]))
    out_ref = refs[len(names)]
    rest = refs[len(names) + 1 :]
    v = dict(zip(names, rest[: len(names)]))
    (
        load_sem, field, near, coef, force, solved,
        up_leaf, up_low, up_high, up_cross, fold, down_high, down_low, down_leaf,
        send_x, send_y, halo_x, halo_y, halo_send, halo_recv, here,
    ) = rest[len(names) : len(names) + 21]
    stage_refs = rest[len(names) + 21 :]
    T, L = tracer_count, leaf_side
    leaves = L * L
    rows = T * leaves
    half = SQUARE // 2

    loads = {}
    for k, name in enumerate(names):
        loads[name] = pltpu.make_async_copy(hbm[name], v[name], load_sem.at[k])
    order = ["u", "tables", "velocity", "inflow", "leaf_skeleton", "merge_first", "merge_second"]
    order += ["merge_rest", "parent_rest", "sibling_rest", "root_map", "parent_second", "parent_first"]
    order += ["leaf_lift", "leaf_solve", "sibling_first", "sibling_second"]

    place = {"gx": lax.axis_index("gx"), "gy": lax.axis_index("gy")}
    count = {"gx": lax.axis_size("gx"), "gy": lax.axis_size("gy")}
    bit_of = lambda axis, bit: lax.rem(place[axis] // (1 << bit), 2)

    def partner(stage, mask):
        target = dict(place)
        for k, (axis, bit) in enumerate(stage):
            if mask >> (len(stage) - 1 - k) & 1:
                target[axis] = target[axis] + (1 - 2 * bit_of(axis, bit)) * (1 << bit)
        return (target["gx"], target["gy"])

    barrier = pltpu.get_barrier_semaphore()
    expected = jnp.int32(0)
    has, beside = {}, {}
    for axis in ("gx", "gy"):
        for way in (-1, 1):
            spot = dict(place)
            spot[axis] = spot[axis] + way
            beside[axis, way] = (spot["gx"], spot["gy"])
            has[axis, way] = place[axis] > 0 if way < 0 else place[axis] < count[axis] - 1

            @pl.when(has[axis, way])
            def _(axis=axis, way=way):
                pl.semaphore_signal(barrier, inc=1, device_id=beside[axis, way], device_id_type=MESH)

            expected = expected + jnp.where(has[axis, way], 1, 0)
    for stage in stages[:-1]:
        for mask in range(1, 1 << len(stage)):
            pl.semaphore_signal(barrier, inc=1, device_id=partner(stage, mask), device_id_type=MESH)
            expected = expected + 1

    by_rank = sorted(stages[-1], key=lambda e: (e == ("gx", 0), e[0] == "gy", -e[1]))
    slots = 1 << len(by_rank)
    rank = jnp.int32(0)
    for axis, bit in by_rank:
        rank = rank * 2 + bit_of(axis, bit)

    cleared = dict(place)
    for axis, bit in by_rank:
        cleared[axis] = cleared[axis] - bit_of(axis, bit) * (1 << bit)

    def ranked(number):
        target = dict(cleared)
        for k, (axis, bit) in enumerate(reversed(by_rank)):
            target[axis] = target[axis] + (number >> k & 1) * (1 << bit)
        return (target["gx"], target["gy"])

    def greet(number):
        @pl.when(rank < number)
        def _():
            pl.semaphore_signal(barrier, inc=1, device_id=ranked(number), device_id_type=MESH)

    def answer(number):
        @pl.when(rank > number)
        def _():
            pl.semaphore_signal(here, inc=1, device_id=ranked(number), device_id_type=MESH)

    expected = expected + rank
    for name in order[:8]:
        loads[name].start()
    for number in reversed(range(slots)):
        greet(number)

    def spot_of(i, j):
        return sum(
            ((i >> b & 1) << (5 - 2 * b)) + ((j >> b & 1) << (4 - 2 * b)) for b in range(3)
        )

    grid = sorted((spot_of(i, j), i, j) for i in range(L) for j in range(L))
    block = lambda i, j: slice(spot_of(i, j) * T, spot_of(i, j) * T + T)
    by_tracer = lambda i, j, h: pl.ds(h * rows + i * L + j, T, stride=leaves)

    loads["u"].wait()
    plain = v["u"][...].astype(F32).reshape(rows, SQUARE)
    for h in range(2):
        field[h * rows : (h + 1) * rows, :] = plain[:, h * half : (h + 1) * half]
    u = jnp.concatenate(
        [
            jnp.concatenate([field[by_tracer(i, j, h), :] for _, i, j in grid], axis=0)
            for h in range(2)
        ],
        axis=1,
    )
    force[...] = u
    loads["tables"].wait()
    near[...] = dot(u.astype(BF16), v["tables"][:, 4 * SQUARE :])
    line = lambda spots, c: jnp.concatenate(
        [near[block(i, j), c * half : (c + 1) * half] for i, j in spots], axis=0
    )
    side = lambda axis, k: [(k, m) if axis == "gx" else (m, k) for m in range(L)]
    send_x[1] = line(side("gx", L - 1), 0).astype(BF16)
    send_x[0] = line(side("gx", 0), 1).astype(BF16)
    for k in range(2):
        spots = side("gy", k * (L - 1))
        send_y[k] = (line(spots, 2) + pltpu.roll(line(spots, 3), 2, 1)).astype(BF16)
    def halo_copy(axis, way):
        k = 0 if way < 0 else 1
        source, target = (send_x, halo_x) if axis == "gx" else (send_y, halo_y)
        slot = k + (0 if axis == "gx" else 2)
        return pltpu.make_async_remote_copy(
            src_ref=source.at[k],
            dst_ref=target.at[k],
            send_sem=halo_send.at[slot],
            recv_sem=halo_recv.at[slot],
            device_id=beside[axis, way],
            device_id_type=MESH,
        )

    sides = [("gy", -1), ("gy", 1), ("gx", -1), ("gx", 1)]
    plan = [entry for stage in stages for entry in stage]
    bits = [bit_of(axis, bit) for axis, bit in plan]
    own_half = lambda k, w: jnp.where(bits[k] == 1, w[:, 128:], w[:, :128])
    twice = lambda w, axis: jnp.concatenate([w, w], axis=axis)
    merge = lambda k: v["merge_rest"][k]
    parent = lambda k: v["parent_rest"][k]

    own_parent = lambda k: own_half(k, parent(4 + k))

    def chained():
        chain = [own_parent(0)]
        for k in range(1, len(plan)):
            step = own_parent(k)
            if k > 1:
                step = product(step, split(own_parent(k - 1)))
            chain.append(product(step, split(chain[max(k - 2, 0)])))
        return chain

    def folded(levels, top, siblings, chain=()):
        weights = top
        for k in reversed(levels):
            groups = 1 << (levels[-1] - k)
            if weights is not None:
                weights = product(merge(4 + k), split(weights))
            elif siblings:
                weights = jnp.zeros((256, 128), F32)
            else:
                weights = merge(4 + k)
            blocks = [weights[:, g * 128 : (g + 1) * 128] for g in range(groups)]
            if siblings:
                sibling = own_half(k, v["sibling_rest"][4 + k])
                if k > 0:
                    sibling = product(sibling, split(chain[k - 1]))
                mine = jnp.int32(0)
                for later in levels:
                    if later > k:
                        mine = mine + bits[later] * (1 << (levels[-1] - later))
                blocks = [x + jnp.where(mine == g, sibling, 0.0) for g, x in enumerate(blocks)]
            weights = jnp.concatenate([x[:128] for x in blocks] + [x[128:] for x in blocks], axis=1)
        return lanes_to_rows(weights)

    first = len(plan) - len(stages[-1])
    last_levels = list(range(first, len(plan)))
    direct, folds = last_levels[: -FOLDED], last_levels[-FOLDED:]
    assert len(direct) == 2
    groups = 1 << len(folds)

    def prepare_up():
        for name in ("leaf_skeleton", "merge_first", "merge_second", "merge_rest"):
            loads[name].wait()
        two = [
            product(v["merge_first"][...].T, split(v["merge_second"][d * 64 : (d + 1) * 64, :]))
            for d in range(2)
        ]
        four = jnp.concatenate([two[d][c * 64 : (c + 1) * 64] for c in range(2) for d in range(2)], axis=1)
        up_leaf[...] = wide_split(lanes_to_rows(product(v["leaf_skeleton"][...].T, split(four))))
        up_low[...] = wide_split(merge_pair(merge(0), merge(1)))
        up_high[...] = wide_split(merge_pair(merge(2), merge(3)))
        up_cross[...] = wide_split(folded(direct, None, False))


    def prepare_down():
        for name in ("parent_rest", "sibling_rest", "root_map"):
            loads[name].wait()
        chain = chained()
        top = product(product(v["root_map"][...], split(own_parent(len(plan) - 1))), split(chain[-2]))
        fold[: groups * 128, :] = wide_split(folded(folds, top, True, chain))
        fold[groups * 128 :, :] = wide_split(folded(direct, None, True, chain))
        down_high[...] = tall_split(parent_pair(parent(3), parent(2)))
        down_low[...] = tall_split(parent_pair(parent(1), parent(0)))
        for name in ("parent_second", "parent_first", "leaf_lift"):
            loads[name].wait()
        halves = lambda x: jnp.concatenate([x, pltpu.roll(x, 64, 1)], axis=0)[:, :64]
        lifts = product(halves(v["parent_first"][...]), split(v["leaf_lift"][...]))
        lifts = jnp.concatenate([lifts[:64], lifts[64:]], axis=1)
        lifts = product(halves(v["parent_second"][...]), split(lifts))
        down_leaf[...] = tall_split(
            jnp.concatenate(
                [
                    lifts[d * 128 : (d + 1) * 128, c * SQUARE : (c + 1) * SQUARE]
                    for c in range(2)
                    for d in range(2)
                ],
                axis=1,
            )
        )

    own = lax.broadcasted_iota(jnp.int32, (leaves, L), 0) % L == lanes((leaves, L))

    def column(values):
        wide = jnp.concatenate(
            [jnp.broadcast_to(values[i : i + 1, :], (L, L)) for i in range(L)], axis=0
        )
        return jnp.sum(jnp.where(own, wide, 0.0), axis=1, keepdims=True)

    tile = (T, half)
    on_0, on_1 = lanes(tile) < NODE, lanes(tile) >= half - NODE
    on_2, on_3 = lanes(tile) % NODE == 0, lanes(tile) % NODE == NODE - 1
    at_leaf = lambda k, i, j: jnp.broadcast_to(coef[k, i * L + j : i * L + j + 1, :], tile)
    keep_if = lambda mask, x: jnp.where(mask, x, 0.0)
    strength = lambda s, i, j: at_leaf(2 + s, i, j)


    def interior():
        loads["velocity"].wait()
        loads["inflow"].wait()
        speed = [v["velocity"][k] for k in range(2)]
        columns = [column(x) for x in speed]
        columns += [
            column(v["inflow"][s].astype(F32) * (NODE * jnp.abs(speed[s // 2]))) for s in range(4)
        ]
        for k, x in enumerate(columns):
            coef[k] = jnp.broadcast_to(x, (leaves, half))

        for q in range(4):
            low, top = q * rows // 4, (q + 1) * rows // 4
            u = force[low:top, :]
            part = u.astype(BF16)
            grads = dot(part, v["tables"][:, : 2 * SQUARE])
            grads = grads + dot(part, v["tables"][:, 2 * SQUARE : 4 * SQUARE])
            for spot, i, j in grid[q * leaves // 4 : (q + 1) * leaves // 4]:
                at = slice(spot * T, spot * T + T)
                inside = slice(spot * T - low, spot * T + T - low)
                speeds = [at_leaf(k, i, j) for k in range(2)]
                w = [strength(s, i, j) for s in range(4)]
                w_2, w_3 = keep_if(on_2, w[2]), keep_if(on_3, w[3])
                for c in range(2):
                    cut = slice(c * half, (c + 1) * half)
                    far = slice((2 + c) * half, (3 + c) * half)
                    total = u[inside, cut] * (1.0 - (keep_if((on_0, on_1)[c], w[c]) + w_2 + w_3))
                    total = total - speeds[0] * grads[inside, cut] - speeds[1] * grads[inside, far]
                    ahead = i - 1 if c == 0 else i + 1
                    if 0 <= ahead < L:
                        total = total + w[c] * near[block(ahead, j), cut]
                    if j > 0:
                        total = total + w_2 * near[block(i, j - 1), far]
                    if j < L - 1:
                        total = total + w_3 * near[block(i, j + 1), far]
                    force[at, cut] = total


    for axis, way in sides:
        slot = 1 if way < 0 else 0

        @pl.when(jnp.logical_not(has[axis, way]))
        def _(axis=axis, slot=slot):
            target = halo_x if axis == "gx" else halo_y
            target[slot] = jnp.zeros_like(target[slot])

    def announce():
        pl.semaphore_wait(barrier, expected)
        for axis, way in sides:

            @pl.when(has[axis, way])
            def _(axis=axis, way=way):
                halo_copy(axis, way).start()

        for number in range(slots):
            answer(number)

    announce()
    for name in order[8:]:
        loads[name].start()
    prepare_up()
    interior()
    early = rank < slots // 16

    @pl.when(early)
    def _():
        prepare_down()


    for axis, way in sides:

        @pl.when(has[axis, way])
        def _(axis=axis, way=way):
            halo_copy(axis, -way).wait_recv()

    for axis, way in sides:
        slot = 1 if way < 0 else 0
        arrived = (halo_x if axis == "gx" else halo_y)[slot].astype(F32)
        shifted = pltpu.roll(arrived, 126, 1) if axis == "gy" else None
        for m, (i, j) in enumerate(side(axis, 0 if way < 0 else L - 1)):
            inside = slice(m * T, m * T + T)
            if axis == "gx":
                c = 0 if way < 0 else 1
                cut = slice(c * half, (c + 1) * half)
                force[block(i, j), cut] = force[block(i, j), cut] + strength(c, i, j) * arrived[inside]
            else:
                w = keep_if(on_2, strength(2, i, j)) if way < 0 else keep_if(on_3, strength(3, i, j))
                for c, x in enumerate((arrived, shifted)):
                    cut = slice(c * half, (c + 1) * half)
                    force[block(i, j), cut] = force[block(i, j), cut] + w * x[inside]

    high, low = split(rows_to_lanes(force[...], 4))
    wide = dot(high, up_leaf[...])
    current_16 = wide[:, :128] + wide[:, 128:] + dot(low, up_leaf[:, :128])
    current_4 = narrow(rows_to_lanes(current_16, 4), up_low[...])
    current = narrow(rows_to_lanes(current_4, 4), up_high[...])

    joined = lambda x: rows_to_lanes(x, 2)
    level = 4
    path = []
    for number, stage in enumerate(stages):
        pool, stage_send, stage_recv = stage_refs[3 * number : 3 * number + 3]
        own_slot = jnp.int32(0)
        for axis, bit in stage:
            own_slot = own_slot * 2 + bit_of(axis, bit)
        pool[own_slot] = current
        final = number == len(stages) - 1
        copies = [] if final else [
            pltpu.make_async_remote_copy(
                src_ref=pool.at[own_slot],
                dst_ref=pool.at[own_slot],
                send_sem=stage_send.at[mask],
                recv_sem=stage_recv.at[mask],
                device_id=partner(stage, mask),
                device_id_type=MESH,
            )
            for mask in range(1, 1 << len(stage))
        ]
        for copy in reversed(copies):
            copy.start()
        if final:

            @pl.when(rank < slots - 1)
            def _():
                pl.semaphore_wait(here, slots - 1 - rank)


            for other in range(slots):

                @pl.when(rank != other)
                def _(other=other):
                    pltpu.make_async_remote_copy(
                        src_ref=pool.at[own_slot],
                        dst_ref=pool.at[own_slot],
                        send_sem=stage_send.at[0],
                        recv_sem=stage_recv.at[0],
                        device_id=ranked(other),
                        device_id_type=MESH,
                    ).start()

            every = pltpu.make_async_remote_copy(
                src_ref=pool.at[pl.ds(0, slots - 1)],
                dst_ref=pool.at[pl.ds(0, slots - 1)],
                send_sem=stage_send.at[0],
                recv_sem=stage_recv.at[0],
                device_id=partner(stage, 1),
                device_id_type=MESH,
            )
        if number == 0:

            @pl.when(jnp.logical_not(early))
            def _():
                prepare_down()

            for name in ("leaf_solve", "sibling_first", "sibling_second"):
                loads[name].wait()
            forcing = force[...]
            sibling = lambda k: split(v["sibling_rest"][k])
            is_left = lambda x: left_half(x.shape)

            def gathered(x):
                middle = x.shape[0] // 2
                return jnp.where(is_left(x[:middle]), x[:middle], x[middle:])

            cat_0 = gathered(product(forcing, split(twice(v["leaf_skeleton"][...], 0).T)))
            cat_1 = gathered(product(cat_0, split(twice(v["merge_first"][...], 0).T)))
            cats = [joined(current_16)]
            cats.append(joined(product(cats[0], split(merge(0)))))
            cats.append(joined(current_4))
            cats.append(joined(product(cats[2], split(merge(2)))))
            own_part = product(cats[3], sibling(3))
            for k in (2, 1, 0):
                own_part = product(lanes_to_rows(own_part), split(parent(k)))
                own_part = own_part + product(cats[k], sibling(k))
            own_part = product(lanes_to_rows(own_part), split(v["parent_second"][...]))
            own_part = own_part + product(cat_1, split(v["sibling_second"][...]))
            own_part = spread_product(own_part, split(v["parent_first"][...]))
            own_part = own_part + product(cat_0, split(v["sibling_first"][...]))
            own_part = spread_product(own_part, split(v["leaf_lift"][...]))
            solved[...] = own_part + product(forcing, split(v["leaf_solve"][...]))
        if final:
            known = jnp.zeros((T, 128), F32)
            chain = chained() if path else ()
            for k, term in enumerate(path):
                term = own_half(k, term)
                known = known + (product(term, split(chain[k - 1])) if k > 0 else term)
        if final:
            for axis, way in sides:

                @pl.when(has[axis, way])
                def _(axis=axis, way=way):
                    halo_copy(axis, way).wait_send()

            every.wait_recv()
            break
        for copy in copies:
            copy.wait()
        current = pool[...].reshape(T << len(stage), 128)
        for k, (axis, bit) in enumerate(stage):
            cat = joined(current)
            mine = cat
            for later_axis, later_bit in stage[k + 1 :]:
                middle = mine.shape[0] // 2
                mine = jnp.where(bit_of(later_axis, later_bit) == 1, mine[middle:], mine[:middle])
            path.append(product(mine, split(v["sibling_rest"][level])))
            current = product(cat, split(merge(level)))
            level += 1

    everyone = pool[...].reshape(slots * T, 128)
    merged = narrow(rows_to_lanes(everyone, slots // groups), up_cross[...])
    mine = jnp.int32(0)
    for k in folds:
        mine = mine * 2 + bits[k]
    slabs = [rows_to_lanes(merged, groups)]
    slabs += [pool[k * groups + mine] for k in range(slots // groups)]
    boundary = narrow(jnp.concatenate(slabs, axis=1), fold[...]) + known
    boundary = lanes_to_rows(broad(boundary, down_high[...]))
    boundary = lanes_to_rows(broad(boundary, down_low[...]))
    high, low = split(boundary)
    lifted = dot(twice(high, 1), down_leaf[...]) + dot(low, down_leaf[:128, :])
    for spot, i, j in grid:
        q, inside = divmod(spot, leaves // 4)
        for h in range(2):
            at = q * SQUARE + h * half
            one = lifted[inside * T : (inside + 1) * T, at : at + half]
            one = one + solved[spot * T : spot * T + T, h * half : (h + 1) * half]
            field[by_tracer(i, j, h), :] = one
    updated = jnp.concatenate([field[:rows, :], field[rows:, :]], axis=1)
    out_ref[...] = updated.reshape(out_ref.shape).astype(out_ref.dtype)
    every.wait_send()


def local(tables, count_first, count_second, tracers, *operands):
    T, L = tracers.shape[0], tracers.shape[1]
    assert L == 8 and local_plan(L) == [1, 2] * 3
    stages = staged(cross_plan(count_first, count_second))
    rows = T * L * L
    args = [tracers, operands[0], operands[1], tables] + list(operands[2:])
    args[5], args[7] = args[5].T, args[7].T
    vmem, dma = pltpu.VMEM, pltpu.SemaphoreType.DMA
    scratch = [vmem(a.shape, a.dtype) for a in args]
    slots = 1 << len(stages[-1])
    groups = 1 << FOLDED
    scratch += [
        dma((len(args),)),
        vmem((2 * rows, 128), F32),
        vmem((rows, 2 * SQUARE), F32),
        vmem((6, L * L, 128), F32),
        vmem((rows, SQUARE), F32),
        vmem((rows, SQUARE), F32),
        vmem((4 * SQUARE, 256), BF16),
        vmem((512, 256), BF16),
        vmem((512, 256), BF16),
        vmem((slots // groups * 128, 256), BF16),
        vmem(((groups + slots // groups) * 128, 256), BF16),
        vmem((256, 512), BF16),
        vmem((256, 512), BF16),
        vmem((256, 4 * SQUARE), BF16),
        vmem((2, T * L, 128), BF16),
        vmem((2, T * L, 128), BF16),
        vmem((2, T * L, 128), BF16),
        vmem((2, T * L, 128), BF16),
        dma((4,)),
        dma((4,)),
        pltpu.SemaphoreType.REGULAR,
    ]
    for stage in stages:
        slots = 1 << len(stage)
        scratch += [vmem((slots, T, 128), F32), dma((slots,)), dma((slots,))]
    return pl.pallas_call(
        functools.partial(kernel, stages, L, T),
        out_shape=jax.ShapeDtypeStruct(tracers.shape, tracers.dtype),
        in_specs=[pl.BlockSpec(memory_space=pl.ANY)] * len(args),
        out_specs=pl.BlockSpec(memory_space=pltpu.VMEM),
        scratch_shapes=scratch,
        compiler_params=pltpu.CompilerParams(
            collective_id=0, has_side_effects=True, vmem_limit_bytes=VMEM_LIMIT
        ),
    )(*[pltpu.with_memory_space_constraint(a, pltpu.HBM) for a in args])


def solution(mesh):
    tables = point_tables()
    split_both = P(None, "gx", "gy")
    in_specs = (P(None, "gx", "gy", None), split_both, split_both) + (P(),) * 13

    def body(*args):
        return local(
            jnp.asarray(tables), mesh.shape["gx"], mesh.shape["gy"], *args
        )

    return jax.shard_map(
        body,
        mesh=mesh,
        in_specs=in_specs,
        out_specs=P(None, "gx", "gy", None),
        check_vma=False,
    )
```

```python
import functools

import jax
import jax.numpy as jnp
import numpy as np
from jax import lax
from jax.experimental import pallas as pl
from jax.experimental.pallas import tpu as pltpu
from jax.sharding import PartitionSpec as P

NODE = 16
SQUARE = NODE * NODE
F32 = jnp.float32
BF16 = jnp.bfloat16
VMEM_LIMIT = 32 * 1024 * 1024
MESH = pl.DeviceIdType.MESH
LAST_STAGE = 5
FOLDED = 3


def local_plan(leaf_side):
    merge_plan = []
    block_span = leaf_side
    while block_span > 1:
        merge_plan = merge_plan + [1, 2]
        block_span = block_span // 2
    return merge_plan


def cross_plan(count_first, count_second):
    merge_plan = []
    bits = {"gx": 0, "gy": 0}
    while count_first * count_second > 1:
        if count_first >= count_second:
            axis, count_first = "gx", count_first // 2
        else:
            axis, count_second = "gy", count_second // 2
        merge_plan.append((axis, bits[axis]))
        bits[axis] += 1
    return merge_plan


def staged(plan):
    stages, rest = [], list(plan)
    while len(rest) > LAST_STAGE:
        size = min(3, len(rest) - LAST_STAGE)
        stages.append(rest[:size])
        rest = rest[size:]
    return stages + [rest]


def point_tables():
    index = np.arange(NODE)
    points = -np.cos(np.pi * index / (NODE - 1))
    weights = np.where(index % 2 == 0, 1.0, -1.0)
    weights[[0, NODE - 1]] *= 2.0
    eye = np.eye(NODE)
    matrix = weights[:, None] / weights[None, :] / (points[:, None] - points[None, :] + eye)
    matrix = matrix * (1.0 - eye)
    matrix = matrix - np.diag(matrix.sum(axis=1))
    both = np.concatenate([np.kron(matrix, eye).T, np.kron(eye, matrix).T], axis=1)
    both = both.astype(np.float32)
    high = both.astype(jnp.bfloat16)
    low = (both - high.astype(np.float32)).astype(jnp.bfloat16)
    facing = np.zeros((SQUARE, 2 * SQUARE), np.float32)
    last = NODE - 1
    for k in range(NODE):
        facing[last * NODE + k, k] = 1.0
        facing[k, last * NODE + k] = 1.0
        facing[k * NODE + last, SQUARE + k * NODE] = 1.0
        facing[k * NODE, SQUARE + k * NODE + last] = 1.0
    packed = np.zeros((SQUARE, SQUARE // 2), np.float32)
    for q in range(4):
        for k in range(NODE):
            packed[(0 if q // 2 else last) * NODE + k, q * 2 * NODE + k] = 1.0
            packed[k * NODE + (0 if q % 2 else last), (q * 2 + 1) * NODE + k] = 1.0
    return np.concatenate([high, low, *(x.astype(jnp.bfloat16) for x in (facing, packed))], axis=1)


def split(x):
    high = x.astype(BF16)
    return high, (x - high.astype(F32)).astype(BF16)


def dot(left, right):
    return jnp.dot(left, right, preferred_element_type=F32)


def product(x, weight):
    high, low = weight
    rows, depth = x.shape
    wide = high.shape[1]
    if rows < 64:
        rest = x - x.astype(BF16).astype(F32)
        both = jnp.concatenate([x, rest], axis=0).astype(BF16)
        if depth == 128:
            both = jnp.concatenate([both, both], axis=1)
            out = dot(both, jnp.concatenate([high, low], axis=0))
        else:
            out = dot(both, high) + dot(both, low)
        return out[:rows] + out[rows:]
    x_high, x_low = split(x)
    if wide == 128:
        weights = jnp.concatenate([high, low], axis=1)
        if depth == 128:
            weights = jnp.concatenate([weights, weights], axis=0)
            out = dot(jnp.concatenate([x_high, x_low], axis=1), weights)
            return out[:, :128] + out[:, 128:]
        out = dot(x_high, weights)
        return out[:, :128] + dot(x_low, high) + out[:, 128:]
    if depth == 128:
        out = dot(jnp.concatenate([x_high, x_high], axis=1), jnp.concatenate([high, low], axis=0))
        return out + dot(x_low, high)
    return dot(x_high, high) + dot(x_low, high) + dot(x_high, low)


def spread_product(x, weight):
    high, low = split(x)
    moved = pltpu.roll(x - high.astype(F32), 64, 1).astype(BF16)
    is_left = left_half(x.shape)
    zero = jnp.zeros_like(high)
    first = [jnp.where(is_left, high, moved), jnp.where(is_left, high, zero)]
    second = [jnp.where(is_left, moved, high), jnp.where(is_left, zero, high)]
    both = jnp.concatenate([jnp.concatenate(k, axis=1) for k in (first, second)], axis=0)
    return dot(both, jnp.concatenate([weight[0]] * 2 + [weight[1]] * 2, axis=0))


def lanes(shape):
    return lax.broadcasted_iota(jnp.int32, shape, len(shape) - 1)


def left_half(shape):
    return lanes(shape) < shape[-1] // 2


def narrow(x, table):
    rows = x.shape[0]
    rest = x - x.astype(BF16).astype(F32)
    out = dot(jnp.concatenate([x, rest], axis=0).astype(BF16), table)
    out = out[:rows] + out[rows:]
    return out[:, :128] + out[:, 128:]


def broad(x, table):
    rows = x.shape[0]
    rest = x - x.astype(BF16).astype(F32)
    both = jnp.concatenate([x, rest], axis=0).astype(BF16)
    out = dot(jnp.concatenate([both, both], axis=1), table)
    return out[:rows] + out[rows:]


def rows_to_lanes(x, count):
    size = x.shape[0] // count
    return jnp.concatenate([x[k * size : (k + 1) * size] for k in range(count)], axis=1)


def lanes_to_rows(x):
    return jnp.concatenate([x[:, k : k + 128] for k in range(0, x.shape[1], 128)], axis=0)


def quarters(x):
    return [x[:128, :128], x[:128, 128:], x[128:, :128], x[128:, 128:]]


def merge_pair(former, latter):
    wide = product(former, split(rows_to_lanes(latter, 2)))
    return jnp.concatenate(quarters(wide), axis=0)


def parent_pair(upper, lower):
    a, b, c, d = quarters(product(lanes_to_rows(upper), split(lower)))
    return jnp.concatenate([a, c, b, d], axis=1)


def wide_split(x):
    return jnp.concatenate(split(x), axis=1)


def tall_split(x):
    return jnp.concatenate(split(x), axis=0)


def kernel(stages, leaf_side, tracer_count, *refs):
    names = ["u", "velocity", "inflow", "tables", "leaf_solve", "leaf_skeleton", "leaf_lift"]
    names += [a + "_" + b for a in ("merge", "parent", "sibling") for b in ("first", "second", "rest")]
    names += ["root_map"]
    hbm = dict(zip(names, refs[: len(names)]))
    out_ref = refs[len(names)]
    rest = refs[len(names) + 1 :]
    v = dict(zip(names, rest[: len(names)]))
    (
        load_sem, field, near, coef, force, solved,
        up_leaf, up_low, up_high, up_cross, fold, down_high, down_low, down_leaf,
        send_x, send_y, halo_x, halo_y, halo_send, halo_recv, here, up_edge, inner_16,
    ) = rest[len(names) : len(names) + 23]
    stage_refs = rest[len(names) + 23 :]
    T, L = tracer_count, leaf_side
    leaves = L * L
    rows = T * leaves
    half = SQUARE // 2

    loads = {}
    for k, name in enumerate(names):
        loads[name] = pltpu.make_async_copy(hbm[name], v[name], load_sem.at[k])
    order = ["u", "tables", "velocity", "inflow", "leaf_skeleton", "merge_first", "merge_second"]
    order += ["merge_rest", "parent_rest", "sibling_rest", "root_map", "parent_second", "parent_first"]
    order += ["leaf_lift", "leaf_solve", "sibling_first", "sibling_second"]

    place = {"gx": lax.axis_index("gx"), "gy": lax.axis_index("gy")}
    count = {"gx": lax.axis_size("gx"), "gy": lax.axis_size("gy")}
    bit_of = lambda axis, bit: lax.rem(place[axis] // (1 << bit), 2)

    def partner(stage, mask):
        target = dict(place)
        for k, (axis, bit) in enumerate(stage):
            if mask >> (len(stage) - 1 - k) & 1:
                target[axis] = target[axis] + (1 - 2 * bit_of(axis, bit)) * (1 << bit)
        return (target["gx"], target["gy"])

    barrier = pltpu.get_barrier_semaphore()
    expected = jnp.int32(0)
    has, beside = {}, {}
    for axis in ("gx", "gy"):
        for way in (-1, 1):
            spot = dict(place)
            spot[axis] = spot[axis] + way
            beside[axis, way] = (spot["gx"], spot["gy"])
            has[axis, way] = place[axis] > 0 if way < 0 else place[axis] < count[axis] - 1

            @pl.when(has[axis, way])
            def _(axis=axis, way=way):
                pl.semaphore_signal(barrier, inc=1, device_id=beside[axis, way], device_id_type=MESH)

            expected = expected + jnp.where(has[axis, way], 1, 0)
    for stage in stages[:-1]:
        for mask in range(1, 1 << len(stage)):
            pl.semaphore_signal(barrier, inc=1, device_id=partner(stage, mask), device_id_type=MESH)
            expected = expected + 1

    by_rank = sorted(stages[-1], key=lambda e: (e == ("gx", 0), e[0] == "gy", -e[1]))
    slots = 1 << len(by_rank)
    rank = jnp.int32(0)
    for axis, bit in by_rank:
        rank = rank * 2 + bit_of(axis, bit)

    cleared = dict(place)
    for axis, bit in by_rank:
        cleared[axis] = cleared[axis] - bit_of(axis, bit) * (1 << bit)

    def ranked(number):
        target = dict(cleared)
        for k, (axis, bit) in enumerate(reversed(by_rank)):
            target[axis] = target[axis] + (number >> k & 1) * (1 << bit)
        return (target["gx"], target["gy"])

    def greet(number):
        @pl.when(rank < number)
        def _():
            pl.semaphore_signal(barrier, inc=1, device_id=ranked(number), device_id_type=MESH)

    def answer(number):
        @pl.when(rank > number)
        def _():
            pl.semaphore_signal(here, inc=1, device_id=ranked(number), device_id_type=MESH)

    expected = expected + rank
    for name in order[:8]:
        loads[name].start()
    for number in reversed(range(slots)):
        greet(number)

    def spot_of(i, j):
        return sum(
            ((i >> b & 1) << (5 - 2 * b)) + ((j >> b & 1) << (4 - 2 * b)) for b in range(3)
        )

    grid = sorted((spot_of(i, j), i, j) for i in range(L) for j in range(L))
    block = lambda i, j: slice(spot_of(i, j) * T, spot_of(i, j) * T + T)
    by_tracer = lambda i, j, h: pl.ds(h * rows + i * L + j, T, stride=leaves)

    loads["u"].wait()
    plain = v["u"][...].astype(F32).reshape(rows, SQUARE)
    for h in range(2):
        field[h * rows : (h + 1) * rows, :] = plain[:, h * half : (h + 1) * half]
    u = jnp.concatenate(
        [
            jnp.concatenate([field[by_tracer(i, j, h), :] for _, i, j in grid], axis=0)
            for h in range(2)
        ],
        axis=1,
    )
    force[...] = u
    loads["tables"].wait()
    near[...] = dot(u.astype(BF16), v["tables"][:, 4 * SQUARE :])
    line = lambda spots, c: jnp.concatenate(
        [near[block(i, j), c * half : (c + 1) * half] for i, j in spots], axis=0
    )
    side = lambda axis, k: [(k, m) if axis == "gx" else (m, k) for m in range(L)]
    for k in range(2):
        for axis, target in (("gx", send_x), ("gy", send_y)):
            target[k] = line(side(axis, k * (L - 1)), 4).astype(BF16)

    def halo_copy(axis, way):
        k = 0 if way < 0 else 1
        source, target = (send_x, halo_x) if axis == "gx" else (send_y, halo_y)
        slot = k + (0 if axis == "gx" else 2)
        return pltpu.make_async_remote_copy(
            src_ref=source.at[k],
            dst_ref=target.at[k],
            send_sem=halo_send.at[slot],
            recv_sem=halo_recv.at[slot],
            device_id=beside[axis, way],
            device_id_type=MESH,
        )

    sides = [("gy", -1), ("gy", 1), ("gx", -1), ("gx", 1)]
    plan = [entry for stage in stages for entry in stage]
    bits = [bit_of(axis, bit) for axis, bit in plan]
    own_half = lambda k, w: jnp.where(bits[k] == 1, w[:, 128:], w[:, :128])
    twice = lambda w, axis: jnp.concatenate([w, w], axis=axis)
    merge = lambda k: v["merge_rest"][k]
    parent = lambda k: v["parent_rest"][k]

    own_parent = lambda k: own_half(k, parent(4 + k))

    def chained():
        chain = [own_parent(0)]
        for k in range(1, len(plan)):
            step = own_parent(k)
            if k > 1:
                step = product(step, split(own_parent(k - 1)))
            chain.append(product(step, split(chain[max(k - 2, 0)])))
        return chain

    def folded(levels, top, siblings, chain=()):
        weights = top
        for k in reversed(levels):
            groups = 1 << (levels[-1] - k)
            if weights is not None:
                weights = product(merge(4 + k), split(weights))
            elif siblings:
                weights = jnp.zeros((256, 128), F32)
            else:
                weights = merge(4 + k)
            blocks = [weights[:, g * 128 : (g + 1) * 128] for g in range(groups)]
            if siblings:
                sibling = own_half(k, v["sibling_rest"][4 + k])
                if k > 0:
                    sibling = product(sibling, split(chain[k - 1]))
                mine = jnp.int32(0)
                for later in levels:
                    if later > k:
                        mine = mine + bits[later] * (1 << (levels[-1] - later))
                blocks = [x + jnp.where(mine == g, sibling, 0.0) for g, x in enumerate(blocks)]
            weights = jnp.concatenate([x[:128] for x in blocks] + [x[128:] for x in blocks], axis=1)
        return lanes_to_rows(weights)

    first = len(plan) - len(stages[-1])
    last_levels = list(range(first, len(plan)))
    direct, folds = last_levels[: -FOLDED], last_levels[-FOLDED:]
    assert len(direct) == 2
    groups = 1 << len(folds)

    def edge_points(q):
        shape = (2 * NODE, SQUARE)
        k = lax.broadcasted_iota(jnp.int32, shape, 0)
        first = k + (SQUARE - NODE if q // 2 else 0)
        second = (k - NODE) * NODE + (NODE - 1 if q % 2 else 0)
        return jnp.where(lanes(shape) == jnp.where(k < NODE, first, second), 1.0, 0.0).astype(BF16)

    def prepare_up():
        for name in ("leaf_skeleton", "merge_first", "merge_second", "merge_rest"):
            loads[name].wait()
        two = [
            product(v["merge_first"][...].T, split(v["merge_second"][d * 64 : (d + 1) * 64, :]))
            for d in range(2)
        ]
        four = jnp.concatenate([two[d][c * 64 : (c + 1) * 64] for c in range(2) for d in range(2)], axis=1)
        up_leaf[...] = wide_split(lanes_to_rows(product(v["leaf_skeleton"][...].T, split(four))))
        at_edges = [
            dot(edge_points(q), up_leaf[q * SQUARE : (q + 1) * SQUARE, :]) for q in range(4)
        ]
        up_edge[...] = jnp.concatenate(at_edges * 2, axis=0).astype(BF16)
        up_low[...] = wide_split(merge_pair(merge(0), merge(1)))
        up_high[...] = wide_split(merge_pair(merge(2), merge(3)))
        up_cross[...] = wide_split(folded(direct, None, False))


    def prepare_down():
        for name in ("parent_rest", "sibling_rest", "root_map"):
            loads[name].wait()
        chain = chained()
        top = product(product(v["root_map"][...], split(own_parent(len(plan) - 1))), split(chain[-2]))
        fold[: groups * 128, :] = wide_split(folded(folds, top, True, chain))
        fold[groups * 128 :, :] = wide_split(folded(direct, None, True, chain))
        down_high[...] = tall_split(parent_pair(parent(3), parent(2)))
        down_low[...] = tall_split(parent_pair(parent(1), parent(0)))
        for name in ("parent_second", "parent_first", "leaf_lift"):
            loads[name].wait()
        halves = lambda x: jnp.concatenate([x, pltpu.roll(x, 64, 1)], axis=0)[:, :64]
        lifts = product(halves(v["parent_first"][...]), split(v["leaf_lift"][...]))
        lifts = jnp.concatenate([lifts[:64], lifts[64:]], axis=1)
        lifts = product(halves(v["parent_second"][...]), split(lifts))
        down_leaf[...] = tall_split(
            jnp.concatenate(
                [
                    lifts[d * 128 : (d + 1) * 128, c * SQUARE : (c + 1) * SQUARE]
                    for c in range(2)
                    for d in range(2)
                ],
                axis=1,
            )
        )

    own = lax.broadcasted_iota(jnp.int32, (leaves, L), 0) % L == lanes((leaves, L))

    def column(values):
        wide = jnp.concatenate(
            [jnp.broadcast_to(values[i : i + 1, :], (L, L)) for i in range(L)], axis=0
        )
        return jnp.sum(jnp.where(own, wide, 0.0), axis=1, keepdims=True)

    tile = (T, half)
    on_0, on_1 = lanes(tile) < NODE, lanes(tile) >= half - NODE
    on_2, on_3 = lanes(tile) % NODE == 0, lanes(tile) % NODE == NODE - 1
    at_leaf = lambda k, i, j: jnp.broadcast_to(coef[k, i * L + j : i * L + j + 1, :], tile)
    keep_if = lambda mask, x: jnp.where(mask, x, 0.0)
    strength = lambda s, i, j: at_leaf(2 + s, i, j)


    def interior():
        loads["velocity"].wait()
        loads["inflow"].wait()
        speed = [v["velocity"][k] for k in range(2)]
        columns = [column(x) for x in speed]
        columns += [
            column(v["inflow"][s].astype(F32) * (NODE * jnp.abs(speed[s // 2]))) for s in range(4)
        ]
        for k, x in enumerate(columns):
            coef[k] = jnp.broadcast_to(x, (leaves, half))

        for q in range(4):
            low, top = q * rows // 4, (q + 1) * rows // 4
            u = force[low:top, :]
            part = u.astype(BF16)
            grads = dot(part, v["tables"][:, : 2 * SQUARE])
            grads = grads + dot(part, v["tables"][:, 2 * SQUARE : 4 * SQUARE])
            for spot, i, j in grid[q * leaves // 4 : (q + 1) * leaves // 4]:
                at = slice(spot * T, spot * T + T)
                inside = slice(spot * T - low, spot * T + T - low)
                speeds = [at_leaf(k, i, j) for k in range(2)]
                w = [strength(s, i, j) for s in range(4)]
                w_2, w_3 = keep_if(on_2, w[2]), keep_if(on_3, w[3])
                for c in range(2):
                    cut = slice(c * half, (c + 1) * half)
                    far = slice((2 + c) * half, (3 + c) * half)
                    total = u[inside, cut] * (1.0 - (keep_if((on_0, on_1)[c], w[c]) + w_2 + w_3))
                    total = total - speeds[0] * grads[inside, cut] - speeds[1] * grads[inside, far]
                    ahead = i - 1 if c == 0 else i + 1
                    if 0 <= ahead < L:
                        total = total + w[c] * near[block(ahead, j), cut]
                    if j > 0:
                        total = total + w_2 * near[block(i, j - 1), far]
                    if j < L - 1:
                        total = total + w_3 * near[block(i, j + 1), far]
                    force[at, cut] = total


    for axis, way in sides:
        slot = 1 if way < 0 else 0

        @pl.when(jnp.logical_not(has[axis, way]))
        def _(axis=axis, slot=slot):
            target = halo_x if axis == "gx" else halo_y
            target[slot] = jnp.zeros_like(target[slot])

    def announce():
        pl.semaphore_wait(barrier, expected)
        for axis, way in sides:

            @pl.when(has[axis, way])
            def _(axis=axis, way=way):
                halo_copy(axis, way).start()

        for number in range(slots):
            answer(number)

    announce()
    for name in order[8:]:
        loads[name].start()
    prepare_up()
    interior()
    high, low = split(rows_to_lanes(force[...], 4))
    wide = dot(high, up_leaf[...])
    inner_16[...] = wide[:, :128] + wide[:, 128:] + dot(low, up_leaf[:, :128])
    early = rank < slots // 16

    @pl.when(early)
    def _():
        prepare_down()


    for axis, way in sides:

        @pl.when(has[axis, way])
        def _(axis=axis, way=way):
            halo_copy(axis, -way).wait_recv()

    edges = [None] * (leaves // 4)
    for axis, way in sides:
        slot = 1 if way < 0 else 0
        arrived = (halo_x if axis == "gx" else halo_y)[slot].astype(F32)
        across = 0 if axis == "gx" else 1
        for m, (i, j) in enumerate(side(axis, 0 if way < 0 else L - 1)):
            q, box = divmod(spot_of(i, j), leaves // 4)
            mine = lanes(tile) // NODE == 2 * q + across
            term = keep_if(mine, strength(2 * across + 1 - slot, i, j)) * arrived[m * T : m * T + T]
            edges[box] = term if edges[box] is None else edges[box] + term
    edges = jnp.concatenate([jnp.zeros(tile, F32) if x is None else x for x in edges], axis=0)
    edges = jnp.concatenate(split(edges), axis=1)
    wide = dot(edges, up_edge[...])
    current_16 = inner_16[...] + wide[:, :128] + wide[:, 128:]
    current_4 = narrow(rows_to_lanes(current_16, 4), up_low[...])
    current = narrow(rows_to_lanes(current_4, 4), up_high[...])

    joined = lambda x: rows_to_lanes(x, 2)
    level = 4
    path = []
    for number, stage in enumerate(stages):
        pool, stage_send, stage_recv = stage_refs[3 * number : 3 * number + 3]
        own_slot = jnp.int32(0)
        for axis, bit in stage:
            own_slot = own_slot * 2 + bit_of(axis, bit)
        pool[own_slot] = current
        final = number == len(stages) - 1
        copies = [] if final else [
            pltpu.make_async_remote_copy(
                src_ref=pool.at[own_slot],
                dst_ref=pool.at[own_slot],
                send_sem=stage_send.at[mask],
                recv_sem=stage_recv.at[mask],
                device_id=partner(stage, mask),
                device_id_type=MESH,
            )
            for mask in range(1, 1 << len(stage))
        ]
        for copy in reversed(copies):
            copy.start()
        if final:

            @pl.when(rank < slots - 1)
            def _():
                pl.semaphore_wait(here, slots - 1 - rank)


            for other in range(slots):

                @pl.when(rank != other)
                def _(other=other):
                    pltpu.make_async_remote_copy(
                        src_ref=pool.at[own_slot],
                        dst_ref=pool.at[own_slot],
                        send_sem=stage_send.at[0],
                        recv_sem=stage_recv.at[0],
                        device_id=ranked(other),
                        device_id_type=MESH,
                    ).start()

            every = pltpu.make_async_remote_copy(
                src_ref=pool.at[pl.ds(0, slots - 1)],
                dst_ref=pool.at[pl.ds(0, slots - 1)],
                send_sem=stage_send.at[0],
                recv_sem=stage_recv.at[0],
                device_id=partner(stage, 1),
                device_id_type=MESH,
            )
        if number == 0:

            @pl.when(jnp.logical_not(early))
            def _():
                prepare_down()

            for name in ("leaf_solve", "sibling_first", "sibling_second"):
                loads[name].wait()
            turned = [jnp.concatenate([edge_points(q)] * 2, axis=0) for q in range(4)]
            of_quarter = lambda q: jnp.concatenate(
                [edges[:, k + q * 32 : k + q * 32 + 32] for k in (0, 128)], axis=1
            )
            forcing = jnp.concatenate(
                [
                    force[q * 128 : (q + 1) * 128, :] + dot(of_quarter(q), turned[q])
                    for q in range(4)
                ],
                axis=0,
            )
            sibling = lambda k: split(v["sibling_rest"][k])
            is_left = lambda x: left_half(x.shape)

            def gathered(x):
                middle = x.shape[0] // 2
                return jnp.where(is_left(x[:middle]), x[:middle], x[middle:])

            cat_0 = gathered(product(forcing, split(twice(v["leaf_skeleton"][...], 0).T)))
            cat_1 = gathered(product(cat_0, split(twice(v["merge_first"][...], 0).T)))
            cats = [joined(current_16)]
            cats.append(joined(product(cats[0], split(merge(0)))))
            cats.append(joined(current_4))
            cats.append(joined(product(cats[2], split(merge(2)))))
            own_part = product(cats[3], sibling(3))
            for k in (2, 1, 0):
                own_part = product(lanes_to_rows(own_part), split(parent(k)))
                own_part = own_part + product(cats[k], sibling(k))
            own_part = product(lanes_to_rows(own_part), split(v["parent_second"][...]))
            own_part = own_part + product(cat_1, split(v["sibling_second"][...]))
            own_part = spread_product(own_part, split(v["parent_first"][...]))
            own_part = own_part + product(cat_0, split(v["sibling_first"][...]))
            own_part = spread_product(own_part, split(v["leaf_lift"][...]))
            solved[...] = own_part + product(forcing, split(v["leaf_solve"][...]))
        if final:
            known = jnp.zeros((T, 128), F32)
            chain = chained() if path else ()
            for k, term in enumerate(path):
                term = own_half(k, term)
                known = known + (product(term, split(chain[k - 1])) if k > 0 else term)
        if final:
            for axis, way in sides:

                @pl.when(has[axis, way])
                def _(axis=axis, way=way):
                    halo_copy(axis, way).wait_send()

            every.wait_recv()
            break
        for copy in copies:
            copy.wait()
        current = pool[...].reshape(T << len(stage), 128)
        for k, (axis, bit) in enumerate(stage):
            cat = joined(current)
            mine = cat
            for later_axis, later_bit in stage[k + 1 :]:
                middle = mine.shape[0] // 2
                mine = jnp.where(bit_of(later_axis, later_bit) == 1, mine[middle:], mine[:middle])
            path.append(product(mine, split(v["sibling_rest"][level])))
            current = product(cat, split(merge(level)))
            level += 1

    everyone = pool[...].reshape(slots * T, 128)
    merged = narrow(rows_to_lanes(everyone, slots // groups), up_cross[...])
    mine = jnp.int32(0)
    for k in folds:
        mine = mine * 2 + bits[k]
    slabs = [rows_to_lanes(merged, groups)]
    slabs += [pool[k * groups + mine] for k in range(slots // groups)]
    boundary = narrow(jnp.concatenate(slabs, axis=1), fold[...]) + known
    boundary = lanes_to_rows(broad(boundary, down_high[...]))
    boundary = lanes_to_rows(broad(boundary, down_low[...]))
    high, low = split(boundary)
    lifted = dot(twice(high, 1), down_leaf[...]) + dot(low, down_leaf[:128, :])
    for spot, i, j in grid:
        q, inside = divmod(spot, leaves // 4)
        for h in range(2):
            at = q * SQUARE + h * half
            one = lifted[inside * T : (inside + 1) * T, at : at + half]
            one = one + solved[spot * T : spot * T + T, h * half : (h + 1) * half]
            field[by_tracer(i, j, h), :] = one
    updated = jnp.concatenate([field[:rows, :], field[rows:, :]], axis=1)
    out_ref[...] = updated.reshape(out_ref.shape).astype(out_ref.dtype)
    every.wait_send()


def local(tables, count_first, count_second, tracers, *operands):
    T, L = tracers.shape[0], tracers.shape[1]
    assert L == 8 and local_plan(L) == [1, 2] * 3
    stages = staged(cross_plan(count_first, count_second))
    rows = T * L * L
    args = [tracers, operands[0], operands[1], tables] + list(operands[2:])
    args[5], args[7] = args[5].T, args[7].T
    vmem, dma = pltpu.VMEM, pltpu.SemaphoreType.DMA
    scratch = [vmem(a.shape, a.dtype) for a in args]
    slots = 1 << len(stages[-1])
    groups = 1 << FOLDED
    scratch += [
        dma((len(args),)),
        vmem((2 * rows, 128), F32),
        vmem((rows, 2 * SQUARE + SQUARE // 2), F32),
        vmem((6, L * L, 128), F32),
        vmem((rows, SQUARE), F32),
        vmem((rows, SQUARE), F32),
        vmem((4 * SQUARE, 256), BF16),
        vmem((512, 256), BF16),
        vmem((512, 256), BF16),
        vmem((slots // groups * 128, 256), BF16),
        vmem(((groups + slots // groups) * 128, 256), BF16),
        vmem((256, 512), BF16),
        vmem((256, 512), BF16),
        vmem((256, 4 * SQUARE), BF16),
        vmem((2, T * L, 128), BF16),
        vmem((2, T * L, 128), BF16),
        vmem((2, T * L, 128), BF16),
        vmem((2, T * L, 128), BF16),
        dma((4,)),
        dma((4,)),
        pltpu.SemaphoreType.REGULAR,
        vmem((256, 256), BF16),
        vmem((T * L * L // 4, 128), F32),
    ]
    for stage in stages:
        slots = 1 << len(stage)
        scratch += [vmem((slots, T, 128), F32), dma((slots,)), dma((slots,))]
    return pl.pallas_call(
        functools.partial(kernel, stages, L, T),
        out_shape=jax.ShapeDtypeStruct(tracers.shape, tracers.dtype),
        in_specs=[pl.BlockSpec(memory_space=pl.ANY)] * len(args),
        out_specs=pl.BlockSpec(memory_space=pltpu.VMEM),
        scratch_shapes=scratch,
        compiler_params=pltpu.CompilerParams(
            collective_id=0, has_side_effects=True, vmem_limit_bytes=VMEM_LIMIT
        ),
    )(*[pltpu.with_memory_space_constraint(a, pltpu.HBM) for a in args])


def solution(mesh):
    tables = point_tables()
    split_both = P(None, "gx", "gy")
    in_specs = (P(None, "gx", "gy", None), split_both, split_both) + (P(),) * 13

    def body(*args):
        return local(
            jnp.asarray(tables), mesh.shape["gx"], mesh.shape["gy"], *args
        )

    return jax.shard_map(
        body,
        mesh=mesh,
        in_specs=in_specs,
        out_specs=P(None, "gx", "gy", None),
        check_vma=False,
    )
```

```python
import functools

import jax
import jax.numpy as jnp
import numpy as np
from jax import lax
from jax.experimental import pallas as pl
from jax.experimental.pallas import tpu as pltpu
from jax.sharding import PartitionSpec as P

NODE = 16
SQUARE = NODE * NODE
F32 = jnp.float32
BF16 = jnp.bfloat16
VMEM_LIMIT = 32 * 1024 * 1024
MESH = pl.DeviceIdType.MESH
LAST_STAGE = 5
FOLDED = 3


def local_plan(leaf_side):
    merge_plan = []
    block_span = leaf_side
    while block_span > 1:
        merge_plan = merge_plan + [1, 2]
        block_span = block_span // 2
    return merge_plan


def cross_plan(count_first, count_second):
    merge_plan = []
    bits = {"gx": 0, "gy": 0}
    while count_first * count_second > 1:
        if count_first >= count_second:
            axis, count_first = "gx", count_first // 2
        else:
            axis, count_second = "gy", count_second // 2
        merge_plan.append((axis, bits[axis]))
        bits[axis] += 1
    return merge_plan


def staged(plan):
    stages, rest = [], list(plan)
    while len(rest) > LAST_STAGE:
        size = min(3, len(rest) - LAST_STAGE)
        stages.append(rest[:size])
        rest = rest[size:]
    return stages + [rest]


def point_tables():
    index = np.arange(NODE)
    points = -np.cos(np.pi * index / (NODE - 1))
    weights = np.where(index % 2 == 0, 1.0, -1.0)
    weights[[0, NODE - 1]] *= 2.0
    eye = np.eye(NODE)
    matrix = weights[:, None] / weights[None, :] / (points[:, None] - points[None, :] + eye)
    matrix = matrix * (1.0 - eye)
    matrix = matrix - np.diag(matrix.sum(axis=1))
    both = np.concatenate([np.kron(matrix, eye).T, np.kron(eye, matrix).T], axis=1)
    both = both.astype(np.float32)
    high = both.astype(jnp.bfloat16)
    low = (both - high.astype(np.float32)).astype(jnp.bfloat16)
    facing = np.zeros((SQUARE, 2 * SQUARE), np.float32)
    last = NODE - 1
    for k in range(NODE):
        facing[last * NODE + k, k] = 1.0
        facing[k, last * NODE + k] = 1.0
        facing[k * NODE + last, SQUARE + k * NODE] = 1.0
        facing[k * NODE, SQUARE + k * NODE + last] = 1.0
    packed = np.zeros((SQUARE, SQUARE // 2), np.float32)
    for q in range(4):
        for k in range(NODE):
            packed[(0 if q // 2 else last) * NODE + k, q * 2 * NODE + k] = 1.0
            packed[k * NODE + (0 if q % 2 else last), (q * 2 + 1) * NODE + k] = 1.0
    return np.concatenate([high, low, *(x.astype(jnp.bfloat16) for x in (facing, packed))], axis=1)


def split(x):
    high = x.astype(BF16)
    return high, (x - high.astype(F32)).astype(BF16)


def dot(left, right):
    return jnp.dot(left, right, preferred_element_type=F32)


def product(x, weight):
    high, low = weight
    rows, depth = x.shape
    wide = high.shape[1]
    if rows < 64:
        rest = x - x.astype(BF16).astype(F32)
        both = jnp.concatenate([x, rest], axis=0).astype(BF16)
        if depth == 128:
            both = jnp.concatenate([both, both], axis=1)
            out = dot(both, jnp.concatenate([high, low], axis=0))
        else:
            out = dot(both, high) + dot(both, low)
        return out[:rows] + out[rows:]
    x_high, x_low = split(x)
    if wide == 128:
        weights = jnp.concatenate([high, low], axis=1)
        if depth == 128:
            weights = jnp.concatenate([weights, weights], axis=0)
            out = dot(jnp.concatenate([x_high, x_low], axis=1), weights)
            return out[:, :128] + out[:, 128:]
        out = dot(x_high, weights)
        return out[:, :128] + dot(x_low, high) + out[:, 128:]
    if depth == 128:
        out = dot(jnp.concatenate([x_high, x_high], axis=1), jnp.concatenate([high, low], axis=0))
        return out + dot(x_low, high)
    return dot(x_high, high) + dot(x_low, high) + dot(x_high, low)


def spread_product(x, weight):
    high, low = split(x)
    moved = pltpu.roll(x - high.astype(F32), 64, 1).astype(BF16)
    is_left = left_half(x.shape)
    zero = jnp.zeros_like(high)
    first = [jnp.where(is_left, high, moved), jnp.where(is_left, high, zero)]
    second = [jnp.where(is_left, moved, high), jnp.where(is_left, zero, high)]
    both = jnp.concatenate([jnp.concatenate(k, axis=1) for k in (first, second)], axis=0)
    return dot(both, jnp.concatenate([weight[0]] * 2 + [weight[1]] * 2, axis=0))


def lanes(shape):
    return lax.broadcasted_iota(jnp.int32, shape, len(shape) - 1)


def left_half(shape):
    return lanes(shape) < shape[-1] // 2


def narrow(x, table):
    rows = x.shape[0]
    rest = x - x.astype(BF16).astype(F32)
    out = dot(jnp.concatenate([x, rest], axis=0).astype(BF16), table)
    out = out[:rows] + out[rows:]
    return out[:, :128] + out[:, 128:]


def broad(x, table):
    rows = x.shape[0]
    rest = x - x.astype(BF16).astype(F32)
    both = jnp.concatenate([x, rest], axis=0).astype(BF16)
    out = dot(jnp.concatenate([both, both], axis=1), table)
    return out[:rows] + out[rows:]


def rows_to_lanes(x, count):
    size = x.shape[0] // count
    return jnp.concatenate([x[k * size : (k + 1) * size] for k in range(count)], axis=1)


def lanes_to_rows(x):
    return jnp.concatenate([x[:, k : k + 128] for k in range(0, x.shape[1], 128)], axis=0)


def quarters(x):
    return [x[:128, :128], x[:128, 128:], x[128:, :128], x[128:, 128:]]


def merge_pair(former, latter):
    wide = product(former, split(rows_to_lanes(latter, 2)))
    return jnp.concatenate(quarters(wide), axis=0)


def parent_pair(upper, lower):
    a, b, c, d = quarters(product(lanes_to_rows(upper), split(lower)))
    return jnp.concatenate([a, c, b, d], axis=1)


def wide_split(x):
    return jnp.concatenate(split(x), axis=1)


def tall_split(x):
    return jnp.concatenate(split(x), axis=0)


def kernel(stages, leaf_side, tracer_count, *refs):
    names = ["u", "velocity", "inflow", "tables", "leaf_solve", "leaf_skeleton", "leaf_lift"]
    names += [a + "_" + b for a in ("merge", "parent", "sibling") for b in ("first", "second", "rest")]
    names += ["root_map"]
    hbm = dict(zip(names, refs[: len(names)]))
    out_ref = refs[len(names)]
    rest = refs[len(names) + 1 :]
    v = dict(zip(names, rest[: len(names)]))
    (
        load_sem, field, near, coef, force, solved,
        up_leaf, up_low, up_high, up_cross, fold, down_high, down_low, down_leaf,
        send_x, send_y, halo_x, halo_y, halo_send, halo_recv, here, up_edge, inner_16,
    ) = rest[len(names) : len(names) + 23]
    stage_refs = rest[len(names) + 23 :]
    T, L = tracer_count, leaf_side
    leaves = L * L
    rows = T * leaves
    half = SQUARE // 2

    loads = {}
    for k, name in enumerate(names):
        loads[name] = pltpu.make_async_copy(hbm[name], v[name], load_sem.at[k])
    order = ["u", "tables", "velocity", "inflow", "leaf_skeleton", "merge_first", "merge_second"]
    order += ["merge_rest", "parent_rest", "sibling_rest", "root_map", "parent_second", "parent_first"]
    order += ["leaf_lift", "leaf_solve", "sibling_first", "sibling_second"]

    place = {"gx": lax.axis_index("gx"), "gy": lax.axis_index("gy")}
    count = {"gx": lax.axis_size("gx"), "gy": lax.axis_size("gy")}
    bit_of = lambda axis, bit: lax.rem(place[axis] // (1 << bit), 2)

    def partner(stage, mask):
        target = dict(place)
        for k, (axis, bit) in enumerate(stage):
            if mask >> (len(stage) - 1 - k) & 1:
                target[axis] = target[axis] + (1 - 2 * bit_of(axis, bit)) * (1 << bit)
        return (target["gx"], target["gy"])

    barrier = pltpu.get_barrier_semaphore()
    expected = jnp.int32(0)
    has, beside = {}, {}
    for axis in ("gx", "gy"):
        for way in (-1, 1):
            spot = dict(place)
            spot[axis] = spot[axis] + way
            beside[axis, way] = (spot["gx"], spot["gy"])
            has[axis, way] = place[axis] > 0 if way < 0 else place[axis] < count[axis] - 1

            @pl.when(has[axis, way])
            def _(axis=axis, way=way):
                pl.semaphore_signal(barrier, inc=1, device_id=beside[axis, way], device_id_type=MESH)

            expected = expected + jnp.where(has[axis, way], 1, 0)
    for stage in stages[:-1]:
        for mask in range(1, 1 << len(stage)):
            pl.semaphore_signal(barrier, inc=1, device_id=partner(stage, mask), device_id_type=MESH)
            expected = expected + 1

    by_rank = sorted(stages[-1], key=lambda e: (e == ("gx", 0), e[0] == "gy", -e[1]))
    slots = 1 << len(by_rank)
    rank = jnp.int32(0)
    for axis, bit in by_rank:
        rank = rank * 2 + bit_of(axis, bit)

    cleared = dict(place)
    for axis, bit in by_rank:
        cleared[axis] = cleared[axis] - bit_of(axis, bit) * (1 << bit)

    def ranked(number):
        target = dict(cleared)
        for k, (axis, bit) in enumerate(reversed(by_rank)):
            target[axis] = target[axis] + (number >> k & 1) * (1 << bit)
        return (target["gx"], target["gy"])

    def greet(number):
        @pl.when(rank < number)
        def _():
            pl.semaphore_signal(barrier, inc=1, device_id=ranked(number), device_id_type=MESH)

    def answer(number):
        @pl.when(rank > number)
        def _():
            pl.semaphore_signal(here, inc=1, device_id=ranked(number), device_id_type=MESH)

    expected = expected + rank
    for name in order[:8]:
        loads[name].start()
    for number in reversed(range(slots)):
        greet(number)

    def spot_of(i, j):
        return sum(
            ((i >> b & 1) << (5 - 2 * b)) + ((j >> b & 1) << (4 - 2 * b)) for b in range(3)
        )

    grid = sorted((spot_of(i, j), i, j) for i in range(L) for j in range(L))
    block = lambda i, j: slice(spot_of(i, j) * T, spot_of(i, j) * T + T)
    by_tracer = lambda i, j, h: pl.ds(h * rows + i * L + j, T, stride=leaves)

    loads["u"].wait()
    plain = v["u"][...].astype(F32).reshape(rows, SQUARE)
    for h in range(2):
        field[h * rows : (h + 1) * rows, :] = plain[:, h * half : (h + 1) * half]
    u = jnp.concatenate(
        [
            jnp.concatenate([field[by_tracer(i, j, h), :] for _, i, j in grid], axis=0)
            for h in range(2)
        ],
        axis=1,
    )
    force[...] = u
    loads["tables"].wait()
    near[...] = dot(u.astype(BF16), v["tables"][:, 4 * SQUARE :])
    line = lambda spots, c: jnp.concatenate(
        [near[block(i, j), c * half : (c + 1) * half] for i, j in spots], axis=0
    )
    side = lambda axis, k: [(k, m) if axis == "gx" else (m, k) for m in range(L)]
    for k in range(2):
        for axis, target in (("gx", send_x), ("gy", send_y)):
            spots = side(axis, k * (L - 1))
            even, odd = line(spots[::2], 4), line(spots[1::2], 4)
            strip = lanes(even.shape) // (2 * NODE if axis == "gx" else 4 * NODE) % 2
            target[k] = jnp.where(strip == 0, even, odd).astype(BF16)

    def halo_copy(axis, way):
        k = 0 if way < 0 else 1
        source, target = (send_x, halo_x) if axis == "gx" else (send_y, halo_y)
        slot = k + (0 if axis == "gx" else 2)
        return pltpu.make_async_remote_copy(
            src_ref=source.at[k],
            dst_ref=target.at[k],
            send_sem=halo_send.at[slot],
            recv_sem=halo_recv.at[slot],
            device_id=beside[axis, way],
            device_id_type=MESH,
        )

    sides = [("gy", -1), ("gy", 1), ("gx", -1), ("gx", 1)]
    plan = [entry for stage in stages for entry in stage]
    bits = [bit_of(axis, bit) for axis, bit in plan]
    own_half = lambda k, w: jnp.where(bits[k] == 1, w[:, 128:], w[:, :128])
    twice = lambda w, axis: jnp.concatenate([w, w], axis=axis)
    merge = lambda k: v["merge_rest"][k]
    parent = lambda k: v["parent_rest"][k]

    own_parent = lambda k: own_half(k, parent(4 + k))

    def chained():
        chain = [own_parent(0)]
        for k in range(1, len(plan)):
            step = own_parent(k)
            if k > 1:
                step = product(step, split(own_parent(k - 1)))
            chain.append(product(step, split(chain[max(k - 2, 0)])))
        return chain

    def folded(levels, top, siblings, chain=()):
        weights = top
        for k in reversed(levels):
            groups = 1 << (levels[-1] - k)
            if weights is not None:
                weights = product(merge(4 + k), split(weights))
            elif siblings:
                weights = jnp.zeros((256, 128), F32)
            else:
                weights = merge(4 + k)
            blocks = [weights[:, g * 128 : (g + 1) * 128] for g in range(groups)]
            if siblings:
                sibling = own_half(k, v["sibling_rest"][4 + k])
                if k > 0:
                    sibling = product(sibling, split(chain[k - 1]))
                mine = jnp.int32(0)
                for later in levels:
                    if later > k:
                        mine = mine + bits[later] * (1 << (levels[-1] - later))
                blocks = [x + jnp.where(mine == g, sibling, 0.0) for g, x in enumerate(blocks)]
            weights = jnp.concatenate([x[:128] for x in blocks] + [x[128:] for x in blocks], axis=1)
        return lanes_to_rows(weights)

    first = len(plan) - len(stages[-1])
    last_levels = list(range(first, len(plan)))
    direct, folds = last_levels[: -FOLDED], last_levels[-FOLDED:]
    assert len(direct) == 2
    groups = 1 << len(folds)

    def edge_points(q):
        shape = (2 * NODE, SQUARE)
        k = lax.broadcasted_iota(jnp.int32, shape, 0)
        first = k + (SQUARE - NODE if q // 2 else 0)
        second = (k - NODE) * NODE + (NODE - 1 if q % 2 else 0)
        return jnp.where(lanes(shape) == jnp.where(k < NODE, first, second), 1.0, 0.0).astype(BF16)

    def prepare_up():
        for name in ("leaf_skeleton", "merge_first", "merge_second", "merge_rest"):
            loads[name].wait()
        two = [
            product(v["merge_first"][...].T, split(v["merge_second"][d * 64 : (d + 1) * 64, :]))
            for d in range(2)
        ]
        four = jnp.concatenate([two[d][c * 64 : (c + 1) * 64] for c in range(2) for d in range(2)], axis=1)
        up_leaf[...] = wide_split(lanes_to_rows(product(v["leaf_skeleton"][...].T, split(four))))
        at_edges = [
            dot(edge_points(q), up_leaf[q * SQUARE : (q + 1) * SQUARE, :]) for q in range(4)
        ]
        up_edge[...] = jnp.concatenate(at_edges * 2, axis=0).astype(BF16)
        up_low[...] = wide_split(merge_pair(merge(0), merge(1)))
        up_high[...] = wide_split(merge_pair(merge(2), merge(3)))


    def prepare_down():
        up_cross[...] = wide_split(folded(direct, None, False))
        for name in ("parent_rest", "sibling_rest", "root_map"):
            loads[name].wait()
        chain = chained()
        top = product(product(v["root_map"][...], split(own_parent(len(plan) - 1))), split(chain[-2]))
        fold[: groups * 128, :] = wide_split(folded(folds, top, True, chain))
        fold[groups * 128 :, :] = wide_split(folded(direct, None, True, chain))
        down_high[...] = tall_split(parent_pair(parent(3), parent(2)))
        down_low[...] = tall_split(parent_pair(parent(1), parent(0)))
        for name in ("parent_second", "parent_first", "leaf_lift"):
            loads[name].wait()
        halves = lambda x: jnp.concatenate([x, pltpu.roll(x, 64, 1)], axis=0)[:, :64]
        lifts = product(halves(v["parent_first"][...]), split(v["leaf_lift"][...]))
        lifts = jnp.concatenate([lifts[:64], lifts[64:]], axis=1)
        lifts = product(halves(v["parent_second"][...]), split(lifts))
        down_leaf[...] = tall_split(
            jnp.concatenate(
                [
                    lifts[d * 128 : (d + 1) * 128, c * SQUARE : (c + 1) * SQUARE]
                    for c in range(2)
                    for d in range(2)
                ],
                axis=1,
            )
        )

    own = lax.broadcasted_iota(jnp.int32, (leaves, L), 0) % L == lanes((leaves, L))

    def column(values):
        wide = jnp.concatenate(
            [jnp.broadcast_to(values[i : i + 1, :], (L, L)) for i in range(L)], axis=0
        )
        return jnp.sum(jnp.where(own, wide, 0.0), axis=1, keepdims=True)

    tile = (T, half)
    on_0, on_1 = lanes(tile) < NODE, lanes(tile) >= half - NODE
    on_2, on_3 = lanes(tile) % NODE == 0, lanes(tile) % NODE == NODE - 1
    at_leaf = lambda k, i, j: jnp.broadcast_to(coef[k, i * L + j : i * L + j + 1, :], tile)
    keep_if = lambda mask, x: jnp.where(mask, x, 0.0)
    strength = lambda s, i, j: at_leaf(2 + s, i, j)


    def interior():
        loads["velocity"].wait()
        loads["inflow"].wait()
        speed = [v["velocity"][k] for k in range(2)]
        columns = [column(x) for x in speed]
        columns += [
            column(v["inflow"][s].astype(F32) * (NODE * jnp.abs(speed[s // 2]))) for s in range(4)
        ]
        for k, x in enumerate(columns):
            coef[k] = jnp.broadcast_to(x, (leaves, half))

        for q in range(4):
            low, top = q * rows // 4, (q + 1) * rows // 4
            u = force[low:top, :]
            part = u.astype(BF16)
            grads = dot(part, v["tables"][:, : 2 * SQUARE])
            grads = grads + dot(part, v["tables"][:, 2 * SQUARE : 4 * SQUARE])
            for spot, i, j in grid[q * leaves // 4 : (q + 1) * leaves // 4]:
                at = slice(spot * T, spot * T + T)
                inside = slice(spot * T - low, spot * T + T - low)
                speeds = [at_leaf(k, i, j) for k in range(2)]
                w = [strength(s, i, j) for s in range(4)]
                w_2, w_3 = keep_if(on_2, w[2]), keep_if(on_3, w[3])
                for c in range(2):
                    cut = slice(c * half, (c + 1) * half)
                    far = slice((2 + c) * half, (3 + c) * half)
                    total = u[inside, cut] * (1.0 - (keep_if((on_0, on_1)[c], w[c]) + w_2 + w_3))
                    total = total - speeds[0] * grads[inside, cut] - speeds[1] * grads[inside, far]
                    ahead = i - 1 if c == 0 else i + 1
                    if 0 <= ahead < L:
                        total = total + w[c] * near[block(ahead, j), cut]
                    if j > 0:
                        total = total + w_2 * near[block(i, j - 1), far]
                    if j < L - 1:
                        total = total + w_3 * near[block(i, j + 1), far]
                    force[at, cut] = total


    for axis, way in sides:
        slot = 1 if way < 0 else 0

        @pl.when(jnp.logical_not(has[axis, way]))
        def _(axis=axis, slot=slot):
            target = halo_x if axis == "gx" else halo_y
            target[slot] = jnp.zeros_like(target[slot])

    def announce():
        pl.semaphore_wait(barrier, expected)
        for axis, way in sides:

            @pl.when(has[axis, way])
            def _(axis=axis, way=way):
                halo_copy(axis, way).start()

        for number in range(slots):
            answer(number)

    announce()
    prepare_up()
    interior()
    high, low = split(rows_to_lanes(force[...], 4))
    wide = dot(high, up_leaf[...])
    inner_16[...] = wide[:, :128] + wide[:, 128:] + dot(low, up_leaf[:, :128])
    for name in order[8:]:
        loads[name].start()
    early = rank < slots // 16

    @pl.when(early)
    def _():
        prepare_down()


    edge_weights = []
    for axis, way in sides:
        across = 0 if axis == "gx" else 1
        k = 2 * across + (0 if way < 0 else 1)
        spots = side(axis, 0 if way < 0 else L - 1)
        for m in range(L // 2):
            w = jnp.zeros(tile, F32)
            for i, j in spots[2 * m : 2 * m + 2]:
                q, box = divmod(spot_of(i, j), leaves // 4)
                w = jnp.where(lanes(tile) // NODE == 2 * q + across, strength(k, i, j), w)
            edge_weights.append((axis, way, m, box, w))
    for axis, way in sides:

        @pl.when(has[axis, way])
        def _(axis=axis, way=way):
            halo_copy(axis, -way).wait_recv()

    edges = [None] * (leaves // 4)
    for axis, way, m, box, w in edge_weights:
        arrived = (halo_x if axis == "gx" else halo_y)[1 if way < 0 else 0].astype(F32)
        term = w * arrived[m * T : m * T + T]
        edges[box] = term if edges[box] is None else edges[box] + term
    edges = jnp.concatenate([jnp.zeros(tile, F32) if x is None else x for x in edges], axis=0)
    edges = jnp.concatenate(split(edges), axis=1)
    wide = dot(edges, up_edge[...])
    current_16 = inner_16[...] + wide[:, :128] + wide[:, 128:]
    current_4 = narrow(rows_to_lanes(current_16, 4), up_low[...])
    current = narrow(rows_to_lanes(current_4, 4), up_high[...])

    joined = lambda x: rows_to_lanes(x, 2)
    level = 4
    path = []
    for number, stage in enumerate(stages):
        pool, stage_send, stage_recv = stage_refs[3 * number : 3 * number + 3]
        own_slot = jnp.int32(0)
        for axis, bit in stage:
            own_slot = own_slot * 2 + bit_of(axis, bit)
        pool[own_slot] = current
        final = number == len(stages) - 1
        copies = [] if final else [
            pltpu.make_async_remote_copy(
                src_ref=pool.at[own_slot],
                dst_ref=pool.at[own_slot],
                send_sem=stage_send.at[mask],
                recv_sem=stage_recv.at[mask],
                device_id=partner(stage, mask),
                device_id_type=MESH,
            )
            for mask in range(1, 1 << len(stage))
        ]
        for copy in reversed(copies):
            copy.start()
        if final:

            @pl.when(rank < slots - 1)
            def _():
                pl.semaphore_wait(here, slots - 1 - rank)


            for other in range(slots):

                @pl.when(rank != other)
                def _(other=other):
                    pltpu.make_async_remote_copy(
                        src_ref=pool.at[own_slot],
                        dst_ref=pool.at[own_slot],
                        send_sem=stage_send.at[0],
                        recv_sem=stage_recv.at[0],
                        device_id=ranked(other),
                        device_id_type=MESH,
                    ).start()

            every = pltpu.make_async_remote_copy(
                src_ref=pool.at[pl.ds(0, slots - 1)],
                dst_ref=pool.at[pl.ds(0, slots - 1)],
                send_sem=stage_send.at[0],
                recv_sem=stage_recv.at[0],
                device_id=partner(stage, 1),
                device_id_type=MESH,
            )
        if number == 0:

            @pl.when(jnp.logical_not(early))
            def _():
                prepare_down()

            for name in ("leaf_solve", "sibling_first", "sibling_second"):
                loads[name].wait()
            turned = [jnp.concatenate([edge_points(q)] * 2, axis=0) for q in range(4)]
            of_quarter = lambda q: jnp.concatenate(
                [edges[:, k + q * 32 : k + q * 32 + 32] for k in (0, 128)], axis=1
            )
            forcing = jnp.concatenate(
                [
                    force[q * 128 : (q + 1) * 128, :] + dot(of_quarter(q), turned[q])
                    for q in range(4)
                ],
                axis=0,
            )
            sibling = lambda k: split(v["sibling_rest"][k])
            is_left = lambda x: left_half(x.shape)

            def gathered(x):
                middle = x.shape[0] // 2
                return jnp.where(is_left(x[:middle]), x[:middle], x[middle:])

            cat_0 = gathered(product(forcing, split(twice(v["leaf_skeleton"][...], 0).T)))
            cat_1 = gathered(product(cat_0, split(twice(v["merge_first"][...], 0).T)))
            cats = [joined(current_16)]
            cats.append(joined(product(cats[0], split(merge(0)))))
            cats.append(joined(current_4))
            cats.append(joined(product(cats[2], split(merge(2)))))
            own_part = product(cats[3], sibling(3))
            for k in (2, 1, 0):
                own_part = product(lanes_to_rows(own_part), split(parent(k)))
                own_part = own_part + product(cats[k], sibling(k))
            own_part = product(lanes_to_rows(own_part), split(v["parent_second"][...]))
            own_part = own_part + product(cat_1, split(v["sibling_second"][...]))
            own_part = spread_product(own_part, split(v["parent_first"][...]))
            own_part = own_part + product(cat_0, split(v["sibling_first"][...]))
            own_part = spread_product(own_part, split(v["leaf_lift"][...]))
            solved[...] = own_part + product(forcing, split(v["leaf_solve"][...]))
        if final:
            known = jnp.zeros((T, 128), F32)
            chain = chained() if path else ()
            for k, term in enumerate(path):
                term = own_half(k, term)
                known = known + (product(term, split(chain[k - 1])) if k > 0 else term)
        if final:
            for axis, way in sides:

                @pl.when(has[axis, way])
                def _(axis=axis, way=way):
                    halo_copy(axis, way).wait_send()

            every.wait_recv()
            break
        for copy in copies:
            copy.wait()
        current = pool[...].reshape(T << len(stage), 128)
        for k, (axis, bit) in enumerate(stage):
            cat = joined(current)
            mine = cat
            for later_axis, later_bit in stage[k + 1 :]:
                middle = mine.shape[0] // 2
                mine = jnp.where(bit_of(later_axis, later_bit) == 1, mine[middle:], mine[:middle])
            path.append(product(mine, split(v["sibling_rest"][level])))
            current = product(cat, split(merge(level)))
            level += 1

    everyone = pool[...].reshape(slots * T, 128)
    merged = narrow(rows_to_lanes(everyone, slots // groups), up_cross[...])
    mine = jnp.int32(0)
    for k in folds:
        mine = mine * 2 + bits[k]
    slabs = [rows_to_lanes(merged, groups)]
    slabs += [pool[k * groups + mine] for k in range(slots // groups)]
    boundary = narrow(jnp.concatenate(slabs, axis=1), fold[...]) + known
    boundary = lanes_to_rows(broad(boundary, down_high[...]))
    boundary = lanes_to_rows(broad(boundary, down_low[...]))
    high, low = split(boundary)
    both = twice(high, 1)
    for q in range(4):
        cut = slice(q * SQUARE, (q + 1) * SQUARE)
        lifted = dot(both, down_leaf[:, cut]) + dot(low, down_leaf[:128, cut])
        for spot, i, j in grid[q * leaves // 4 : (q + 1) * leaves // 4]:
            inside = spot * T - q * rows // 4
            for h in range(2):
                one = lifted[inside : inside + T, h * half : (h + 1) * half]
                one = one + solved[spot * T : spot * T + T, h * half : (h + 1) * half]
                field[by_tracer(i, j, h), :] = one
    updated = jnp.concatenate([field[:rows, :], field[rows:, :]], axis=1)
    out_ref[...] = updated.reshape(out_ref.shape).astype(out_ref.dtype)
    every.wait_send()


def local(tables, count_first, count_second, tracers, *operands):
    T, L = tracers.shape[0], tracers.shape[1]
    assert L == 8 and local_plan(L) == [1, 2] * 3
    stages = staged(cross_plan(count_first, count_second))
    rows = T * L * L
    args = [tracers, operands[0], operands[1], tables] + list(operands[2:])
    args[5], args[7] = args[5].T, args[7].T
    vmem, dma = pltpu.VMEM, pltpu.SemaphoreType.DMA
    scratch = [vmem(a.shape, a.dtype) for a in args]
    slots = 1 << len(stages[-1])
    groups = 1 << FOLDED
    scratch += [
        dma((len(args),)),
        vmem((2 * rows, 128), F32),
        vmem((rows, 2 * SQUARE + SQUARE // 2), F32),
        vmem((6, L * L, 128), F32),
        vmem((rows, SQUARE), F32),
        vmem((rows, SQUARE), F32),
        vmem((4 * SQUARE, 256), BF16),
        vmem((512, 256), BF16),
        vmem((512, 256), BF16),
        vmem((slots // groups * 128, 256), BF16),
        vmem(((groups + slots // groups) * 128, 256), BF16),
        vmem((256, 512), BF16),
        vmem((256, 512), BF16),
        vmem((256, 4 * SQUARE), BF16),
        vmem((2, T * L // 2, 128), BF16),
        vmem((2, T * L // 2, 128), BF16),
        vmem((2, T * L // 2, 128), BF16),
        vmem((2, T * L // 2, 128), BF16),
        dma((4,)),
        dma((4,)),
        pltpu.SemaphoreType.REGULAR,
        vmem((256, 256), BF16),
        vmem((T * L * L // 4, 128), F32),
    ]
    for stage in stages:
        slots = 1 << len(stage)
        scratch += [vmem((slots, T, 128), F32), dma((slots,)), dma((slots,))]
    return pl.pallas_call(
        functools.partial(kernel, stages, L, T),
        out_shape=jax.ShapeDtypeStruct(tracers.shape, tracers.dtype),
        in_specs=[pl.BlockSpec(memory_space=pl.ANY)] * len(args),
        out_specs=pl.BlockSpec(memory_space=pltpu.VMEM),
        scratch_shapes=scratch,
        compiler_params=pltpu.CompilerParams(
            collective_id=0, has_side_effects=True, vmem_limit_bytes=VMEM_LIMIT
        ),
    )(*[pltpu.with_memory_space_constraint(a, pltpu.HBM) for a in args])


def solution(mesh):
    tables = point_tables()
    split_both = P(None, "gx", "gy")
    in_specs = (P(None, "gx", "gy", None), split_both, split_both) + (P(),) * 13

    def body(*args):
        return local(
            jnp.asarray(tables), mesh.shape["gx"], mesh.shape["gy"], *args
        )

    return jax.shard_map(
        body,
        mesh=mesh,
        in_specs=in_specs,
        out_specs=P(None, "gx", "gy", None),
        check_vma=False,
    )
```

```python
import functools

import jax
import jax.numpy as jnp
import numpy as np
from jax import lax
from jax.experimental import pallas as pl
from jax.experimental.pallas import tpu as pltpu
from jax.sharding import PartitionSpec as P

NODE = 16
SQUARE = NODE * NODE
F32 = jnp.float32
BF16 = jnp.bfloat16
VMEM_LIMIT = 32 * 1024 * 1024
MESH = pl.DeviceIdType.MESH
LAST_STAGE = 5
FOLDED = 3


def local_plan(leaf_side):
    merge_plan = []
    block_span = leaf_side
    while block_span > 1:
        merge_plan = merge_plan + [1, 2]
        block_span = block_span // 2
    return merge_plan


def cross_plan(count_first, count_second):
    merge_plan = []
    bits = {"gx": 0, "gy": 0}
    while count_first * count_second > 1:
        if count_first >= count_second:
            axis, count_first = "gx", count_first // 2
        else:
            axis, count_second = "gy", count_second // 2
        merge_plan.append((axis, bits[axis]))
        bits[axis] += 1
    return merge_plan


def staged(plan):
    stages, rest = [], list(plan)
    while len(rest) > LAST_STAGE:
        size = min(3, len(rest) - LAST_STAGE)
        stages.append(rest[:size])
        rest = rest[size:]
    return stages + [rest]


def point_tables():
    index = np.arange(NODE)
    points = -np.cos(np.pi * index / (NODE - 1))
    weights = np.where(index % 2 == 0, 1.0, -1.0)
    weights[[0, NODE - 1]] *= 2.0
    eye = np.eye(NODE)
    matrix = weights[:, None] / weights[None, :] / (points[:, None] - points[None, :] + eye)
    matrix = matrix * (1.0 - eye)
    matrix = matrix - np.diag(matrix.sum(axis=1))
    both = np.concatenate([np.kron(matrix, eye).T, np.kron(eye, matrix).T], axis=1)
    both = both.astype(np.float32)
    high = both.astype(jnp.bfloat16)
    low = (both - high.astype(np.float32)).astype(jnp.bfloat16)
    facing = np.zeros((SQUARE, 2 * SQUARE), np.float32)
    last = NODE - 1
    for k in range(NODE):
        facing[last * NODE + k, k] = 1.0
        facing[k, last * NODE + k] = 1.0
        facing[k * NODE + last, SQUARE + k * NODE] = 1.0
        facing[k * NODE, SQUARE + k * NODE + last] = 1.0
    packed = np.zeros((SQUARE, SQUARE // 2), np.float32)
    for q in range(4):
        for k in range(NODE):
            packed[(0 if q // 2 else last) * NODE + k, q * 2 * NODE + k] = 1.0
            packed[k * NODE + (0 if q % 2 else last), (q * 2 + 1) * NODE + k] = 1.0
    return np.concatenate([high, low, *(x.astype(jnp.bfloat16) for x in (facing, packed))], axis=1)


def split(x):
    high = x.astype(BF16)
    return high, (x - high.astype(F32)).astype(BF16)


def dot(left, right):
    return jnp.dot(left, right, preferred_element_type=F32)


def product(x, weight):
    high, low = weight
    rows, depth = x.shape
    wide = high.shape[1]
    if rows < 64:
        rest = x - x.astype(BF16).astype(F32)
        both = jnp.concatenate([x, rest], axis=0).astype(BF16)
        if depth == 128:
            both = jnp.concatenate([both, both], axis=1)
            out = dot(both, jnp.concatenate([high, low], axis=0))
        else:
            out = dot(both, high) + dot(both, low)
        return out[:rows] + out[rows:]
    x_high, x_low = split(x)
    if wide == 128:
        weights = jnp.concatenate([high, low], axis=1)
        if depth == 128:
            weights = jnp.concatenate([weights, weights], axis=0)
            out = dot(jnp.concatenate([x_high, x_low], axis=1), weights)
            return out[:, :128] + out[:, 128:]
        out = dot(x_high, weights)
        return out[:, :128] + dot(x_low, high) + out[:, 128:]
    if depth == 128:
        out = dot(jnp.concatenate([x_high, x_high], axis=1), jnp.concatenate([high, low], axis=0))
        return out + dot(x_low, high)
    return dot(x_high, high) + dot(x_low, high) + dot(x_high, low)


def spread_product(x, weight):
    high, low = split(x)
    moved = pltpu.roll(x - high.astype(F32), 64, 1).astype(BF16)
    is_left = left_half(x.shape)
    zero = jnp.zeros_like(high)
    first = [jnp.where(is_left, high, moved), jnp.where(is_left, high, zero)]
    second = [jnp.where(is_left, moved, high), jnp.where(is_left, zero, high)]
    both = jnp.concatenate([jnp.concatenate(k, axis=1) for k in (first, second)], axis=0)
    return dot(both, jnp.concatenate([weight[0]] * 2 + [weight[1]] * 2, axis=0))


def lanes(shape):
    return lax.broadcasted_iota(jnp.int32, shape, len(shape) - 1)


def left_half(shape):
    return lanes(shape) < shape[-1] // 2


def narrow(x, table):
    rows = x.shape[0]
    rest = x - x.astype(BF16).astype(F32)
    out = dot(jnp.concatenate([x, rest], axis=0).astype(BF16), table)
    out = out[:rows] + out[rows:]
    return out[:, :128] + out[:, 128:]


def broad(x, table):
    rows = x.shape[0]
    rest = x - x.astype(BF16).astype(F32)
    both = jnp.concatenate([x, rest], axis=0).astype(BF16)
    out = dot(jnp.concatenate([both, both], axis=1), table)
    return out[:rows] + out[rows:]


def rows_to_lanes(x, count):
    size = x.shape[0] // count
    return jnp.concatenate([x[k * size : (k + 1) * size] for k in range(count)], axis=1)


def lanes_to_rows(x):
    return jnp.concatenate([x[:, k : k + 128] for k in range(0, x.shape[1], 128)], axis=0)


def quarters(x):
    return [x[:128, :128], x[:128, 128:], x[128:, :128], x[128:, 128:]]


def merge_pair(former, latter):
    wide = product(former, split(rows_to_lanes(latter, 2)))
    return jnp.concatenate(quarters(wide), axis=0)


def parent_pair(upper, lower):
    a, b, c, d = quarters(product(lanes_to_rows(upper), split(lower)))
    return jnp.concatenate([a, c, b, d], axis=1)


def wide_split(x):
    return jnp.concatenate(split(x), axis=1)


def tall_split(x):
    return jnp.concatenate(split(x), axis=0)


def kernel(stages, leaf_side, tracer_count, *refs):
    names = ["u", "velocity", "inflow", "tables", "leaf_solve", "leaf_skeleton", "leaf_lift"]
    names += [a + "_" + b for a in ("merge", "parent", "sibling") for b in ("first", "second", "rest")]
    names += ["root_map"]
    hbm = dict(zip(names, refs[: len(names)]))
    out_ref = refs[len(names)]
    rest = refs[len(names) + 1 :]
    v = dict(zip(names, rest[: len(names)]))
    (
        load_sem, field, near, coef, force, solved,
        up_leaf, up_low, up_high, up_cross, fold, down_high, down_low, down_leaf,
        send_x, send_y, halo_x, halo_y, halo_send, halo_recv, here, up_edge, inner_16,
    ) = rest[len(names) : len(names) + 23]
    stage_refs = rest[len(names) + 23 :]
    T, L = tracer_count, leaf_side
    leaves = L * L
    rows = T * leaves
    half = SQUARE // 2

    loads = {}
    for k, name in enumerate(names):
        loads[name] = pltpu.make_async_copy(hbm[name], v[name], load_sem.at[k])
    order = ["u", "tables", "velocity", "inflow", "leaf_skeleton", "merge_first", "merge_second"]
    order += ["merge_rest", "parent_rest", "sibling_rest", "root_map", "parent_second", "parent_first"]
    order += ["leaf_lift", "leaf_solve", "sibling_first", "sibling_second"]

    place = {"gx": lax.axis_index("gx"), "gy": lax.axis_index("gy")}
    count = {"gx": lax.axis_size("gx"), "gy": lax.axis_size("gy")}
    bit_of = lambda axis, bit: lax.rem(place[axis] // (1 << bit), 2)

    def partner(stage, mask):
        target = dict(place)
        for k, (axis, bit) in enumerate(stage):
            if mask >> (len(stage) - 1 - k) & 1:
                target[axis] = target[axis] + (1 - 2 * bit_of(axis, bit)) * (1 << bit)
        return (target["gx"], target["gy"])

    barrier = pltpu.get_barrier_semaphore()
    expected = jnp.int32(0)
    has, beside = {}, {}
    for axis in ("gx", "gy"):
        for way in (-1, 1):
            spot = dict(place)
            spot[axis] = spot[axis] + way
            beside[axis, way] = (spot["gx"], spot["gy"])
            has[axis, way] = place[axis] > 0 if way < 0 else place[axis] < count[axis] - 1

            @pl.when(has[axis, way])
            def _(axis=axis, way=way):
                pl.semaphore_signal(barrier, inc=1, device_id=beside[axis, way], device_id_type=MESH)

            expected = expected + jnp.where(has[axis, way], 1, 0)
    for stage in stages[:-1]:
        for mask in range(1, 1 << len(stage)):
            pl.semaphore_signal(barrier, inc=1, device_id=partner(stage, mask), device_id_type=MESH)
            expected = expected + 1

    by_rank = sorted(stages[-1], key=lambda e: (e == ("gx", 0), e[0] == "gy", -e[1]))
    slots = 1 << len(by_rank)
    rank = jnp.int32(0)
    for axis, bit in by_rank:
        rank = rank * 2 + bit_of(axis, bit)

    cleared = dict(place)
    for axis, bit in by_rank:
        cleared[axis] = cleared[axis] - bit_of(axis, bit) * (1 << bit)

    def ranked(number):
        target = dict(cleared)
        for k, (axis, bit) in enumerate(reversed(by_rank)):
            target[axis] = target[axis] + (number >> k & 1) * (1 << bit)
        return (target["gx"], target["gy"])

    def greet(number):
        @pl.when(rank < number)
        def _():
            pl.semaphore_signal(barrier, inc=1, device_id=ranked(number), device_id_type=MESH)

    def answer(number):
        @pl.when(rank > number)
        def _():
            pl.semaphore_signal(here, inc=1, device_id=ranked(number), device_id_type=MESH)

    expected = expected + rank
    for name in order[:8]:
        loads[name].start()
    for number in reversed(range(slots)):
        greet(number)

    def spot_of(i, j):
        return sum(
            ((i >> b & 1) << (5 - 2 * b)) + ((j >> b & 1) << (4 - 2 * b)) for b in range(3)
        )

    grid = sorted((spot_of(i, j), i, j) for i in range(L) for j in range(L))
    block = lambda i, j: slice(spot_of(i, j) * T, spot_of(i, j) * T + T)
    by_tracer = lambda i, j, h: pl.ds(h * rows + i * L + j, T, stride=leaves)

    loads["u"].wait()
    plain = v["u"][...].astype(F32).reshape(rows, SQUARE)
    for h in range(2):
        field[h * rows : (h + 1) * rows, :] = plain[:, h * half : (h + 1) * half]

    def of_leaves(spots):
        return jnp.concatenate(
            [
                jnp.concatenate([field[by_tracer(i, j, h), :] for i, j in spots], axis=0)
                for h in range(2)
            ],
            axis=1,
        )

    side = lambda axis, k: [(k, m) if axis == "gx" else (m, k) for m in range(L)]
    borders = [(axis, k) for axis in ("gx", "gy") for k in range(2)]
    spots = [side(axis, k * (L - 1)) for axis, k in borders]
    border = of_leaves([x for line in spots for x in line[::2] + line[1::2]]).astype(BF16)
    loads["tables"].wait()
    border = dot(border, v["tables"][:, 6 * SQUARE :])
    for number, (axis, k) in enumerate(borders):
        low = number * T * L
        even = border[low : low + T * L // 2]
        odd = border[low + T * L // 2 : low + T * L]
        strip = lanes(even.shape) // (2 * NODE if axis == "gx" else 4 * NODE) % 2
        target = send_x if axis == "gx" else send_y
        target[k] = jnp.where(strip == 0, even, odd).astype(BF16)

    def halo_copy(axis, way):
        k = 0 if way < 0 else 1
        source, target = (send_x, halo_x) if axis == "gx" else (send_y, halo_y)
        slot = k + (0 if axis == "gx" else 2)
        return pltpu.make_async_remote_copy(
            src_ref=source.at[k],
            dst_ref=target.at[k],
            send_sem=halo_send.at[slot],
            recv_sem=halo_recv.at[slot],
            device_id=beside[axis, way],
            device_id_type=MESH,
        )

    sides = [("gy", -1), ("gy", 1), ("gx", -1), ("gx", 1)]
    plan = [entry for stage in stages for entry in stage]
    bits = [bit_of(axis, bit) for axis, bit in plan]
    own_half = lambda k, w: jnp.where(bits[k] == 1, w[:, 128:], w[:, :128])
    twice = lambda w, axis: jnp.concatenate([w, w], axis=axis)
    merge = lambda k: v["merge_rest"][k]
    parent = lambda k: v["parent_rest"][k]

    own_parent = lambda k: own_half(k, parent(4 + k))

    def chained():
        chain = [own_parent(0)]
        for k in range(1, len(plan)):
            step = own_parent(k)
            if k > 1:
                step = product(step, split(own_parent(k - 1)))
            chain.append(product(step, split(chain[max(k - 2, 0)])))
        return chain

    def folded(levels, top, siblings, chain=()):
        weights = top
        for k in reversed(levels):
            groups = 1 << (levels[-1] - k)
            if weights is not None:
                weights = product(merge(4 + k), split(weights))
            elif siblings:
                weights = jnp.zeros((256, 128), F32)
            else:
                weights = merge(4 + k)
            blocks = [weights[:, g * 128 : (g + 1) * 128] for g in range(groups)]
            if siblings:
                sibling = own_half(k, v["sibling_rest"][4 + k])
                if k > 0:
                    sibling = product(sibling, split(chain[k - 1]))
                mine = jnp.int32(0)
                for later in levels:
                    if later > k:
                        mine = mine + bits[later] * (1 << (levels[-1] - later))
                blocks = [x + jnp.where(mine == g, sibling, 0.0) for g, x in enumerate(blocks)]
            weights = jnp.concatenate([x[:128] for x in blocks] + [x[128:] for x in blocks], axis=1)
        return lanes_to_rows(weights)

    first = len(plan) - len(stages[-1])
    last_levels = list(range(first, len(plan)))
    direct, folds = last_levels[: -FOLDED], last_levels[-FOLDED:]
    assert len(direct) == 2
    groups = 1 << len(folds)

    def edge_points(q):
        shape = (2 * NODE, SQUARE)
        k = lax.broadcasted_iota(jnp.int32, shape, 0)
        first = k + (SQUARE - NODE if q // 2 else 0)
        second = (k - NODE) * NODE + (NODE - 1 if q % 2 else 0)
        return jnp.where(lanes(shape) == jnp.where(k < NODE, first, second), 1.0, 0.0).astype(BF16)

    def prepare_up():
        for name in ("leaf_skeleton", "merge_first", "merge_second", "merge_rest"):
            loads[name].wait()
        two = [
            product(v["merge_first"][...].T, split(v["merge_second"][d * 64 : (d + 1) * 64, :]))
            for d in range(2)
        ]
        four = jnp.concatenate([two[d][c * 64 : (c + 1) * 64] for c in range(2) for d in range(2)], axis=1)
        up_leaf[...] = wide_split(lanes_to_rows(product(v["leaf_skeleton"][...].T, split(four))))
        at_edges = [
            dot(edge_points(q), up_leaf[q * SQUARE : (q + 1) * SQUARE, :]) for q in range(4)
        ]
        up_edge[...] = jnp.concatenate(at_edges * 2, axis=0).astype(BF16)
        up_low[...] = wide_split(merge_pair(merge(0), merge(1)))
        up_high[...] = wide_split(merge_pair(merge(2), merge(3)))


    def prepare_down():
        up_cross[...] = wide_split(folded(direct, None, False))
        for name in ("parent_rest", "sibling_rest", "root_map"):
            loads[name].wait()
        chain = chained()
        top = product(product(v["root_map"][...], split(own_parent(len(plan) - 1))), split(chain[-2]))
        fold[: groups * 128, :] = wide_split(folded(folds, top, True, chain))
        fold[groups * 128 :, :] = wide_split(folded(direct, None, True, chain))
        down_high[...] = tall_split(parent_pair(parent(3), parent(2)))
        down_low[...] = tall_split(parent_pair(parent(1), parent(0)))
        for name in ("parent_second", "parent_first", "leaf_lift"):
            loads[name].wait()
        halves = lambda x: jnp.concatenate([x, pltpu.roll(x, 64, 1)], axis=0)[:, :64]
        lifts = product(halves(v["parent_first"][...]), split(v["leaf_lift"][...]))
        lifts = jnp.concatenate([lifts[:64], lifts[64:]], axis=1)
        lifts = product(halves(v["parent_second"][...]), split(lifts))
        down_leaf[...] = tall_split(
            jnp.concatenate(
                [
                    lifts[d * 128 : (d + 1) * 128, c * SQUARE : (c + 1) * SQUARE]
                    for c in range(2)
                    for d in range(2)
                ],
                axis=1,
            )
        )

    own = lax.broadcasted_iota(jnp.int32, (leaves, L), 0) % L == lanes((leaves, L))

    def column(values):
        wide = jnp.concatenate(
            [jnp.broadcast_to(values[i : i + 1, :], (L, L)) for i in range(L)], axis=0
        )
        return jnp.sum(jnp.where(own, wide, 0.0), axis=1, keepdims=True)

    tile = (T, half)
    on_0, on_1 = lanes(tile) < NODE, lanes(tile) >= half - NODE
    on_2, on_3 = lanes(tile) % NODE == 0, lanes(tile) % NODE == NODE - 1
    at_leaf = lambda k, i, j: jnp.broadcast_to(coef[k, i * L + j : i * L + j + 1, :], tile)
    keep_if = lambda mask, x: jnp.where(mask, x, 0.0)
    strength = lambda s, i, j: at_leaf(2 + s, i, j)


    def interior():
        whole = of_leaves([(i, j) for _, i, j in grid])
        force[...] = whole
        whole = whole.astype(BF16)
        near[...] = dot(whole, v["tables"][:, 4 * SQUARE : 6 * SQUARE])
        loads["velocity"].wait()
        loads["inflow"].wait()
        speed = [v["velocity"][k] for k in range(2)]
        columns = [column(x) for x in speed]
        columns += [
            column(v["inflow"][s].astype(F32) * (NODE * jnp.abs(speed[s // 2]))) for s in range(4)
        ]
        for k, x in enumerate(columns):
            coef[k] = jnp.broadcast_to(x, (leaves, half))

        for q in range(4):
            low, top = q * rows // 4, (q + 1) * rows // 4
            u = force[low:top, :]
            part = u.astype(BF16)
            grads = dot(part, v["tables"][:, : 2 * SQUARE])
            grads = grads + dot(part, v["tables"][:, 2 * SQUARE : 4 * SQUARE])
            for spot, i, j in grid[q * leaves // 4 : (q + 1) * leaves // 4]:
                at = slice(spot * T, spot * T + T)
                inside = slice(spot * T - low, spot * T + T - low)
                speeds = [at_leaf(k, i, j) for k in range(2)]
                w = [strength(s, i, j) for s in range(4)]
                w_2, w_3 = keep_if(on_2, w[2]), keep_if(on_3, w[3])
                for c in range(2):
                    cut = slice(c * half, (c + 1) * half)
                    far = slice((2 + c) * half, (3 + c) * half)
                    total = u[inside, cut] * (1.0 - (keep_if((on_0, on_1)[c], w[c]) + w_2 + w_3))
                    total = total - speeds[0] * grads[inside, cut] - speeds[1] * grads[inside, far]
                    ahead = i - 1 if c == 0 else i + 1
                    if 0 <= ahead < L:
                        total = total + w[c] * near[block(ahead, j), cut]
                    if j > 0:
                        total = total + w_2 * near[block(i, j - 1), far]
                    if j < L - 1:
                        total = total + w_3 * near[block(i, j + 1), far]
                    force[at, cut] = total


    for axis, way in sides:
        slot = 1 if way < 0 else 0

        @pl.when(jnp.logical_not(has[axis, way]))
        def _(axis=axis, slot=slot):
            target = halo_x if axis == "gx" else halo_y
            target[slot] = jnp.zeros_like(target[slot])

    def announce():
        pl.semaphore_wait(barrier, expected)
        for axis, way in sides:

            @pl.when(has[axis, way])
            def _(axis=axis, way=way):
                halo_copy(axis, way).start()

        for number in range(slots):
            answer(number)

    announce()
    prepare_up()
    interior()
    high, low = split(rows_to_lanes(force[...], 4))
    wide = dot(high, up_leaf[...])
    inner_16[...] = wide[:, :128] + wide[:, 128:] + dot(low, up_leaf[:, :128])
    for name in order[8:]:
        loads[name].start()
    early = rank < slots // 16

    @pl.when(early)
    def _():
        prepare_down()


    edge_weights = []
    for axis, way in sides:
        across = 0 if axis == "gx" else 1
        k = 2 * across + (0 if way < 0 else 1)
        spots = side(axis, 0 if way < 0 else L - 1)
        for m in range(L // 2):
            w = jnp.zeros(tile, F32)
            for i, j in spots[2 * m : 2 * m + 2]:
                q, box = divmod(spot_of(i, j), leaves // 4)
                w = jnp.where(lanes(tile) // NODE == 2 * q + across, strength(k, i, j), w)
            edge_weights.append((axis, way, m, box, w))
    for axis, way in sides:

        @pl.when(has[axis, way])
        def _(axis=axis, way=way):
            halo_copy(axis, -way).wait_recv()

    edges = [None] * (leaves // 4)
    for axis, way, m, box, w in edge_weights:
        arrived = (halo_x if axis == "gx" else halo_y)[1 if way < 0 else 0].astype(F32)
        term = w * arrived[m * T : m * T + T]
        edges[box] = term if edges[box] is None else edges[box] + term
    edges = jnp.concatenate([jnp.zeros(tile, F32) if x is None else x for x in edges], axis=0)
    edges = jnp.concatenate(split(edges), axis=1)
    wide = dot(edges, up_edge[...])
    current_16 = inner_16[...] + wide[:, :128] + wide[:, 128:]
    current_4 = narrow(rows_to_lanes(current_16, 4), up_low[...])
    current = narrow(rows_to_lanes(current_4, 4), up_high[...])

    joined = lambda x: rows_to_lanes(x, 2)
    level = 4
    path = []
    for number, stage in enumerate(stages):
        pool, stage_send, stage_recv = stage_refs[3 * number : 3 * number + 3]
        own_slot = jnp.int32(0)
        for axis, bit in stage:
            own_slot = own_slot * 2 + bit_of(axis, bit)
        pool[own_slot] = current
        final = number == len(stages) - 1
        copies = [] if final else [
            pltpu.make_async_remote_copy(
                src_ref=pool.at[own_slot],
                dst_ref=pool.at[own_slot],
                send_sem=stage_send.at[mask],
                recv_sem=stage_recv.at[mask],
                device_id=partner(stage, mask),
                device_id_type=MESH,
            )
            for mask in range(1, 1 << len(stage))
        ]
        for copy in reversed(copies):
            copy.start()
        if final:

            @pl.when(rank < slots - 1)
            def _():
                pl.semaphore_wait(here, slots - 1 - rank)


            for other in range(slots):

                @pl.when(rank != other)
                def _(other=other):
                    pltpu.make_async_remote_copy(
                        src_ref=pool.at[own_slot],
                        dst_ref=pool.at[own_slot],
                        send_sem=stage_send.at[0],
                        recv_sem=stage_recv.at[0],
                        device_id=ranked(other),
                        device_id_type=MESH,
                    ).start()

            every = pltpu.make_async_remote_copy(
                src_ref=pool.at[pl.ds(0, slots - 1)],
                dst_ref=pool.at[pl.ds(0, slots - 1)],
                send_sem=stage_send.at[0],
                recv_sem=stage_recv.at[0],
                device_id=partner(stage, 1),
                device_id_type=MESH,
            )
        if number == 0:

            @pl.when(jnp.logical_not(early))
            def _():
                prepare_down()

            for name in ("leaf_solve", "sibling_first", "sibling_second"):
                loads[name].wait()
            turned = [jnp.concatenate([edge_points(q)] * 2, axis=0) for q in range(4)]
            of_quarter = lambda q: jnp.concatenate(
                [edges[:, k + q * 32 : k + q * 32 + 32] for k in (0, 128)], axis=1
            )
            forcing = jnp.concatenate(
                [
                    force[q * 128 : (q + 1) * 128, :] + dot(of_quarter(q), turned[q])
                    for q in range(4)
                ],
                axis=0,
            )
            sibling = lambda k: split(v["sibling_rest"][k])
            is_left = lambda x: left_half(x.shape)

            def gathered(x):
                middle = x.shape[0] // 2
                return jnp.where(is_left(x[:middle]), x[:middle], x[middle:])

            cat_0 = gathered(product(forcing, split(twice(v["leaf_skeleton"][...], 0).T)))
            cat_1 = gathered(product(cat_0, split(twice(v["merge_first"][...], 0).T)))
            cats = [joined(current_16)]
            cats.append(joined(product(cats[0], split(merge(0)))))
            cats.append(joined(current_4))
            cats.append(joined(product(cats[2], split(merge(2)))))
            own_part = product(cats[3], sibling(3))
            for k in (2, 1, 0):
                own_part = product(lanes_to_rows(own_part), split(parent(k)))
                own_part = own_part + product(cats[k], sibling(k))
            own_part = product(lanes_to_rows(own_part), split(v["parent_second"][...]))
            own_part = own_part + product(cat_1, split(v["sibling_second"][...]))
            own_part = spread_product(own_part, split(v["parent_first"][...]))
            own_part = own_part + product(cat_0, split(v["sibling_first"][...]))
            own_part = spread_product(own_part, split(v["leaf_lift"][...]))
            solved[...] = own_part + product(forcing, split(v["leaf_solve"][...]))
        if final:
            known = jnp.zeros((T, 128), F32)
            chain = chained() if path else ()
            for k, term in enumerate(path):
                term = own_half(k, term)
                known = known + (product(term, split(chain[k - 1])) if k > 0 else term)
        if final:
            for axis, way in sides:

                @pl.when(has[axis, way])
                def _(axis=axis, way=way):
                    halo_copy(axis, way).wait_send()

            every.wait_recv()
            break
        for copy in copies:
            copy.wait()
        current = pool[...].reshape(T << len(stage), 128)
        for k, (axis, bit) in enumerate(stage):
            cat = joined(current)
            mine = cat
            for later_axis, later_bit in stage[k + 1 :]:
                middle = mine.shape[0] // 2
                mine = jnp.where(bit_of(later_axis, later_bit) == 1, mine[middle:], mine[:middle])
            path.append(product(mine, split(v["sibling_rest"][level])))
            current = product(cat, split(merge(level)))
            level += 1

    everyone = pool[...].reshape(slots * T, 128)
    merged = narrow(rows_to_lanes(everyone, slots // groups), up_cross[...])
    mine = jnp.int32(0)
    for k in folds:
        mine = mine * 2 + bits[k]
    slabs = [rows_to_lanes(merged, groups)]
    slabs += [pool[k * groups + mine] for k in range(slots // groups)]
    boundary = narrow(jnp.concatenate(slabs, axis=1), fold[...]) + known
    boundary = lanes_to_rows(broad(boundary, down_high[...]))
    boundary = lanes_to_rows(broad(boundary, down_low[...]))
    high, low = split(boundary)
    both = twice(high, 1)
    for q in range(4):
        cut = slice(q * SQUARE, (q + 1) * SQUARE)
        lifted = dot(both, down_leaf[:, cut]) + dot(low, down_leaf[:128, cut])
        for spot, i, j in grid[q * leaves // 4 : (q + 1) * leaves // 4]:
            inside = spot * T - q * rows // 4
            for h in range(2):
                one = lifted[inside : inside + T, h * half : (h + 1) * half]
                one = one + solved[spot * T : spot * T + T, h * half : (h + 1) * half]
                field[by_tracer(i, j, h), :] = one
    updated = jnp.concatenate([field[:rows, :], field[rows:, :]], axis=1)
    out_ref[...] = updated.reshape(out_ref.shape).astype(out_ref.dtype)
    every.wait_send()


def local(tables, count_first, count_second, tracers, *operands):
    T, L = tracers.shape[0], tracers.shape[1]
    assert L == 8 and local_plan(L) == [1, 2] * 3
    stages = staged(cross_plan(count_first, count_second))
    rows = T * L * L
    args = [tracers, operands[0], operands[1], tables] + list(operands[2:])
    args[5], args[7] = args[5].T, args[7].T
    vmem, dma = pltpu.VMEM, pltpu.SemaphoreType.DMA
    scratch = [vmem(a.shape, a.dtype) for a in args]
    slots = 1 << len(stages[-1])
    groups = 1 << FOLDED
    scratch += [
        dma((len(args),)),
        vmem((2 * rows, 128), F32),
        vmem((rows, 2 * SQUARE), F32),
        vmem((6, L * L, 128), F32),
        vmem((rows, SQUARE), F32),
        vmem((rows, SQUARE), F32),
        vmem((4 * SQUARE, 256), BF16),
        vmem((512, 256), BF16),
        vmem((512, 256), BF16),
        vmem((slots // groups * 128, 256), BF16),
        vmem(((groups + slots // groups) * 128, 256), BF16),
        vmem((256, 512), BF16),
        vmem((256, 512), BF16),
        vmem((256, 4 * SQUARE), BF16),
        vmem((2, T * L // 2, 128), BF16),
        vmem((2, T * L // 2, 128), BF16),
        vmem((2, T * L // 2, 128), BF16),
        vmem((2, T * L // 2, 128), BF16),
        dma((4,)),
        dma((4,)),
        pltpu.SemaphoreType.REGULAR,
        vmem((256, 256), BF16),
        vmem((T * L * L // 4, 128), F32),
    ]
    for stage in stages:
        slots = 1 << len(stage)
        scratch += [vmem((slots, T, 128), F32), dma((slots,)), dma((slots,))]
    return pl.pallas_call(
        functools.partial(kernel, stages, L, T),
        out_shape=jax.ShapeDtypeStruct(tracers.shape, tracers.dtype),
        in_specs=[pl.BlockSpec(memory_space=pl.ANY)] * len(args),
        out_specs=pl.BlockSpec(memory_space=pltpu.VMEM),
        scratch_shapes=scratch,
        compiler_params=pltpu.CompilerParams(
            collective_id=0, has_side_effects=True, vmem_limit_bytes=VMEM_LIMIT
        ),
    )(*[pltpu.with_memory_space_constraint(a, pltpu.HBM) for a in args])


def solution(mesh):
    tables = point_tables()
    split_both = P(None, "gx", "gy")
    in_specs = (P(None, "gx", "gy", None), split_both, split_both) + (P(),) * 13

    def body(*args):
        return local(
            jnp.asarray(tables), mesh.shape["gx"], mesh.shape["gy"], *args
        )

    return jax.shard_map(
        body,
        mesh=mesh,
        in_specs=in_specs,
        out_specs=P(None, "gx", "gy", None),
        check_vma=False,
    )
```

```python
import functools

import jax
import jax.numpy as jnp
import numpy as np
from jax import lax
from jax.experimental import pallas as pl
from jax.experimental.pallas import tpu as pltpu
from jax.sharding import PartitionSpec as P

NODE = 16
SQUARE = NODE * NODE
F32 = jnp.float32
BF16 = jnp.bfloat16
VMEM_LIMIT = 32 * 1024 * 1024
MESH = pl.DeviceIdType.MESH
LAST_STAGE = 5
FOLDED = 3


def local_plan(leaf_side):
    merge_plan = []
    block_span = leaf_side
    while block_span > 1:
        merge_plan = merge_plan + [1, 2]
        block_span = block_span // 2
    return merge_plan


def cross_plan(count_first, count_second):
    merge_plan = []
    bits = {"gx": 0, "gy": 0}
    while count_first * count_second > 1:
        if count_first >= count_second:
            axis, count_first = "gx", count_first // 2
        else:
            axis, count_second = "gy", count_second // 2
        merge_plan.append((axis, bits[axis]))
        bits[axis] += 1
    return merge_plan


def staged(plan):
    stages, rest = [], list(plan)
    while len(rest) > LAST_STAGE:
        size = min(3, len(rest) - LAST_STAGE)
        stages.append(rest[:size])
        rest = rest[size:]
    return stages + [rest]


def point_tables():
    index = np.arange(NODE)
    points = -np.cos(np.pi * index / (NODE - 1))
    weights = np.where(index % 2 == 0, 1.0, -1.0)
    weights[[0, NODE - 1]] *= 2.0
    eye = np.eye(NODE)
    matrix = weights[:, None] / weights[None, :] / (points[:, None] - points[None, :] + eye)
    matrix = matrix * (1.0 - eye)
    matrix = matrix - np.diag(matrix.sum(axis=1))
    both = np.concatenate([np.kron(matrix, eye).T, np.kron(eye, matrix).T], axis=1)
    both = both.astype(np.float32)
    high = both.astype(jnp.bfloat16)
    low = (both - high.astype(np.float32)).astype(jnp.bfloat16)
    facing = np.zeros((SQUARE, 2 * SQUARE), np.float32)
    last = NODE - 1
    for k in range(NODE):
        facing[last * NODE + k, k] = 1.0
        facing[k, last * NODE + k] = 1.0
        facing[k * NODE + last, SQUARE + k * NODE] = 1.0
        facing[k * NODE, SQUARE + k * NODE + last] = 1.0
    packed = np.zeros((SQUARE, SQUARE // 2), np.float32)
    for q in range(4):
        for k in range(NODE):
            packed[(0 if q // 2 else last) * NODE + k, q * 2 * NODE + k] = 1.0
            packed[k * NODE + (0 if q % 2 else last), (q * 2 + 1) * NODE + k] = 1.0
    return np.concatenate([high, low, *(x.astype(jnp.bfloat16) for x in (facing, packed))], axis=1)


def split(x):
    high = x.astype(BF16)
    return high, (x - high.astype(F32)).astype(BF16)


def dot(left, right):
    return jnp.dot(left, right, preferred_element_type=F32)


def product(x, weight):
    high, low = weight
    rows, depth = x.shape
    wide = high.shape[1]
    if rows < 64:
        rest = x - x.astype(BF16).astype(F32)
        both = jnp.concatenate([x, rest], axis=0).astype(BF16)
        if depth == 128:
            both = jnp.concatenate([both, both], axis=1)
            out = dot(both, jnp.concatenate([high, low], axis=0))
        else:
            out = dot(both, high) + dot(both, low)
        return out[:rows] + out[rows:]
    x_high, x_low = split(x)
    if wide == 128:
        weights = jnp.concatenate([high, low], axis=1)
        if depth == 128:
            weights = jnp.concatenate([weights, weights], axis=0)
            out = dot(jnp.concatenate([x_high, x_low], axis=1), weights)
            return out[:, :128] + out[:, 128:]
        out = dot(x_high, weights)
        return out[:, :128] + dot(x_low, high) + out[:, 128:]
    if depth == 128:
        out = dot(jnp.concatenate([x_high, x_high], axis=1), jnp.concatenate([high, low], axis=0))
        return out + dot(x_low, high)
    return dot(x_high, high) + dot(x_low, high) + dot(x_high, low)


def spread_product(x, weight):
    high, low = split(x)
    moved = pltpu.roll(x - high.astype(F32), 64, 1).astype(BF16)
    is_left = left_half(x.shape)
    zero = jnp.zeros_like(high)
    first = [jnp.where(is_left, high, moved), jnp.where(is_left, high, zero)]
    second = [jnp.where(is_left, moved, high), jnp.where(is_left, zero, high)]
    both = jnp.concatenate([jnp.concatenate(k, axis=1) for k in (first, second)], axis=0)
    return dot(both, jnp.concatenate([weight[0]] * 2 + [weight[1]] * 2, axis=0))


def lanes(shape):
    return lax.broadcasted_iota(jnp.int32, shape, len(shape) - 1)


def left_half(shape):
    return lanes(shape) < shape[-1] // 2


def narrow(x, table):
    rows = x.shape[0]
    rest = x - x.astype(BF16).astype(F32)
    out = dot(jnp.concatenate([x, rest], axis=0).astype(BF16), table)
    out = out[:rows] + out[rows:]
    return out[:, :128] + out[:, 128:]


def broad(x, table):
    rows = x.shape[0]
    rest = x - x.astype(BF16).astype(F32)
    both = jnp.concatenate([x, rest], axis=0).astype(BF16)
    out = dot(jnp.concatenate([both, both], axis=1), table)
    return out[:rows] + out[rows:]


def rows_to_lanes(x, count):
    size = x.shape[0] // count
    return jnp.concatenate([x[k * size : (k + 1) * size] for k in range(count)], axis=1)


def lanes_to_rows(x):
    return jnp.concatenate([x[:, k : k + 128] for k in range(0, x.shape[1], 128)], axis=0)


def quarters(x):
    return [x[:128, :128], x[:128, 128:], x[128:, :128], x[128:, 128:]]


def merge_pair(former, latter):
    wide = product(former, split(rows_to_lanes(latter, 2)))
    return jnp.concatenate(quarters(wide), axis=0)


def parent_pair(upper, lower):
    a, b, c, d = quarters(product(lanes_to_rows(upper), split(lower)))
    return jnp.concatenate([a, c, b, d], axis=1)


def wide_split(x):
    return jnp.concatenate(split(x), axis=1)


def tall_split(x):
    return jnp.concatenate(split(x), axis=0)


def kernel(stages, leaf_side, tracer_count, *refs):
    names = ["u", "velocity", "inflow", "tables", "leaf_solve", "leaf_skeleton", "leaf_lift"]
    names += [a + "_" + b for a in ("merge", "parent", "sibling") for b in ("first", "second", "rest")]
    names += ["root_map"]
    hbm = dict(zip(names, refs[: len(names)]))
    out_ref = refs[len(names)]
    rest = refs[len(names) + 1 :]
    v = dict(zip(names, rest[: len(names)]))
    (
        load_sem, field, near, coef, force, solved,
        up_leaf, up_low, up_high, up_cross, fold, down_high, down_low, down_leaf,
        send_x, send_y, halo_x, halo_y, halo_send, halo_recv, here, up_edge, inner_16,
    ) = rest[len(names) : len(names) + 23]
    stage_refs = rest[len(names) + 23 :]
    T, L = tracer_count, leaf_side
    leaves = L * L
    rows = T * leaves
    half = SQUARE // 2

    loads = {}
    for k, name in enumerate(names):
        loads[name] = pltpu.make_async_copy(hbm[name], v[name], load_sem.at[k])
    order = ["u", "tables", "velocity", "inflow", "leaf_skeleton", "merge_first", "merge_second"]
    order += ["merge_rest", "parent_rest", "sibling_rest", "root_map", "parent_second", "parent_first"]
    order += ["leaf_lift", "leaf_solve", "sibling_first", "sibling_second"]

    for name in order[:2]:
        loads[name].start()

    place = {"gx": lax.axis_index("gx"), "gy": lax.axis_index("gy")}
    count = {"gx": lax.axis_size("gx"), "gy": lax.axis_size("gy")}
    bit_of = lambda axis, bit: lax.rem(place[axis] // (1 << bit), 2)

    def partner(stage, mask):
        target = dict(place)
        for k, (axis, bit) in enumerate(stage):
            if mask >> (len(stage) - 1 - k) & 1:
                target[axis] = target[axis] + (1 - 2 * bit_of(axis, bit)) * (1 << bit)
        return (target["gx"], target["gy"])

    barrier = pltpu.get_barrier_semaphore()
    expected = jnp.int32(0)
    has, beside = {}, {}
    for axis in ("gx", "gy"):
        for way in (-1, 1):
            spot = dict(place)
            spot[axis] = spot[axis] + way
            beside[axis, way] = (spot["gx"], spot["gy"])
            has[axis, way] = place[axis] > 0 if way < 0 else place[axis] < count[axis] - 1

            @pl.when(has[axis, way])
            def _(axis=axis, way=way):
                pl.semaphore_signal(barrier, inc=1, device_id=beside[axis, way], device_id_type=MESH)

            expected = expected + jnp.where(has[axis, way], 1, 0)
    for stage in stages[:-1]:
        for mask in range(1, 1 << len(stage)):
            pl.semaphore_signal(barrier, inc=1, device_id=partner(stage, mask), device_id_type=MESH)
            expected = expected + 1

    by_rank = sorted(stages[-1], key=lambda e: (e == ("gx", 0), e[0] == "gy", -e[1]))
    slots = 1 << len(by_rank)
    rank = jnp.int32(0)
    for axis, bit in by_rank:
        rank = rank * 2 + bit_of(axis, bit)

    cleared = dict(place)
    for axis, bit in by_rank:
        cleared[axis] = cleared[axis] - bit_of(axis, bit) * (1 << bit)

    def ranked(number):
        target = dict(cleared)
        for k, (axis, bit) in enumerate(reversed(by_rank)):
            target[axis] = target[axis] + (number >> k & 1) * (1 << bit)
        return (target["gx"], target["gy"])

    def greet(number):
        @pl.when(rank < number)
        def _():
            pl.semaphore_signal(barrier, inc=1, device_id=ranked(number), device_id_type=MESH)

    def answer(number):
        @pl.when(rank > number)
        def _():
            pl.semaphore_signal(here, inc=1, device_id=ranked(number), device_id_type=MESH)

    expected = expected + rank

    for number in reversed(range(slots)):
        greet(number)

    for name in order[2:8]:
        loads[name].start()

    def spot_of(i, j):
        return sum(
            ((i >> b & 1) << (5 - 2 * b)) + ((j >> b & 1) << (4 - 2 * b)) for b in range(3)
        )

    grid = sorted((spot_of(i, j), i, j) for i in range(L) for j in range(L))
    block = lambda i, j: slice(spot_of(i, j) * T, spot_of(i, j) * T + T)
    by_tracer = lambda i, j, h: pl.ds(h * rows + i * L + j, T, stride=leaves)

    loads["u"].wait()
    plain = v["u"][...].astype(F32).reshape(rows, SQUARE)
    for h in range(2):
        field[h * rows : (h + 1) * rows, :] = plain[:, h * half : (h + 1) * half]

    def of_leaves(spots):
        return jnp.concatenate(
            [
                jnp.concatenate([field[by_tracer(i, j, h), :] for i, j in spots], axis=0)
                for h in range(2)
            ],
            axis=1,
        )

    side = lambda axis, k: [(k, m) if axis == "gx" else (m, k) for m in range(L)]
    borders = [(axis, k) for axis in ("gx", "gy") for k in range(2)]
    spots = [side(axis, k * (L - 1)) for axis, k in borders]
    border = of_leaves([x for line in spots for x in line[::2] + line[1::2]]).astype(BF16)
    loads["tables"].wait()
    border = dot(border, v["tables"][:, 6 * SQUARE :])
    for number, (axis, k) in enumerate(borders):
        low = number * T * L
        even = border[low : low + T * L // 2]
        odd = border[low + T * L // 2 : low + T * L]
        strip = lanes(even.shape) // (2 * NODE if axis == "gx" else 4 * NODE) % 2
        target = send_x if axis == "gx" else send_y
        target[k] = jnp.where(strip == 0, even, odd).astype(BF16)

    def halo_copy(axis, way):
        k = 0 if way < 0 else 1
        source, target = (send_x, halo_x) if axis == "gx" else (send_y, halo_y)
        slot = k + (0 if axis == "gx" else 2)
        return pltpu.make_async_remote_copy(
            src_ref=source.at[k],
            dst_ref=target.at[k],
            send_sem=halo_send.at[slot],
            recv_sem=halo_recv.at[slot],
            device_id=beside[axis, way],
            device_id_type=MESH,
        )

    sides = [("gy", -1), ("gy", 1), ("gx", -1), ("gx", 1)]
    plan = [entry for stage in stages for entry in stage]
    bits = [bit_of(axis, bit) for axis, bit in plan]
    own_half = lambda k, w: jnp.where(bits[k] == 1, w[:, 128:], w[:, :128])
    twice = lambda w, axis: jnp.concatenate([w, w], axis=axis)
    merge = lambda k: v["merge_rest"][k]
    parent = lambda k: v["parent_rest"][k]

    own_parent = lambda k: own_half(k, parent(4 + k))

    def chained():
        chain = [own_parent(0)]
        for k in range(1, len(plan)):
            step = own_parent(k)
            if k > 1:
                step = product(step, split(own_parent(k - 1)))
            chain.append(product(step, split(chain[max(k - 2, 0)])))
        return chain

    def folded(levels, top, siblings, chain=()):
        weights = top
        for k in reversed(levels):
            groups = 1 << (levels[-1] - k)
            if weights is not None:
                weights = product(merge(4 + k), split(weights))
            elif siblings:
                weights = jnp.zeros((256, 128), F32)
            else:
                weights = merge(4 + k)
            blocks = [weights[:, g * 128 : (g + 1) * 128] for g in range(groups)]
            if siblings:
                sibling = own_half(k, v["sibling_rest"][4 + k])
                if k > 0:
                    sibling = product(sibling, split(chain[k - 1]))
                mine = jnp.int32(0)
                for later in levels:
                    if later > k:
                        mine = mine + bits[later] * (1 << (levels[-1] - later))
                blocks = [x + jnp.where(mine == g, sibling, 0.0) for g, x in enumerate(blocks)]
            weights = jnp.concatenate([x[:128] for x in blocks] + [x[128:] for x in blocks], axis=1)
        return lanes_to_rows(weights)

    first = len(plan) - len(stages[-1])
    last_levels = list(range(first, len(plan)))
    direct, folds = last_levels[: -FOLDED], last_levels[-FOLDED:]
    assert len(direct) == 2
    groups = 1 << len(folds)

    def edge_points(q):
        shape = (2 * NODE, SQUARE)
        k = lax.broadcasted_iota(jnp.int32, shape, 0)
        first = k + (SQUARE - NODE if q // 2 else 0)
        second = (k - NODE) * NODE + (NODE - 1 if q % 2 else 0)
        return jnp.where(lanes(shape) == jnp.where(k < NODE, first, second), 1.0, 0.0).astype(BF16)

    def prepare_up():
        for name in ("leaf_skeleton", "merge_first", "merge_second", "merge_rest"):
            loads[name].wait()
        two = [
            product(v["merge_first"][...].T, split(v["merge_second"][d * 64 : (d + 1) * 64, :]))
            for d in range(2)
        ]
        four = jnp.concatenate([two[d][c * 64 : (c + 1) * 64] for c in range(2) for d in range(2)], axis=1)
        up_leaf[...] = wide_split(lanes_to_rows(product(v["leaf_skeleton"][...].T, split(four))))
        at_edges = [
            dot(edge_points(q), up_leaf[q * SQUARE : (q + 1) * SQUARE, :]) for q in range(4)
        ]
        up_edge[...] = jnp.concatenate(at_edges * 2, axis=0).astype(BF16)
        up_low[...] = wide_split(merge_pair(merge(0), merge(1)))
        up_high[...] = wide_split(merge_pair(merge(2), merge(3)))


    def prepare_down():
        up_cross[...] = wide_split(folded(direct, None, False))
        for name in ("parent_rest", "sibling_rest", "root_map"):
            loads[name].wait()
        chain = chained()
        top = product(product(v["root_map"][...], split(own_parent(len(plan) - 1))), split(chain[-2]))
        fold[: groups * 128, :] = wide_split(folded(folds, top, True, chain))
        fold[groups * 128 :, :] = wide_split(folded(direct, None, True, chain))
        down_high[...] = tall_split(parent_pair(parent(3), parent(2)))
        down_low[...] = tall_split(parent_pair(parent(1), parent(0)))
        for name in ("parent_second", "parent_first", "leaf_lift"):
            loads[name].wait()
        halves = lambda x: jnp.concatenate([x, pltpu.roll(x, 64, 1)], axis=0)[:, :64]
        lifts = product(halves(v["parent_first"][...]), split(v["leaf_lift"][...]))
        lifts = jnp.concatenate([lifts[:64], lifts[64:]], axis=1)
        lifts = product(halves(v["parent_second"][...]), split(lifts))
        down_leaf[...] = tall_split(
            jnp.concatenate(
                [
                    lifts[d * 128 : (d + 1) * 128, c * SQUARE : (c + 1) * SQUARE]
                    for c in range(2)
                    for d in range(2)
                ],
                axis=1,
            )
        )

    own = lax.broadcasted_iota(jnp.int32, (leaves, L), 0) % L == lanes((leaves, L))

    def column(values):
        wide = jnp.concatenate(
            [jnp.broadcast_to(values[i : i + 1, :], (L, L)) for i in range(L)], axis=0
        )
        return jnp.sum(jnp.where(own, wide, 0.0), axis=1, keepdims=True)

    tile = (T, half)
    on_0, on_1 = lanes(tile) < NODE, lanes(tile) >= half - NODE
    on_2, on_3 = lanes(tile) % NODE == 0, lanes(tile) % NODE == NODE - 1
    at_leaf = lambda k, i, j: jnp.broadcast_to(coef[k, i * L + j : i * L + j + 1, :], tile)
    keep_if = lambda mask, x: jnp.where(mask, x, 0.0)
    strength = lambda s, i, j: at_leaf(2 + s, i, j)


    def interior():
        whole = of_leaves([(i, j) for _, i, j in grid])
        force[...] = whole
        whole = whole.astype(BF16)
        near[...] = dot(whole, v["tables"][:, 4 * SQUARE : 6 * SQUARE])
        loads["velocity"].wait()
        loads["inflow"].wait()
        speed = [v["velocity"][k] for k in range(2)]
        columns = [column(x) for x in speed]
        columns += [
            column(v["inflow"][s].astype(F32) * (NODE * jnp.abs(speed[s // 2]))) for s in range(4)
        ]
        for k, x in enumerate(columns):
            coef[k] = jnp.broadcast_to(x, (leaves, half))

        for q in range(4):
            low, top = q * rows // 4, (q + 1) * rows // 4
            u = force[low:top, :]
            part = u.astype(BF16)
            grads = dot(part, v["tables"][:, : 2 * SQUARE])
            grads = grads + dot(part, v["tables"][:, 2 * SQUARE : 4 * SQUARE])
            for spot, i, j in grid[q * leaves // 4 : (q + 1) * leaves // 4]:
                at = slice(spot * T, spot * T + T)
                inside = slice(spot * T - low, spot * T + T - low)
                speeds = [at_leaf(k, i, j) for k in range(2)]
                w = [strength(s, i, j) for s in range(4)]
                w_2, w_3 = keep_if(on_2, w[2]), keep_if(on_3, w[3])
                for c in range(2):
                    cut = slice(c * half, (c + 1) * half)
                    far = slice((2 + c) * half, (3 + c) * half)
                    total = u[inside, cut] * (1.0 - (keep_if((on_0, on_1)[c], w[c]) + w_2 + w_3))
                    total = total - speeds[0] * grads[inside, cut] - speeds[1] * grads[inside, far]
                    ahead = i - 1 if c == 0 else i + 1
                    if 0 <= ahead < L:
                        total = total + w[c] * near[block(ahead, j), cut]
                    if j > 0:
                        total = total + w_2 * near[block(i, j - 1), far]
                    if j < L - 1:
                        total = total + w_3 * near[block(i, j + 1), far]
                    force[at, cut] = total


    for axis, way in sides:
        slot = 1 if way < 0 else 0

        @pl.when(jnp.logical_not(has[axis, way]))
        def _(axis=axis, slot=slot):
            target = halo_x if axis == "gx" else halo_y
            target[slot] = jnp.zeros_like(target[slot])

    def announce():
        pl.semaphore_wait(barrier, expected)
        for axis, way in sides:

            @pl.when(has[axis, way])
            def _(axis=axis, way=way):
                halo_copy(axis, way).start()

        for number in range(slots):
            answer(number)

    announce()
    prepare_up()
    interior()
    high, low = split(rows_to_lanes(force[...], 4))
    wide = dot(high, up_leaf[...])
    inner_16[...] = wide[:, :128] + wide[:, 128:] + dot(low, up_leaf[:, :128])
    for name in order[8:]:
        loads[name].start()
    early = rank < slots // 16

    @pl.when(early)
    def _():
        prepare_down()


    edge_weights = []
    for axis, way in sides:
        across = 0 if axis == "gx" else 1
        k = 2 * across + (0 if way < 0 else 1)
        spots = side(axis, 0 if way < 0 else L - 1)
        for m in range(L // 2):
            w = jnp.zeros(tile, F32)
            for i, j in spots[2 * m : 2 * m + 2]:
                q, box = divmod(spot_of(i, j), leaves // 4)
                w = jnp.where(lanes(tile) // NODE == 2 * q + across, strength(k, i, j), w)
            edge_weights.append((axis, way, m, box, w))
    for axis, way in sides:

        @pl.when(has[axis, way])
        def _(axis=axis, way=way):
            halo_copy(axis, -way).wait_recv()

    edges = [None] * (leaves // 4)
    for axis, way, m, box, w in edge_weights:
        arrived = (halo_x if axis == "gx" else halo_y)[1 if way < 0 else 0].astype(F32)
        term = w * arrived[m * T : m * T + T]
        edges[box] = term if edges[box] is None else edges[box] + term
    edges = jnp.concatenate([jnp.zeros(tile, F32) if x is None else x for x in edges], axis=0)
    edges = jnp.concatenate(split(edges), axis=1)
    wide = dot(edges, up_edge[...])
    current_16 = inner_16[...] + wide[:, :128] + wide[:, 128:]
    current_4 = narrow(rows_to_lanes(current_16, 4), up_low[...])
    current = narrow(rows_to_lanes(current_4, 4), up_high[...])

    joined = lambda x: rows_to_lanes(x, 2)
    level = 4
    path = []
    for number, stage in enumerate(stages):
        pool, stage_send, stage_recv = stage_refs[3 * number : 3 * number + 3]
        own_slot = jnp.int32(0)
        for axis, bit in stage:
            own_slot = own_slot * 2 + bit_of(axis, bit)
        pool[own_slot] = current
        final = number == len(stages) - 1
        copies = [] if final else [
            pltpu.make_async_remote_copy(
                src_ref=pool.at[own_slot],
                dst_ref=pool.at[own_slot],
                send_sem=stage_send.at[mask],
                recv_sem=stage_recv.at[mask],
                device_id=partner(stage, mask),
                device_id_type=MESH,
            )
            for mask in range(1, 1 << len(stage))
        ]
        for copy in reversed(copies):
            copy.start()
        if final:

            @pl.when(rank < slots - 1)
            def _():
                pl.semaphore_wait(here, slots - 1 - rank)


            for other in range(slots):

                @pl.when(rank != other)
                def _(other=other):
                    pltpu.make_async_remote_copy(
                        src_ref=pool.at[own_slot],
                        dst_ref=pool.at[own_slot],
                        send_sem=stage_send.at[0],
                        recv_sem=stage_recv.at[0],
                        device_id=ranked(other),
                        device_id_type=MESH,
                    ).start()

            every = pltpu.make_async_remote_copy(
                src_ref=pool.at[pl.ds(0, slots - 1)],
                dst_ref=pool.at[pl.ds(0, slots - 1)],
                send_sem=stage_send.at[0],
                recv_sem=stage_recv.at[0],
                device_id=partner(stage, 1),
                device_id_type=MESH,
            )
        if number == 0:

            @pl.when(jnp.logical_not(early))
            def _():
                prepare_down()

            for name in ("leaf_solve", "sibling_first", "sibling_second"):
                loads[name].wait()
            turned = [jnp.concatenate([edge_points(q)] * 2, axis=0) for q in range(4)]
            of_quarter = lambda q: jnp.concatenate(
                [edges[:, k + q * 32 : k + q * 32 + 32] for k in (0, 128)], axis=1
            )
            forcing = jnp.concatenate(
                [
                    force[q * 128 : (q + 1) * 128, :] + dot(of_quarter(q), turned[q])
                    for q in range(4)
                ],
                axis=0,
            )
            sibling = lambda k: split(v["sibling_rest"][k])
            is_left = lambda x: left_half(x.shape)

            def gathered(x):
                middle = x.shape[0] // 2
                return jnp.where(is_left(x[:middle]), x[:middle], x[middle:])

            cat_0 = gathered(product(forcing, split(twice(v["leaf_skeleton"][...], 0).T)))
            cat_1 = gathered(product(cat_0, split(twice(v["merge_first"][...], 0).T)))
            cats = [joined(current_16)]
            cats.append(joined(product(cats[0], split(merge(0)))))
            cats.append(joined(current_4))
            cats.append(joined(product(cats[2], split(merge(2)))))
            own_part = product(cats[3], sibling(3))
            for k in (2, 1, 0):
                own_part = product(lanes_to_rows(own_part), split(parent(k)))
                own_part = own_part + product(cats[k], sibling(k))
            own_part = product(lanes_to_rows(own_part), split(v["parent_second"][...]))
            own_part = own_part + product(cat_1, split(v["sibling_second"][...]))
            own_part = spread_product(own_part, split(v["parent_first"][...]))
            own_part = own_part + product(cat_0, split(v["sibling_first"][...]))
            own_part = spread_product(own_part, split(v["leaf_lift"][...]))
            solved[...] = own_part + product(forcing, split(v["leaf_solve"][...]))
        if final:
            known = jnp.zeros((T, 128), F32)
            chain = chained() if path else ()
            for k, term in enumerate(path):
                term = own_half(k, term)
                known = known + (product(term, split(chain[k - 1])) if k > 0 else term)
        if final:
            for axis, way in sides:

                @pl.when(has[axis, way])
                def _(axis=axis, way=way):
                    halo_copy(axis, way).wait_send()

            every.wait_recv()
            break
        for copy in copies:
            copy.wait()
        current = pool[...].reshape(T << len(stage), 128)
        for k, (axis, bit) in enumerate(stage):
            cat = joined(current)
            mine = cat
            for later_axis, later_bit in stage[k + 1 :]:
                middle = mine.shape[0] // 2
                mine = jnp.where(bit_of(later_axis, later_bit) == 1, mine[middle:], mine[:middle])
            path.append(product(mine, split(v["sibling_rest"][level])))
            current = product(cat, split(merge(level)))
            level += 1

    everyone = pool[...].reshape(slots * T, 128)
    merged = narrow(rows_to_lanes(everyone, slots // groups), up_cross[...])
    mine = jnp.int32(0)
    for k in folds:
        mine = mine * 2 + bits[k]
    slabs = [rows_to_lanes(merged, groups)]
    slabs += [pool[k * groups + mine] for k in range(slots // groups)]
    boundary = narrow(jnp.concatenate(slabs, axis=1), fold[...]) + known
    boundary = lanes_to_rows(broad(boundary, down_high[...]))
    boundary = lanes_to_rows(broad(boundary, down_low[...]))
    high, low = split(boundary)
    both = twice(high, 1)
    for q in range(4):
        cut = slice(q * SQUARE, (q + 1) * SQUARE)
        lifted = dot(both, down_leaf[:, cut]) + dot(low, down_leaf[:128, cut])
        for spot, i, j in grid[q * leaves // 4 : (q + 1) * leaves // 4]:
            inside = spot * T - q * rows // 4
            for h in range(2):
                one = lifted[inside : inside + T, h * half : (h + 1) * half]
                one = one + solved[spot * T : spot * T + T, h * half : (h + 1) * half]
                field[by_tracer(i, j, h), :] = one
    updated = jnp.concatenate([field[:rows, :], field[rows:, :]], axis=1)
    out_ref[...] = updated.reshape(out_ref.shape).astype(out_ref.dtype)
    every.wait_send()


def local(tables, count_first, count_second, tracers, *operands):
    T, L = tracers.shape[0], tracers.shape[1]
    assert L == 8 and local_plan(L) == [1, 2] * 3
    stages = staged(cross_plan(count_first, count_second))
    rows = T * L * L
    args = [tracers, operands[0], operands[1], tables] + list(operands[2:])
    args[5], args[7] = args[5].T, args[7].T
    vmem, dma = pltpu.VMEM, pltpu.SemaphoreType.DMA
    scratch = [vmem(a.shape, a.dtype) for a in args]
    slots = 1 << len(stages[-1])
    groups = 1 << FOLDED
    scratch += [
        dma((len(args),)),
        vmem((2 * rows, 128), F32),
        vmem((rows, 2 * SQUARE), F32),
        vmem((6, L * L, 128), F32),
        vmem((rows, SQUARE), F32),
        vmem((rows, SQUARE), F32),
        vmem((4 * SQUARE, 256), BF16),
        vmem((512, 256), BF16),
        vmem((512, 256), BF16),
        vmem((slots // groups * 128, 256), BF16),
        vmem(((groups + slots // groups) * 128, 256), BF16),
        vmem((256, 512), BF16),
        vmem((256, 512), BF16),
        vmem((256, 4 * SQUARE), BF16),
        vmem((2, T * L // 2, 128), BF16),
        vmem((2, T * L // 2, 128), BF16),
        vmem((2, T * L // 2, 128), BF16),
        vmem((2, T * L // 2, 128), BF16),
        dma((4,)),
        dma((4,)),
        pltpu.SemaphoreType.REGULAR,
        vmem((256, 256), BF16),
        vmem((T * L * L // 4, 128), F32),
    ]
    for stage in stages:
        slots = 1 << len(stage)
        scratch += [vmem((slots, T, 128), F32), dma((slots,)), dma((slots,))]
    return pl.pallas_call(
        functools.partial(kernel, stages, L, T),
        out_shape=jax.ShapeDtypeStruct(tracers.shape, tracers.dtype),
        in_specs=[pl.BlockSpec(memory_space=pl.ANY)] * len(args),
        out_specs=pl.BlockSpec(memory_space=pltpu.VMEM),
        scratch_shapes=scratch,
        compiler_params=pltpu.CompilerParams(
            collective_id=0, has_side_effects=True, vmem_limit_bytes=VMEM_LIMIT
        ),
    )(*[pltpu.with_memory_space_constraint(a, pltpu.HBM) for a in args])


def solution(mesh):
    tables = point_tables()
    split_both = P(None, "gx", "gy")
    in_specs = (P(None, "gx", "gy", None), split_both, split_both) + (P(),) * 13

    def body(*args):
        return local(
            jnp.asarray(tables), mesh.shape["gx"], mesh.shape["gy"], *args
        )

    return jax.shard_map(
        body,
        mesh=mesh,
        in_specs=in_specs,
        out_specs=P(None, "gx", "gy", None),
        check_vma=False,
    )
```

```python
import functools

import jax
import jax.numpy as jnp
import numpy as np
from jax import lax
from jax.experimental import pallas as pl
from jax.experimental.pallas import tpu as pltpu
from jax.sharding import PartitionSpec as P

NODE = 16
SQUARE = NODE * NODE
F32 = jnp.float32
BF16 = jnp.bfloat16
VMEM_LIMIT = 32 * 1024 * 1024
MESH = pl.DeviceIdType.MESH
LAST_STAGE = 5
FOLDED = 3


def local_plan(leaf_side):
    merge_plan = []
    block_span = leaf_side
    while block_span > 1:
        merge_plan = merge_plan + [1, 2]
        block_span = block_span // 2
    return merge_plan


def cross_plan(count_first, count_second):
    merge_plan = []
    bits = {"gx": 0, "gy": 0}
    while count_first * count_second > 1:
        if count_first >= count_second:
            axis, count_first = "gx", count_first // 2
        else:
            axis, count_second = "gy", count_second // 2
        merge_plan.append((axis, bits[axis]))
        bits[axis] += 1
    return merge_plan


def staged(plan):
    stages, rest = [], list(plan)
    while len(rest) > LAST_STAGE:
        size = min(3, len(rest) - LAST_STAGE)
        stages.append(rest[:size])
        rest = rest[size:]
    return stages + [rest]


def point_tables():
    index = np.arange(NODE)
    points = -np.cos(np.pi * index / (NODE - 1))
    weights = np.where(index % 2 == 0, 1.0, -1.0)
    weights[[0, NODE - 1]] *= 2.0
    eye = np.eye(NODE)
    matrix = weights[:, None] / weights[None, :] / (points[:, None] - points[None, :] + eye)
    matrix = matrix * (1.0 - eye)
    matrix = matrix - np.diag(matrix.sum(axis=1))
    both = np.concatenate([np.kron(matrix, eye).T, np.kron(eye, matrix).T], axis=1)
    both = both.astype(np.float32)
    high = both.astype(jnp.bfloat16)
    low = (both - high.astype(np.float32)).astype(jnp.bfloat16)
    facing = np.zeros((SQUARE, 2 * SQUARE), np.float32)
    last = NODE - 1
    for k in range(NODE):
        facing[last * NODE + k, k] = 1.0
        facing[k, last * NODE + k] = 1.0
        facing[k * NODE + last, SQUARE + k * NODE] = 1.0
        facing[k * NODE, SQUARE + k * NODE + last] = 1.0
    packed = np.zeros((SQUARE, SQUARE // 2), np.float32)
    for q in range(4):
        for k in range(NODE):
            packed[(0 if q // 2 else last) * NODE + k, q * 2 * NODE + k] = 1.0
            packed[k * NODE + (0 if q % 2 else last), (q * 2 + 1) * NODE + k] = 1.0
    return np.concatenate([high, low, *(x.astype(jnp.bfloat16) for x in (facing, packed))], axis=1)


def split(x):
    high = x.astype(BF16)
    return high, (x - high.astype(F32)).astype(BF16)


def dot(left, right):
    return jnp.dot(left, right, preferred_element_type=F32)


def product(x, weight):
    high, low = weight
    rows, depth = x.shape
    wide = high.shape[1]
    if rows < 64:
        rest = x - x.astype(BF16).astype(F32)
        both = jnp.concatenate([x, rest], axis=0).astype(BF16)
        if depth == 128:
            both = jnp.concatenate([both, both], axis=1)
            out = dot(both, jnp.concatenate([high, low], axis=0))
        else:
            out = dot(both, high) + dot(both, low)
        return out[:rows] + out[rows:]
    x_high, x_low = split(x)
    if wide == 128:
        weights = jnp.concatenate([high, low], axis=1)
        if depth == 128:
            weights = jnp.concatenate([weights, weights], axis=0)
            out = dot(jnp.concatenate([x_high, x_low], axis=1), weights)
            return out[:, :128] + out[:, 128:]
        out = dot(x_high, weights)
        return out[:, :128] + dot(x_low, high) + out[:, 128:]
    if depth == 128:
        out = dot(jnp.concatenate([x_high, x_high], axis=1), jnp.concatenate([high, low], axis=0))
        return out + dot(x_low, high)
    return dot(x_high, high) + dot(x_low, high) + dot(x_high, low)


def spread_product(x, weight):
    high, low = split(x)
    moved = pltpu.roll(x - high.astype(F32), 64, 1).astype(BF16)
    is_left = left_half(x.shape)
    zero = jnp.zeros_like(high)
    first = [jnp.where(is_left, high, moved), jnp.where(is_left, high, zero)]
    second = [jnp.where(is_left, moved, high), jnp.where(is_left, zero, high)]
    both = jnp.concatenate([jnp.concatenate(k, axis=1) for k in (first, second)], axis=0)
    return dot(both, jnp.concatenate([weight[0]] * 2 + [weight[1]] * 2, axis=0))


def lanes(shape):
    return lax.broadcasted_iota(jnp.int32, shape, len(shape) - 1)


def left_half(shape):
    return lanes(shape) < shape[-1] // 2


def narrow(x, table):
    rows = x.shape[0]
    rest = x - x.astype(BF16).astype(F32)
    out = dot(jnp.concatenate([x, rest], axis=0).astype(BF16), table)
    out = out[:rows] + out[rows:]
    return out[:, :128] + out[:, 128:]


def broad(x, table):
    rows = x.shape[0]
    rest = x - x.astype(BF16).astype(F32)
    both = jnp.concatenate([x, rest], axis=0).astype(BF16)
    out = dot(jnp.concatenate([both, both], axis=1), table)
    return out[:rows] + out[rows:]


def rows_to_lanes(x, count):
    size = x.shape[0] // count
    return jnp.concatenate([x[k * size : (k + 1) * size] for k in range(count)], axis=1)


def lanes_to_rows(x):
    return jnp.concatenate([x[:, k : k + 128] for k in range(0, x.shape[1], 128)], axis=0)


def quarters(x):
    return [x[:128, :128], x[:128, 128:], x[128:, :128], x[128:, 128:]]


def merge_pair(former, latter):
    wide = product(former, split(rows_to_lanes(latter, 2)))
    return jnp.concatenate(quarters(wide), axis=0)


def parent_pair(upper, lower):
    a, b, c, d = quarters(product(lanes_to_rows(upper), split(lower)))
    return jnp.concatenate([a, c, b, d], axis=1)


def wide_split(x):
    return jnp.concatenate(split(x), axis=1)


def tall_split(x):
    return jnp.concatenate(split(x), axis=0)


def kernel(stages, leaf_side, tracer_count, *refs):
    names = ["u", "velocity", "inflow", "tables", "leaf_solve", "leaf_skeleton", "leaf_lift"]
    names += [a + "_" + b for a in ("merge", "parent", "sibling") for b in ("first", "second", "rest")]
    names += ["root_map"]
    hbm = dict(zip(names, refs[: len(names)]))
    out_ref = refs[len(names)]
    rest = refs[len(names) + 1 :]
    v = dict(zip(names, rest[: len(names)]))
    (
        load_sem, field, near, coef, force, solved,
        up_leaf, up_low, up_high, up_cross, fold, down_high, down_low, down_leaf,
        send_x, send_y, halo_x, halo_y, halo_send, halo_recv, here, up_edge, inner_16,
    ) = rest[len(names) : len(names) + 23]
    stage_refs = rest[len(names) + 23 :]
    T, L = tracer_count, leaf_side
    leaves = L * L
    rows = T * leaves
    half = SQUARE // 2

    loads = {}
    for k, name in enumerate(names):
        loads[name] = pltpu.make_async_copy(hbm[name], v[name], load_sem.at[k])
    order = ["u", "tables", "velocity", "inflow", "leaf_skeleton", "merge_first", "merge_second"]
    order += ["merge_rest", "parent_rest", "sibling_rest", "root_map", "parent_second", "parent_first"]
    order += ["leaf_lift", "leaf_solve", "sibling_first", "sibling_second"]

    for name in order[:2]:
        loads[name].start()

    place = {"gx": lax.axis_index("gx"), "gy": lax.axis_index("gy")}
    count = {"gx": lax.axis_size("gx"), "gy": lax.axis_size("gy")}
    bit_of = lambda axis, bit: lax.rem(place[axis] // (1 << bit), 2)

    def partner(stage, mask):
        target = dict(place)
        for k, (axis, bit) in enumerate(stage):
            if mask >> (len(stage) - 1 - k) & 1:
                target[axis] = target[axis] + (1 - 2 * bit_of(axis, bit)) * (1 << bit)
        return (target["gx"], target["gy"])

    barrier = pltpu.get_barrier_semaphore()
    expected = jnp.int32(0)
    has, beside = {}, {}
    for axis in ("gx", "gy"):
        for way in (-1, 1):
            spot = dict(place)
            spot[axis] = spot[axis] + way
            beside[axis, way] = (spot["gx"], spot["gy"])
            has[axis, way] = place[axis] > 0 if way < 0 else place[axis] < count[axis] - 1

            @pl.when(has[axis, way])
            def _(axis=axis, way=way):
                pl.semaphore_signal(barrier, inc=1, device_id=beside[axis, way], device_id_type=MESH)

            expected = expected + jnp.where(has[axis, way], 1, 0)
    for stage in stages[:-1]:
        for mask in range(1, 1 << len(stage)):
            pl.semaphore_signal(barrier, inc=1, device_id=partner(stage, mask), device_id_type=MESH)
            expected = expected + 1

    by_rank = sorted(stages[-1], key=lambda e: (e == ("gx", 0), e[0] == "gy", -e[1]))
    slots = 1 << len(by_rank)
    rank = jnp.int32(0)
    for axis, bit in by_rank:
        rank = rank * 2 + bit_of(axis, bit)

    cleared = dict(place)
    for axis, bit in by_rank:
        cleared[axis] = cleared[axis] - bit_of(axis, bit) * (1 << bit)

    def ranked(number):
        target = dict(cleared)
        for k, (axis, bit) in enumerate(reversed(by_rank)):
            target[axis] = target[axis] + (number >> k & 1) * (1 << bit)
        return (target["gx"], target["gy"])

    def greet(number):
        @pl.when(rank < number)
        def _():
            pl.semaphore_signal(barrier, inc=1, device_id=ranked(number), device_id_type=MESH)

    def answer(number):
        @pl.when(rank > number)
        def _():
            pl.semaphore_signal(here, inc=1, device_id=ranked(number), device_id_type=MESH)

    expected = expected + rank

    for number in reversed(range(slots)):
        greet(number)

    for name in order[2:8]:
        loads[name].start()

    def spot_of(i, j):
        return sum(
            ((i >> b & 1) << (5 - 2 * b)) + ((j >> b & 1) << (4 - 2 * b)) for b in range(3)
        )

    grid = sorted((spot_of(i, j), i, j) for i in range(L) for j in range(L))
    block = lambda i, j: slice(spot_of(i, j) * T, spot_of(i, j) * T + T)
    by_tracer = lambda i, j, h: pl.ds(h * rows + i * L + j, T, stride=leaves)

    loads["u"].wait()
    plain = v["u"][...].astype(F32).reshape(rows, SQUARE)
    for h in range(2):
        field[h * rows : (h + 1) * rows, :] = plain[:, h * half : (h + 1) * half]

    def of_leaves(spots):
        return jnp.concatenate(
            [
                jnp.concatenate([field[by_tracer(i, j, h), :] for i, j in spots], axis=0)
                for h in range(2)
            ],
            axis=1,
        )

    side = lambda axis, k: [(k, m) if axis == "gx" else (m, k) for m in range(L)]
    borders = [(axis, k) for axis in ("gx", "gy") for k in range(2)]
    spots = [side(axis, k * (L - 1)) for axis, k in borders]
    border = of_leaves([x for line in spots for x in line[::2] + line[1::2]]).astype(BF16)
    loads["tables"].wait()
    border = dot(border, v["tables"][:, 6 * SQUARE :])
    for number, (axis, k) in enumerate(borders):
        low = number * T * L
        even = border[low : low + T * L // 2]
        odd = border[low + T * L // 2 : low + T * L]
        strip = lanes(even.shape) // (2 * NODE if axis == "gx" else 4 * NODE) % 2
        target = send_x if axis == "gx" else send_y
        target[k] = jnp.where(strip == 0, even, odd).astype(BF16)

    def halo_copy(axis, way):
        k = 0 if way < 0 else 1
        source, target = (send_x, halo_x) if axis == "gx" else (send_y, halo_y)
        slot = k + (0 if axis == "gx" else 2)
        return pltpu.make_async_remote_copy(
            src_ref=source.at[k],
            dst_ref=target.at[k],
            send_sem=halo_send.at[slot],
            recv_sem=halo_recv.at[slot],
            device_id=beside[axis, way],
            device_id_type=MESH,
        )

    sides = [("gy", -1), ("gy", 1), ("gx", -1), ("gx", 1)]
    plan = [entry for stage in stages for entry in stage]
    bits = [bit_of(axis, bit) for axis, bit in plan]
    own_half = lambda k, w: jnp.where(bits[k] == 1, w[:, 128:], w[:, :128])
    twice = lambda w, axis: jnp.concatenate([w, w], axis=axis)
    merge = lambda k: v["merge_rest"][k]
    parent = lambda k: v["parent_rest"][k]

    own_parent = lambda k: own_half(k, parent(4 + k))

    def chained():
        chain = [own_parent(0)]
        for k in range(1, len(plan)):
            step = own_parent(k)
            if k > 1:
                step = product(step, split(own_parent(k - 1)))
            chain.append(product(step, split(chain[max(k - 2, 0)])))
        return chain

    def folded(levels, top, siblings, chain=()):
        weights = top
        for k in reversed(levels):
            groups = 1 << (levels[-1] - k)
            if weights is not None:
                weights = product(merge(4 + k), split(weights))
            elif siblings:
                weights = jnp.zeros((256, 128), F32)
            else:
                weights = merge(4 + k)
            blocks = [weights[:, g * 128 : (g + 1) * 128] for g in range(groups)]
            if siblings:
                sibling = own_half(k, v["sibling_rest"][4 + k])
                if k > 0:
                    sibling = product(sibling, split(chain[k - 1]))
                mine = jnp.int32(0)
                for later in levels:
                    if later > k:
                        mine = mine + bits[later] * (1 << (levels[-1] - later))
                blocks = [x + jnp.where(mine == g, sibling, 0.0) for g, x in enumerate(blocks)]
            weights = jnp.concatenate([x[:128] for x in blocks] + [x[128:] for x in blocks], axis=1)
        return lanes_to_rows(weights)

    first = len(plan) - len(stages[-1])
    last_levels = list(range(first, len(plan)))
    direct, folds = last_levels[: -FOLDED], last_levels[-FOLDED:]
    assert len(direct) == 2
    groups = 1 << len(folds)

    def edge_points(q):
        shape = (2 * NODE, SQUARE)
        k = lax.broadcasted_iota(jnp.int32, shape, 0)
        first = k + (SQUARE - NODE if q // 2 else 0)
        second = (k - NODE) * NODE + (NODE - 1 if q % 2 else 0)
        return jnp.where(lanes(shape) == jnp.where(k < NODE, first, second), 1.0, 0.0).astype(BF16)

    def prepare_up():
        for name in ("leaf_skeleton", "merge_first", "merge_second", "merge_rest"):
            loads[name].wait()
        two = [
            product(v["merge_first"][...].T, split(v["merge_second"][d * 64 : (d + 1) * 64, :]))
            for d in range(2)
        ]
        four = jnp.concatenate([two[d][c * 64 : (c + 1) * 64] for c in range(2) for d in range(2)], axis=1)
        up_leaf[...] = wide_split(lanes_to_rows(product(v["leaf_skeleton"][...].T, split(four))))
        at_edges = [
            dot(edge_points(q), up_leaf[q * SQUARE : (q + 1) * SQUARE, :]) for q in range(4)
        ]
        up_edge[...] = jnp.concatenate(at_edges * 2, axis=0).astype(BF16)
        up_low[...] = wide_split(merge_pair(merge(0), merge(1)))
        up_high[...] = wide_split(merge_pair(merge(2), merge(3)))


    def prepare_down():
        up_cross[...] = wide_split(folded(direct, None, False))
        for name in ("parent_rest", "sibling_rest", "root_map"):
            loads[name].wait()
        chain = chained()
        top = product(product(v["root_map"][...], split(own_parent(len(plan) - 1))), split(chain[-2]))
        fold[: groups * 128, :] = wide_split(folded(folds, top, True, chain))
        fold[groups * 128 :, :] = wide_split(folded(direct, None, True, chain))
        down_high[...] = tall_split(parent_pair(parent(3), parent(2)))
        down_low[...] = tall_split(parent_pair(parent(1), parent(0)))
        for name in ("parent_second", "parent_first", "leaf_lift"):
            loads[name].wait()
        halves = lambda x: jnp.concatenate([x, pltpu.roll(x, 64, 1)], axis=0)[:, :64]
        lifts = product(halves(v["parent_first"][...]), split(v["leaf_lift"][...]))
        lifts = jnp.concatenate([lifts[:64], lifts[64:]], axis=1)
        lifts = product(halves(v["parent_second"][...]), split(lifts))
        down_leaf[...] = tall_split(
            jnp.concatenate(
                [
                    lifts[d * 128 : (d + 1) * 128, c * SQUARE : (c + 1) * SQUARE]
                    for c in range(2)
                    for d in range(2)
                ],
                axis=1,
            )
        )

    own = lax.broadcasted_iota(jnp.int32, (leaves, L), 0) % L == lanes((leaves, L))

    def column(values):
        wide = jnp.concatenate(
            [jnp.broadcast_to(values[i : i + 1, :], (L, L)) for i in range(L)], axis=0
        )
        return jnp.sum(jnp.where(own, wide, 0.0), axis=1, keepdims=True)

    tile = (T, half)
    on_0, on_1 = lanes(tile) < NODE, lanes(tile) >= half - NODE
    on_2, on_3 = lanes(tile) % NODE == 0, lanes(tile) % NODE == NODE - 1
    at_leaf = lambda k, i, j: jnp.broadcast_to(coef[k, i * L + j : i * L + j + 1, :], tile)
    keep_if = lambda mask, x: jnp.where(mask, x, 0.0)
    strength = lambda s, i, j: at_leaf(2 + s, i, j)


    def interior():
        whole = of_leaves([(i, j) for _, i, j in grid])
        force[...] = whole
        whole = whole.astype(BF16)
        near[...] = dot(whole, v["tables"][:, 4 * SQUARE : 6 * SQUARE])
        loads["velocity"].wait()
        loads["inflow"].wait()
        speed = [v["velocity"][k] for k in range(2)]
        columns = [column(x) for x in speed]
        columns += [
            column(v["inflow"][s].astype(F32) * (NODE * jnp.abs(speed[s // 2]))) for s in range(4)
        ]
        for k, x in enumerate(columns):
            coef[k] = jnp.broadcast_to(x, (leaves, half))

        for q in range(4):
            low, top = q * rows // 4, (q + 1) * rows // 4
            u = force[low:top, :]
            part = u.astype(BF16)
            grads = dot(part, v["tables"][:, : 2 * SQUARE])
            grads = grads + dot(part, v["tables"][:, 2 * SQUARE : 4 * SQUARE])
            for spot, i, j in grid[q * leaves // 4 : (q + 1) * leaves // 4]:
                at = slice(spot * T, spot * T + T)
                inside = slice(spot * T - low, spot * T + T - low)
                speeds = [at_leaf(k, i, j) for k in range(2)]
                w = [strength(s, i, j) for s in range(4)]
                w_2, w_3 = keep_if(on_2, w[2]), keep_if(on_3, w[3])
                for c in range(2):
                    cut = slice(c * half, (c + 1) * half)
                    far = slice((2 + c) * half, (3 + c) * half)
                    total = u[inside, cut] * (1.0 - (keep_if((on_0, on_1)[c], w[c]) + w_2 + w_3))
                    total = total - speeds[0] * grads[inside, cut] - speeds[1] * grads[inside, far]
                    ahead = i - 1 if c == 0 else i + 1
                    if 0 <= ahead < L:
                        total = total + w[c] * near[block(ahead, j), cut]
                    if j > 0:
                        total = total + w_2 * near[block(i, j - 1), far]
                    if j < L - 1:
                        total = total + w_3 * near[block(i, j + 1), far]
                    force[at, cut] = total


    for axis, way in sides:
        slot = 1 if way < 0 else 0

        @pl.when(jnp.logical_not(has[axis, way]))
        def _(axis=axis, slot=slot):
            target = halo_x if axis == "gx" else halo_y
            target[slot] = jnp.zeros_like(target[slot])

    def announce():
        pl.semaphore_wait(barrier, expected)
        for axis, way in sides:

            @pl.when(has[axis, way])
            def _(axis=axis, way=way):
                halo_copy(axis, way).start()

        for number in range(slots):
            answer(number)

    announce()
    prepare_up()
    interior()
    high, low = split(rows_to_lanes(force[...], 4))
    wide = dot(high, up_leaf[...])
    inner_16[...] = wide[:, :128] + wide[:, 128:] + dot(low, up_leaf[:, :128])
    for name in order[8:]:
        loads[name].start()
    early = rank < slots // 16

    @pl.when(early)
    def _():
        prepare_down()


    edge_weights = []
    for axis, way in sides:
        across = 0 if axis == "gx" else 1
        k = 2 * across + (0 if way < 0 else 1)
        spots = side(axis, 0 if way < 0 else L - 1)
        for m in range(L // 2):
            w = jnp.zeros(tile, F32)
            for i, j in spots[2 * m : 2 * m + 2]:
                q, box = divmod(spot_of(i, j), leaves // 4)
                w = jnp.where(lanes(tile) // NODE == 2 * q + across, strength(k, i, j), w)
            edge_weights.append((axis, way, m, box, w))
    for axis, way in sides:

        @pl.when(has[axis, way])
        def _(axis=axis, way=way):
            halo_copy(axis, -way).wait_recv()

    edges = [None] * (leaves // 4)
    for axis, way, m, box, w in edge_weights:
        arrived = (halo_x if axis == "gx" else halo_y)[1 if way < 0 else 0].astype(F32)
        term = w * arrived[m * T : m * T + T]
        edges[box] = term if edges[box] is None else edges[box] + term
    edges = jnp.concatenate([jnp.zeros(tile, F32) if x is None else x for x in edges], axis=0)
    edges = jnp.concatenate(split(edges), axis=1)
    wide = dot(edges, up_edge[...])
    current_16 = inner_16[...] + wide[:, :128] + wide[:, 128:]
    current_4 = narrow(rows_to_lanes(current_16, 4), up_low[...])
    current = narrow(rows_to_lanes(current_4, 4), up_high[...])

    joined = lambda x: rows_to_lanes(x, 2)
    level = 4
    path = []
    for number, stage in enumerate(stages):
        pool, stage_send, stage_recv = stage_refs[3 * number : 3 * number + 3]
        own_slot = jnp.int32(0)
        for axis, bit in stage:
            own_slot = own_slot * 2 + bit_of(axis, bit)
        pool[own_slot] = current
        final = number == len(stages) - 1
        copies = [] if final else [
            pltpu.make_async_remote_copy(
                src_ref=pool.at[own_slot],
                dst_ref=pool.at[own_slot],
                send_sem=stage_send.at[mask],
                recv_sem=stage_recv.at[mask],
                device_id=partner(stage, mask),
                device_id_type=MESH,
            )
            for mask in range(1, 1 << len(stage))
        ]
        for copy in reversed(copies):
            copy.start()
        if final:

            @pl.when(rank < slots - 1)
            def _():
                pl.semaphore_wait(here, slots - 1 - rank)


            for other in range(slots):

                @pl.when(rank != other)
                def _(other=other):
                    pltpu.make_async_remote_copy(
                        src_ref=pool.at[own_slot],
                        dst_ref=pool.at[own_slot],
                        send_sem=stage_send.at[0],
                        recv_sem=stage_recv.at[0],
                        device_id=ranked(other),
                        device_id_type=MESH,
                    ).start()

            every = pltpu.make_async_remote_copy(
                src_ref=pool.at[pl.ds(0, slots - 1)],
                dst_ref=pool.at[pl.ds(0, slots - 1)],
                send_sem=stage_send.at[0],
                recv_sem=stage_recv.at[0],
                device_id=partner(stage, 1),
                device_id_type=MESH,
            )
        if number == 0:

            @pl.when(jnp.logical_not(early))
            def _():
                prepare_down()

            for name in ("leaf_solve", "sibling_first", "sibling_second"):
                loads[name].wait()
            turned = [jnp.concatenate([edge_points(q)] * 2, axis=0) for q in range(4)]
            of_quarter = lambda q: jnp.concatenate(
                [edges[:, k + q * 32 : k + q * 32 + 32] for k in (0, 128)], axis=1
            )
            forcing = jnp.concatenate(
                [
                    force[q * 128 : (q + 1) * 128, :] + dot(of_quarter(q), turned[q])
                    for q in range(4)
                ],
                axis=0,
            )
            sibling = lambda k: split(v["sibling_rest"][k])
            is_left = lambda x: left_half(x.shape)

            def gathered(x):
                middle = x.shape[0] // 2
                return jnp.where(is_left(x[:middle]), x[:middle], x[middle:])

            cat_0 = gathered(product(forcing, split(twice(v["leaf_skeleton"][...], 0).T)))
            cat_1 = gathered(product(cat_0, split(twice(v["merge_first"][...], 0).T)))
            cats = [joined(current_16)]
            cats.append(joined(product(cats[0], split(merge(0)))))
            cats.append(joined(current_4))
            cats.append(joined(product(cats[2], split(merge(2)))))
            own_part = product(cats[3], sibling(3))
            for k in (2, 1, 0):
                own_part = product(lanes_to_rows(own_part), split(parent(k)))
                own_part = own_part + product(cats[k], sibling(k))
            own_part = product(lanes_to_rows(own_part), split(v["parent_second"][...]))
            own_part = own_part + product(cat_1, split(v["sibling_second"][...]))
            own_part = spread_product(own_part, split(v["parent_first"][...]))
            own_part = own_part + product(cat_0, split(v["sibling_first"][...]))
            own_part = spread_product(own_part, split(v["leaf_lift"][...]))
            solved[...] = own_part + product(forcing, split(v["leaf_solve"][...]))
        if final:
            known = jnp.zeros((T, 128), F32)
            chain = chained() if path else ()
            for k, term in enumerate(path):
                term = own_half(k, term)
                known = known + (product(term, split(chain[k - 1])) if k > 0 else term)
        if final:
            for axis, way in sides:

                @pl.when(has[axis, way])
                def _(axis=axis, way=way):
                    halo_copy(axis, way).wait_send()

            every.wait_recv()
            break
        for copy in copies:
            copy.wait()
        current = pool[...].reshape(T << len(stage), 128)
        for k, (axis, bit) in enumerate(stage):
            cat = joined(current)
            mine = cat
            for later_axis, later_bit in stage[k + 1 :]:
                middle = mine.shape[0] // 2
                mine = jnp.where(bit_of(later_axis, later_bit) == 1, mine[middle:], mine[:middle])
            path.append(product(mine, split(v["sibling_rest"][level])))
            current = product(cat, split(merge(level)))
            level += 1

    everyone = pool[...].reshape(slots * T, 128)
    merged = narrow(rows_to_lanes(everyone, slots // groups), up_cross[...])
    mine = jnp.int32(0)
    for k in folds:
        mine = mine * 2 + bits[k]
    slabs = [rows_to_lanes(merged, groups)]
    slabs += [pool[k * groups + mine] for k in range(slots // groups)]
    boundary = narrow(jnp.concatenate(slabs, axis=1), fold[...]) + known
    boundary = lanes_to_rows(broad(boundary, down_high[...]))
    boundary = lanes_to_rows(broad(boundary, down_low[...]))
    high, low = split(boundary)
    both = twice(high, 1)
    for q in range(4):
        cut = slice(q * SQUARE, (q + 1) * SQUARE)
        lifted = dot(both, down_leaf[:, cut]) + dot(low, down_leaf[:128, cut])
        for spot, i, j in grid[q * leaves // 4 : (q + 1) * leaves // 4]:
            inside = spot * T - q * rows // 4
            for h in range(2):
                one = lifted[inside : inside + T, h * half : (h + 1) * half]
                one = one + solved[spot * T : spot * T + T, h * half : (h + 1) * half]
                field[by_tracer(i, j, h), :] = one
    for t in range(T):
        at = t * leaves
        one = [field[h * rows + at : h * rows + at + leaves, :] for h in range(2)]
        one = jnp.concatenate(one, axis=1).reshape(out_ref.shape[1:])
        out_ref[t] = one.astype(out_ref.dtype)
    every.wait_send()


def local(tables, count_first, count_second, tracers, *operands):
    T, L = tracers.shape[0], tracers.shape[1]
    assert L == 8 and local_plan(L) == [1, 2] * 3
    stages = staged(cross_plan(count_first, count_second))
    rows = T * L * L
    args = [tracers, operands[0], operands[1], tables] + list(operands[2:])
    args[5], args[7] = args[5].T, args[7].T
    vmem, dma = pltpu.VMEM, pltpu.SemaphoreType.DMA
    scratch = [vmem(a.shape, a.dtype) for a in args]
    slots = 1 << len(stages[-1])
    groups = 1 << FOLDED
    scratch += [
        dma((len(args),)),
        vmem((2 * rows, 128), F32),
        vmem((rows, 2 * SQUARE), F32),
        vmem((6, L * L, 128), F32),
        vmem((rows, SQUARE), F32),
        vmem((rows, SQUARE), F32),
        vmem((4 * SQUARE, 256), BF16),
        vmem((512, 256), BF16),
        vmem((512, 256), BF16),
        vmem((slots // groups * 128, 256), BF16),
        vmem(((groups + slots // groups) * 128, 256), BF16),
        vmem((256, 512), BF16),
        vmem((256, 512), BF16),
        vmem((256, 4 * SQUARE), BF16),
        vmem((2, T * L // 2, 128), BF16),
        vmem((2, T * L // 2, 128), BF16),
        vmem((2, T * L // 2, 128), BF16),
        vmem((2, T * L // 2, 128), BF16),
        dma((4,)),
        dma((4,)),
        pltpu.SemaphoreType.REGULAR,
        vmem((256, 256), BF16),
        vmem((T * L * L // 4, 128), F32),
    ]
    for stage in stages:
        slots = 1 << len(stage)
        scratch += [vmem((slots, T, 128), F32), dma((slots,)), dma((slots,))]
    return pl.pallas_call(
        functools.partial(kernel, stages, L, T),
        out_shape=jax.ShapeDtypeStruct(tracers.shape, tracers.dtype),
        in_specs=[pl.BlockSpec(memory_space=pl.ANY)] * len(args),
        out_specs=pl.BlockSpec(memory_space=pltpu.VMEM),
        scratch_shapes=scratch,
        compiler_params=pltpu.CompilerParams(
            collective_id=0, has_side_effects=True, vmem_limit_bytes=VMEM_LIMIT
        ),
    )(*[pltpu.with_memory_space_constraint(a, pltpu.HBM) for a in args])


def solution(mesh):
    tables = point_tables()
    split_both = P(None, "gx", "gy")
    in_specs = (P(None, "gx", "gy", None), split_both, split_both) + (P(),) * 13

    def body(*args):
        return local(
            jnp.asarray(tables), mesh.shape["gx"], mesh.shape["gy"], *args
        )

    return jax.shard_map(
        body,
        mesh=mesh,
        in_specs=in_specs,
        out_specs=P(None, "gx", "gy", None),
        check_vma=False,
    )
```
